128 devices in a mesh: gz: 16 (over z_hi, x, core), gy: 8 (over z_lo, y).
Axes of the slice: x: 4, y: 4, z: 4 (z_hi: 2, z_lo: 2; z = z_hi * 2 + z_lo), core: 2. Of those that a mesh axis runs over, the one named last changes fastest.
Arguments:
- gauge_links: float32 [3, 2, 3, 3, 128, 128, 128], P(None, None, None, None, 'gz', 'gy'), may hold values from -22 to 22
Outputs:
- rotated: float32 [3, 2, 3, 3, 128, 128, 128], P(None, None, None, None, 'gz', 'gy')
The draws below stay inside these ranges and needn't reach their ends.
All inputs are finite; a program needn't handle non-finite values.
Results may differ from the reference program's by a relative error of at most 0.00015.
Values sent between devices are 32-bit elements; how exact they have to be, the bound alone decides.
A program may use at most 64 MiB of HBM per device.

```python
import jax
import jax.numpy as jnp

L = 128
ITERS = 1
ORDER = 8


def draw_product(left_re, left_im, right_re, right_im):
    total_re = None
    total_im = None
    for column in range(3):
        lr = left_re[:, :, column][:, :, None]
        li = left_im[:, :, column][:, :, None]
        rr = right_re[:, column][:, None]
        ri = right_im[:, column][:, None]
        part_re = lr * rr - li * ri
        part_im = lr * ri + li * rr
        if total_re is None:
            total_re, total_im = (part_re, part_im)
        else:
            total_re = total_re + part_re
            total_im = total_im + part_im
    return (total_re, total_im)


def draw_gauge_links(key, part):
    dims = (3, 2, 3, 3, L, L, L)
    raw_draw = 0.45 * jax.random.truncated_normal(key, -2.0, 2.0, dims, jnp.float32)
    gen_re = 0.5 * (raw_draw[:, 0] - jnp.swapaxes(raw_draw[:, 0], 1, 2))
    gen_im = 0.5 * (raw_draw[:, 1] + jnp.swapaxes(raw_draw[:, 1], 1, 2))
    square_re, square_im = draw_product(gen_re, gen_im, gen_re, gen_im)
    cube_re, cube_im = draw_product(square_re, square_im, gen_re, gen_im)
    identity = jnp.eye(3, dtype=jnp.float32).reshape(1, 3, 3, 1, 1, 1)
    link_re = identity + gen_re + square_re / 2.0 + cube_re / 6.0
    link_im = gen_im + square_im / 2.0 + cube_im / 6.0
    return jnp.stack([link_re, link_im], axis=1).astype(jnp.float32)


def setup_inputs(seed: int = 0) -> dict:
    key_list = jax.random.split(jax.random.key(seed), 2)
    gauge_links = draw_gauge_links(jax.random.fold_in(key_list[1], 71), 0)
    return dict(gauge_links=gauge_links)


ALPHA_HALF = 0.04


def complex_mul(left_re, left_im, right_re, right_im):
    total_re = None
    total_im = None
    for column in range(3):
        lr = left_re[:, column][:, None]
        li = left_im[:, column][:, None]
        rr = right_re[column][None]
        ri = right_im[column][None]
        part_re = lr * rr - li * ri
        part_im = lr * ri + li * rr
        if total_re is None:
            total_re, total_im = part_re, part_im
        else:
            total_re = total_re + part_re
            total_im = total_im + part_im
    return total_re, total_im


def exponent(gen_re, gen_im):
    identity = jnp.eye(3, dtype=jnp.float32).reshape((3, 3) + (1,) * (gen_re.ndim - 2))
    term_re = jnp.broadcast_to(identity, gen_re.shape).astype(gen_re.dtype)
    term_im = jnp.zeros_like(gen_re)
    total_re, total_im = term_re, term_im
    for degree in range(1, ORDER + 1):
        term_re, term_im = complex_mul(term_re, term_im, gen_re, gen_im)
        term_re = term_re / degree
        term_im = term_im / degree
        total_re = total_re + term_re
        total_im = total_im + term_im
    return total_re, total_im


def algebra(m_re, m_im):
    trace_part = (m_im[0, 0] + m_im[1, 1] + m_im[2, 2]) / 3.0
    return jnp.stack([
        m_im[0, 0] - trace_part,
        m_im[1, 1] - trace_part,
        (m_re[0, 1] - m_re[1, 0]) / 2.0,
        (m_im[0, 1] + m_im[1, 0]) / 2.0,
        (m_re[0, 2] - m_re[2, 0]) / 2.0,
        (m_im[0, 2] + m_im[2, 0]) / 2.0,
        (m_re[1, 2] - m_re[2, 1]) / 2.0,
        (m_im[1, 2] + m_im[2, 1]) / 2.0,
    ])


def generator(half_gen):
    empty_entry = jnp.zeros_like(half_gen[0])
    gen_re = jnp.stack([
        jnp.stack([empty_entry, half_gen[2], half_gen[4]]),
        jnp.stack([-half_gen[2], empty_entry, half_gen[6]]),
        jnp.stack([-half_gen[4], -half_gen[6], empty_entry]),
    ])
    gen_im = jnp.stack([
        jnp.stack([half_gen[0], half_gen[3], half_gen[5]]),
        jnp.stack([half_gen[3], half_gen[1], half_gen[7]]),
        jnp.stack([half_gen[5], half_gen[7], -half_gen[0] - half_gen[1]]),
    ])
    return gen_re, gen_im


def lattice_momentum(wave):
    value = jnp.sin(jnp.pi * wave.astype(jnp.float32) / L)
    return 4.0 * value * value


def scale_table(wave_z, wave_y, wave_x):
    squared = lattice_momentum(wave_z)[:, None, None] + lattice_momentum(wave_y)[None, :, None] + lattice_momentum(wave_x)[None, None, :]
    is_anchor = (wave_z[:, None, None] == 0) & (wave_y[None, :, None] == 0) & (wave_x[None, None, :] == 0)
    safe = jnp.where(is_anchor, 1.0, squared)
    return jnp.where(is_anchor, 1.0, 12.0 / safe)


def iterate(gauge_links):
    near_x = jnp.roll(gauge_links[0], 1, axis=-1)
    near_y = jnp.roll(gauge_links[1], 1, axis=-2)
    near_z = jnp.roll(gauge_links[2], 1, axis=-3)
    mixed_sum = (near_x + near_y + near_z) - (gauge_links[0] + gauge_links[1] + gauge_links[2])
    components = algebra(mixed_sum[0], mixed_sum[1])
    spectrum = jnp.fft.fftn(components, axes=(1, 2, 3))
    wavenumbers = jnp.arange(L).astype(jnp.int32)
    weights = scale_table(wavenumbers, wavenumbers, wavenumbers)
    smooth = jnp.real(jnp.fft.ifftn(spectrum * weights[None], axes=(1, 2, 3))).astype(jnp.float32)
    half_gen = ALPHA_HALF * smooth
    g_re, g_im = exponent(*generator(half_gen))
    result = []
    for direction, axis in ((0, -1), (1, -2), (2, -3)):
        ahead_re = jnp.roll(g_re, -1, axis=axis)
        ahead_im = jnp.roll(g_im, -1, axis=axis)
        left_re, left_im = complex_mul(g_re, g_im, gauge_links[direction, 0], gauge_links[direction, 1])
        out_re, out_im = complex_mul(left_re, left_im, jnp.swapaxes(ahead_re, 0, 1), -jnp.swapaxes(ahead_im, 0, 1))
        result.append(jnp.stack([out_re, out_im]))
    return jnp.stack(result)


def reference(gauge_links):
    current = gauge_links
    for sweep in range(ITERS):
        current = iterate(current)
    return current
```

```python
import functools
import math

import jax
import jax.numpy as jnp
import numpy as np
from jax import lax
from jax.experimental import pallas as pl
from jax.experimental.pallas import tpu as pltpu
from jax.sharding import PartitionSpec as P

L = 128
ALPHA_HALF = 0.04
BZ = 8
BY = 16
NC = 8
NP = BZ + 1
MESH = pl.DeviceIdType.MESH
F32 = jnp.float32
BF16 = jnp.bfloat16
CHUNKS = ((0, 3), (3, 6), (6, 9))


def tables():
    k = np.arange(L)
    angle = 2.0 * np.pi / L * (np.outer(k, k) % L)
    hartley = np.cos(angle) + np.sin(angle)
    high = hartley.astype(np.float32).astype(jnp.bfloat16)
    low = (hartley - high.astype(np.float64)).astype(np.float32).astype(jnp.bfloat16)
    half = np.concatenate([high, low], axis=1)
    mat_x = np.concatenate([half, half], axis=0)
    mat_y = np.ascontiguousarray(mat_x.T)
    momentum = 4.0 * np.sin(np.pi * k / L) ** 2
    mass = momentum[:, None] + momentum[None, :]
    mass[0, 0] = 1.0
    root = np.sqrt(mass * mass / 4.0 + mass)
    decay = 1.0 / (1.0 + mass / 2.0 + root)
    factor = 12.0 * ALPHA_HALF / (L * L) / (2.0 * root)
    decay[0, 0] = 0.0
    factor[0, 0] = 0.0
    return mat_x, mat_y, decay.astype(np.float32), factor.astype(np.float32)


def split(x):
    high = x.astype(BF16)
    low = (x - high.astype(F32)).astype(BF16)
    return high, low


def transform_x(x, mat_x):
    high, low = split(x)
    out = jnp.dot(jnp.concatenate([high, low], axis=1), mat_x, preferred_element_type=F32)
    return out[:, :L] + out[:, L:]


def transform_y(planes, mat_y):
    wide = jnp.concatenate(planes, axis=1)
    high, low = split(wide)
    out = jnp.dot(mat_y, jnp.concatenate([high, low], axis=0), preferred_element_type=F32)
    return out[:L] + out[L:]


def algebra(re, im):
    trace_part = (im(0, 0) + im(1, 1) + im(2, 2)) * (1.0 / 3.0)
    return [
        im(0, 0) - trace_part,
        im(1, 1) - trace_part,
        (re(0, 1) - re(1, 0)) * 0.5,
        (im(0, 1) + im(1, 0)) * 0.5,
        (re(0, 2) - re(2, 0)) * 0.5,
        (im(0, 2) + im(2, 0)) * 0.5,
        (re(1, 2) - re(2, 1)) * 0.5,
        (im(1, 2) + im(2, 1)) * 0.5,
    ]


def smooth_kernel(
    nz,
    ny,
    links,
    mat_x_in,
    mat_y_in,
    decay_in,
    factor_in,
    out_main,
    out_face,
    link,
    send_a,
    face_a,
    recv_a,
    face_r,
    field,
    send_b,
    recv_b,
    send_e,
    recv_e,
    send_c,
    recv_c,
    send_d,
    face_d,
    mat_x,
    mat_y,
    decay,
    factor,
    load_sem,
    own_sem,
    a_send,
    a_recv,
    b_send,
    b_recv,
    c_send,
    c_recv,
    d_send,
    d_recv,
):
    gz = lax.axis_index("gz")
    gy = lax.axis_index("gy")
    lines = L // nz
    extent = nz * BZ
    last = len(CHUNKS)

    barrier = pltpu.get_barrier_semaphore()
    for r in range(1, ny):
        pl.semaphore_signal(
            barrier, inc=1, device_id=(gz, lax.rem(gy + r, ny)), device_id_type=MESH
        )
    for r in range(1, nz):
        pl.semaphore_signal(
            barrier, inc=1, device_id=(lax.rem(gz + r, nz), gy), device_id_type=MESH
        )

    loads = [pltpu.make_async_copy(links.at[1], link.at[1], load_sem.at[0])]
    ranges = [(lo, min(hi, BZ)) for lo, hi in CHUNKS]
    for n, (lo, hi) in enumerate(ranges):
        for m, mu in enumerate((0, 2)):
            loads.append(
                pltpu.make_async_copy(
                    links.at[mu, :, :, :, lo:hi],
                    link.at[mu, :, :, :, lo:hi],
                    load_sem.at[1 + 2 * n + m],
                )
            )
    base = 1 + 2 * len(CHUNKS)
    small = [
        pltpu.make_async_copy(src, dst, load_sem.at[base + n])
        for n, (src, dst) in enumerate(
            ((mat_x_in, mat_x), (mat_y_in, mat_y), (decay_in, decay), (factor_in, factor))
        )
    ]
    for copy in loads:
        copy.start()
    for copy in small:
        copy.start()

    def remote(src, dst, send, recv, device):
        return pltpu.make_async_remote_copy(
            src_ref=src,
            dst_ref=dst,
            send_sem=send,
            recv_sem=recv,
            device_id=device,
            device_id_type=MESH,
        )

    def rows(block):
        return pl.ds(pl.multiple_of(block * BY, BY), BY)

    def tile(block):
        return pl.ds(pl.multiple_of(block * BZ, BZ), BZ)

    def copy_a(n, r, sender):
        lo, hi = CHUNKS[n]
        target = lax.rem(gy + r, ny)
        return remote(
            send_a.at[target, lo:hi],
            recv_a.at[lo:hi, rows(sender)],
            a_send.at[n, r],
            a_recv.at[n, r],
            (gz, target),
        )

    def copy_face_a(r, sender):
        target = lax.rem(gy + r, ny)
        return remote(
            face_a.at[tile(target)],
            face_r.at[tile(sender)],
            a_send.at[last, r],
            a_recv.at[last, r],
            (gz, target),
        )

    row_index = lax.broadcasted_iota(jnp.int32, (BY, L), 0)
    first_row = row_index == 0

    def entries(mu, z):
        def re(i, j):
            return link[mu, 0, i, j, z]

        def im(i, j):
            return link[mu, 1, i, j, z]

        return re, im

    loads[0].wait()

    def part_y(z, carry):
        parts = algebra(*entries(1, z))
        for c in range(NC):
            behind = jnp.where(first_row, 0.0, pltpu.roll(parts[c], 1, 0))
            send_a[c, z] = behind - parts[c]
            face_a[pl.ds(c * BZ + z, 1), :] = parts[c][BY - 1 : BY]
        return carry

    lax.fori_loop(0, BZ, part_y, 0)

    pl.semaphore_wait(barrier, nz + ny - 2)
    for r in range(1, ny):
        copy_face_a(r, gy).start()
    own_face = pltpu.make_async_copy(face_a.at[tile(gy)], face_r.at[tile(gy)], own_sem.at[last])
    own_face.start()

    carry = [jnp.zeros((BY, L), F32) for _ in range(NC)]
    own_a = []
    for n, (lo, hi) in enumerate(ranges):
        loads[1 + 2 * n].wait()
        loads[2 + 2 * n].wait()

        def part_xz(z, below):
            along_x = algebra(*entries(0, z))
            along_z = algebra(*entries(2, z))
            for c in range(NC):
                shifted = pltpu.roll(along_x[c], 1, 1)
                send_a[c, z] += (shifted - along_x[c]) + (below[c] - along_z[c])
            return along_z

        carry = lax.fori_loop(lo, hi, part_xz, carry)
        if CHUNKS[n][1] == NP:
            for c in range(NC):
                send_a[c, BZ] = carry[c]
        for r in range(1, ny):
            copy_a(n, r, gy).start()
        lo, hi = CHUNKS[n]
        own = pltpu.make_async_copy(
            send_a.at[gy, lo:hi], recv_a.at[lo:hi, rows(gy)], own_sem.at[n]
        )
        own.start()
        own_a.append(own)

    for copy in small:
        copy.wait()
    own_face.wait()
    for r in range(1, ny):
        copy_face_a(r, lax.rem(gy + ny - r, ny)).wait_recv()

    for n, (lo, hi) in enumerate(CHUNKS):
        own_a[n].wait()
        for r in range(1, ny):
            copy_a(n, r, lax.rem(gy + ny - r, ny)).wait_recv()
        for z in range(lo, min(hi, BZ)):
            edge = pltpu.roll(face_r[pl.ds(z, ny, stride=BZ), :], 1, 0)
            recv_a[z, pl.ds(0, ny, stride=BY), :] += edge
        data = transform_x(recv_a[lo:hi].reshape((hi - lo) * L, L), mat_x[...])
        data = transform_y([data[i * L : (i + 1) * L] for i in range(hi - lo)], mat_y[...])
        for i in range(hi - lo):
            field[lo + i] = data[:, i * L : (i + 1) * L]

    rate = decay[...]
    up = field[0]
    down = field[BZ]
    for i in range(1, NP):
        up = field[i] + rate * up
        down = field[BZ - i] + rate * down
    send_b[:, 0] = up.reshape(nz, lines, L)
    send_b[:, 1] = down.reshape(nz, lines, L)
    lane = lax.broadcasted_iota(jnp.int32, (1, L), 1)
    packed = jnp.zeros((1, L), F32)
    for i in range(NP):
        packed = jnp.where(lane == i, jnp.sum(jnp.where(lane == 0, field[i, 0:1, :], 0.0)), packed)
    send_e[0] = packed

    def copy_b(r, sender):
        target = lax.rem(gz + r, nz)
        return remote(
            send_b.at[target], recv_b.at[sender], b_send.at[0, r], b_recv.at[0, r], (target, gy)
        )

    def copy_e(r, sender):
        target = lax.rem(gz + r, nz)
        return remote(
            send_e.at[0], recv_e.at[sender], b_send.at[1, r], b_recv.at[1, r], (target, gy)
        )

    def copy_c(r, sender):
        target = lax.rem(gz + r, nz)
        return remote(
            send_c.at[target], recv_c.at[sender], c_send.at[r], c_recv.at[r], (target, gy)
        )

    for r in range(1, nz):
        copy_b(r, gz).start()
    for r in range(1, nz):
        copy_e(r, gz).start()
    recv_b[gz] = send_b[gz]
    recv_e[gz] = packed

    rate8 = decay[pl.ds(pl.multiple_of(gz * lines, lines), lines), :]
    rate8 = rate8 * rate8
    rate8 = rate8 * rate8
    rate8 = rate8 * rate8
    whole = rate8
    for _ in range(int(math.log2(nz))):
        whole = whole * whole
    images = 1.0 / (1.0 - whole)

    for r in range(1, nz):
        copy_b(r, lax.rem(gz + nz - r, nz)).wait_recv()

    up = recv_b[0, 0]
    down = recv_b[nz - 1, 1]
    for j in range(1, nz):
        up = recv_b[j, 0] + rate8 * up
        down = recv_b[nz - 1 - j, 1] + rate8 * down
    up = up * images
    down = down * images
    for j in range(nz):
        send_c[j, 0] = up
        send_c[nz - 1 - j, 1] = down
        if j < nz - 1:
            up = recv_b[j, 0] + rate8 * up
            down = recv_b[nz - 1 - j, 1] + rate8 * down
    for r in range(1, nz):
        copy_c(r, gz).start()
    recv_c[gz] = send_c[gz]

    for r in range(1, nz):
        copy_e(r, lax.rem(gz + nz - r, nz)).wait_recv()
    sources = recv_e[:, 0, :]
    block = lax.broadcasted_iota(jnp.int32, (nz, L), 0)
    plane = lax.broadcasted_iota(jnp.int32, (nz, L), 1)
    corner = (lax.broadcasted_iota(jnp.int32, (8, L), 0) == 0) & (
        lax.broadcasted_iota(jnp.int32, (8, L), 1) == 0
    )
    constant = (1.0 + extent * extent - 1.0) / extent
    zero_line = []
    for i in range(NP):
        gap = BZ * (gz - block) + i - plane
        gap = jnp.where(gap < 0, gap + extent, gap).astype(F32)
        weight = constant - (6.0 / extent) * gap * (extent - gap)
        weight = jnp.where(plane < NP, weight * (ALPHA_HALF / (L * L)), 0.0)
        zero_line.append(jnp.where(corner, jnp.sum(weight * sources), 0.0))

    for r in range(1, nz):
        copy_c(r, lax.rem(gz + nz - r, nz)).wait_recv()

    rate = decay[...]
    scale = factor[...]
    down = recv_c[:, 1].reshape(L, L)
    ahead = [None] * NP
    for i in range(BZ, -1, -1):
        recv_a[i] = down
        if i > 0:
            down = rate * (down + field[i])
    up = field[0] + recv_c[:, 0].reshape(L, L)
    for i in range(NP):
        if i > 0:
            up = field[i] + rate * up
        recv_a[i] = scale * (up + recv_a[i])
        recv_a[i, 0:8, :] += zero_line[i]

    def copy_d(n, r, owner):
        lo, hi = CHUNKS[n]
        target = lax.rem(gy + r, ny)
        return remote(
            send_d.at[lo:hi, rows(target)],
            out_main.at[owner, lo:hi],
            d_send.at[n, r],
            d_recv.at[n, r],
            (gz, target),
        )

    def copy_face_d(r, owner):
        target = lax.rem(gy + r, ny)
        return remote(
            face_d.at[tile(target)],
            out_face.at[tile(owner)],
            d_send.at[last, r],
            d_recv.at[last, r],
            (gz, target),
        )

    own_d = []
    for n, (lo, hi) in enumerate(CHUNKS):
        data = transform_y([recv_a[i] for i in range(lo, hi)], mat_y[...])
        data = jnp.concatenate(
            [data[:, i * L : (i + 1) * L] for i in range(hi - lo)], axis=0
        )
        data = transform_x(data, mat_x[...])
        send_d[lo:hi] = data.reshape(hi - lo, L, L)
        for r in range(1, ny):
            copy_d(n, r, gy).start()
        own = pltpu.make_async_copy(
            send_d.at[lo:hi, rows(gy)], out_main.at[gy, lo:hi], own_sem.at[last + 1 + n]
        )
        own.start()
        own_d.append(own)
        for z in range(lo, min(hi, BZ)):
            edge = send_d[z, pl.ds(0, ny, stride=BY), :]
            face_d[pl.ds(z, ny, stride=BZ), :] = pltpu.roll(edge, ny - 1, 0)
    for r in range(1, ny):
        copy_face_d(r, gy).start()
    own = pltpu.make_async_copy(
        face_d.at[tile(gy)], out_face.at[tile(gy)], own_sem.at[2 * last + 1]
    )
    own.start()
    own_d.append(own)

    for copy in own_d:
        copy.wait()
    for r in range(1, ny):
        sender = lax.rem(gy + ny - r, ny)
        for n in range(last):
            copy_d(n, r, sender).wait_recv()
        copy_face_d(r, sender).wait_recv()
    for r in range(1, ny):
        for n in range(last):
            copy_a(n, r, gy).wait_send()
            copy_d(n, r, gy).wait_send()
        copy_face_a(r, gy).wait_send()
        copy_face_d(r, gy).wait_send()
    for r in range(1, nz):
        copy_b(r, gz).wait_send()
        copy_e(r, gz).wait_send()
        copy_c(r, gz).wait_send()


def smooth(links, nz, ny):
    mat_x, mat_y, decay, factor = tables()
    last = len(CHUNKS)
    lines = L // nz
    vmem = pltpu.VMEM
    dma = pltpu.SemaphoreType.DMA
    anywhere = pl.BlockSpec(memory_space=pl.ANY)
    return pl.pallas_call(
        functools.partial(smooth_kernel, nz, ny),
        out_shape=(
            jax.ShapeDtypeStruct((NC, NP, BY, L), F32),
            jax.ShapeDtypeStruct((NC * BZ, L), F32),
        ),
        in_specs=[anywhere] * 5,
        out_specs=(anywhere, anywhere),
        scratch_shapes=[
            vmem((3, 2, 3, 3, BZ, BY, L), F32),
            vmem((NC, NP, BY, L), F32),
            vmem((NC * BZ, L), F32),
            vmem((NP, L, L), F32),
            vmem((ny * BZ, L), F32),
            vmem((NP, L, L), F32),
            vmem((nz, 2, lines, L), F32),
            vmem((nz, 2, lines, L), F32),
            vmem((1, 1, L), F32),
            vmem((nz, 1, L), F32),
            vmem((nz, 2, lines, L), F32),
            vmem((nz, 2, lines, L), F32),
            vmem((NP, L, L), F32),
            vmem((ny * BZ, L), F32),
            vmem((2 * L, 2 * L), BF16),
            vmem((2 * L, 2 * L), BF16),
            vmem((L, L), F32),
            vmem((L, L), F32),
            dma((5 + 2 * last,)),
            dma((2 * last + 2,)),
            dma((last + 1, ny)),
            dma((last + 1, ny)),
            dma((2, nz)),
            dma((2, nz)),
            dma((nz,)),
            dma((nz,)),
            dma((last + 1, ny)),
            dma((last + 1, ny)),
        ],
        compiler_params=pltpu.CompilerParams(collective_id=0, has_side_effects=True),
        name="smooth",
    )(links, jnp.asarray(mat_x), jnp.asarray(mat_y), jnp.asarray(decay), jnp.asarray(factor))


def exponent(h):
    h2 = -(h[0] + h[1])
    diag = (h[0], h[1], h2)
    re01, im01 = h[3], -h[2]
    re02, im02 = h[5], -h[4]
    re12, im12 = h[7], -h[6]
    n01 = re01 * re01 + im01 * im01
    n02 = re02 * re02 + im02 * im02
    n12 = re12 * re12 + im12 * im12
    s0 = h[0] * h[0] + n01 + n02
    s1 = h[1] * h[1] + n01 + n12
    s2 = h2 * h2 + n02 + n12
    s01re = re02 * re12 + im02 * im12 - h2 * re01
    s01im = im02 * re12 - re02 * im12 - h2 * im01
    s02re = re01 * re12 - im01 * im12 - h[1] * re02
    s02im = re01 * im12 + im01 * re12 - h[1] * im02
    s12re = re01 * re02 + im01 * im02 - h[0] * re12
    s12im = re01 * im02 - im01 * re02 - h[0] * im12
    p = 0.5 * (s0 + s1 + s2)
    cross = (re01 * re12 - im01 * im12) * re02 + (re01 * im12 + im01 * re12) * im02
    d = h[0] * h[1] * h2 + 2.0 * cross - h[0] * n12 - h[1] * n02 - h2 * n01
    pp = p * p
    dd = d * d
    dp = d * p
    cubes = dd + p * pp
    a0 = 1.0 + dd * (p * (2.0 / 40320.0) - 1.0 / 720.0)
    b0 = d * (-1.0 / 6.0 + p * (1.0 / 120.0) - pp * (1.0 / 5040.0))
    a1 = d * (1.0 / 24.0 - p * (2.0 / 720.0) + pp * (3.0 / 40320.0))
    b1 = 1.0 - p * (1.0 / 6.0) + pp * (1.0 / 120.0) - cubes * (1.0 / 5040.0)
    a2 = -0.5 + p * (1.0 / 24.0) - pp * (1.0 / 720.0) + cubes * (1.0 / 40320.0)
    b2 = d * (1.0 / 120.0) - dp * (2.0 / 5040.0)
    re = {}
    im = {}
    for j, s in enumerate((s0, s1, s2)):
        re[j, j] = a0 + a1 * diag[j] + a2 * s
        im[j, j] = b0 + b1 * diag[j] + b2 * s
    for i, j, hr, hi, sr, si in (
        (0, 1, re01, im01, s01re, s01im),
        (0, 2, re02, im02, s02re, s02im),
        (1, 2, re12, im12, s12re, s12im),
    ):
        rr = a1 * hr + a2 * sr
        ii = b1 * hi + b2 * si
        ri = a1 * hi + a2 * si
        ir = b1 * hr + b2 * sr
        re[i, j] = rr - ii
        im[i, j] = ri + ir
        re[j, i] = rr + ii
        im[j, i] = ir - ri
    return [re[i, j] for i in range(3) for j in range(3)] + [
        im[i, j] for i in range(3) for j in range(3)
    ]


def rotate_kernel(link, main, face, out, here, edge):
    z = pl.program_id(0)
    slot = lax.rem(z, 2)
    other = 1 - slot

    def fill(where, plane):
        for s in range(0, BY, 8):
            g = exponent([main[c, plane, s : s + 8] for c in range(NC)])
            for k in range(18):
                here[where, k, s : s + 8] = g[k]

    @pl.when(z == 0)
    def _():
        g = exponent([face[c * BZ : (c + 1) * BZ] for c in range(NC)])
        for k in range(18):
            edge[k] = g[k]
        fill(0, 0)

    fill(other, z + 1)
    for k in range(18):
        here[slot, k, BY : BY + 1] = edge[k, pl.ds(z, 1)]

    for s in range(0, BY, 8):
        g = [here[slot, k, s : s + 8] for k in range(18)]
        for mu in range(3):
            if mu == 0:
                ahead = [pltpu.roll(x, L - 1, 1) for x in g]
            elif mu == 1:
                ahead = [here[slot, k, s + 1 : s + 9] for k in range(18)]
            else:
                ahead = [here[other, k, s : s + 8] for k in range(18)]
            u = [
                link[mu, p, i, j, 0, s : s + 8]
                for p in range(2)
                for i in range(3)
                for j in range(3)
            ]
            for i in range(3):
                left = []
                for k in range(3):
                    re = im = None
                    for j in range(3):
                        ar, ai = g[3 * i + j], g[9 + 3 * i + j]
                        br, bi = u[3 * j + k], u[9 + 3 * j + k]
                        tr = ar * br - ai * bi
                        ti = ar * bi + ai * br
                        re = tr if re is None else re + tr
                        im = ti if im is None else im + ti
                    left.append((re, im))
                for l in range(3):
                    re = im = None
                    for k in range(3):
                        ar, ai = left[k]
                        br, bi = ahead[3 * l + k], ahead[9 + 3 * l + k]
                        tr = ar * br + ai * bi
                        ti = ai * br - ar * bi
                        re = tr if re is None else re + tr
                        im = ti if im is None else im + ti
                    out[mu, 0, i, l, 0, s : s + 8] = re
                    out[mu, 1, i, l, 0, s : s + 8] = im


def rotate(links, main, face):
    block = pl.BlockSpec((3, 2, 3, 3, 1, BY, L), lambda z: (0, 0, 0, 0, z, 0, 0))
    return pl.pallas_call(
        rotate_kernel,
        grid=(BZ,),
        out_shape=jax.ShapeDtypeStruct(links.shape, F32),
        in_specs=[
            block,
            pl.BlockSpec((NC, NP, BY, L), lambda z: (0, 0, 0, 0)),
            pl.BlockSpec((NC * BZ, L), lambda z: (0, 0)),
        ],
        out_specs=block,
        scratch_shapes=[pltpu.VMEM((2, 18, BY + 8, L), F32), pltpu.VMEM((18, BZ, L), F32)],
        compiler_params=pltpu.CompilerParams(dimension_semantics=("arbitrary",)),
        name="rotate",
    )(links, main, face)


def solution(mesh):
    nz, ny = mesh.shape["gz"], mesh.shape["gy"]

    def body(links):
        main, face = smooth(links, nz, ny)
        return rotate(links, main, face)

    spec = P(None, None, None, None, "gz", "gy", None)
    return jax.shard_map(body, mesh=mesh, in_specs=(spec,), out_specs=spec, check_vma=False)
```

```python
import functools
import math

import jax
import jax.numpy as jnp
import numpy as np
from jax import lax
from jax.experimental import pallas as pl
from jax.experimental.pallas import tpu as pltpu
from jax.sharding import PartitionSpec as P

L = 128
ALPHA_HALF = 0.04
BZ = 8
BY = 16
NC = 8
MESH = pl.DeviceIdType.MESH
F32 = jnp.float32
BF16 = jnp.bfloat16
FORTH = ((6, 8), (4, 6), (2, 4), (1, 2), (0, 1))
BACK = ((0, 2), (2, 4), (4, 6), (6, 8))
BACK_EARLY = 2


def tables():
    k = np.arange(L)
    angle = 2.0 * np.pi / L * (np.outer(k, k) % L)
    hartley = np.cos(angle) + np.sin(angle)
    high = hartley.astype(np.float32).astype(jnp.bfloat16)
    low = (hartley - high.astype(np.float64)).astype(np.float32).astype(jnp.bfloat16)
    half = np.concatenate([high, low], axis=1)
    mat_x = np.concatenate([half, half], axis=0)
    mat_y = np.ascontiguousarray(mat_x.T)
    momentum = 4.0 * np.sin(np.pi * k / L) ** 2
    mass = momentum[:, None] + momentum[None, :]
    mass[0, 0] = 1.0
    root = np.sqrt(mass * mass / 4.0 + mass)
    decay = 1.0 / (1.0 + mass / 2.0 + root)
    factor = 12.0 * ALPHA_HALF / (L * L) / (2.0 * root)
    decay[0, 0] = 0.0
    factor[0, 0] = 0.0
    return mat_x, mat_y, decay.astype(np.float32), factor.astype(np.float32)


def split(x):
    high = x.astype(BF16)
    low = (x - high.astype(F32)).astype(BF16)
    return high, low


def transform_x(planes, mat_x):
    high, low = split(jnp.concatenate(planes, axis=0))
    out = jnp.dot(jnp.concatenate([high, low], axis=1), mat_x, preferred_element_type=F32)
    out = out[:, :L] + out[:, L:]
    return [out[i * L : (i + 1) * L] for i in range(len(planes))]


def transform_y(planes, mat_y):
    high, low = split(jnp.concatenate(planes, axis=1))
    out = jnp.dot(mat_y, jnp.concatenate([high, low], axis=0), preferred_element_type=F32)
    out = out[:L] + out[L:]
    return [out[:, i * L : (i + 1) * L] for i in range(len(planes))]


def algebra(re, im):
    trace_part = (im(0, 0) + im(1, 1) + im(2, 2)) * (1.0 / 3.0)
    return [
        im(0, 0) - trace_part,
        im(1, 1) - trace_part,
        (re(0, 1) - re(1, 0)) * 0.5,
        (im(0, 1) + im(1, 0)) * 0.5,
        (re(0, 2) - re(2, 0)) * 0.5,
        (im(0, 2) + im(2, 0)) * 0.5,
        (re(1, 2) - re(2, 1)) * 0.5,
        (im(1, 2) + im(2, 1)) * 0.5,
    ]


def fix_kernel(
    nz,
    ny,
    links,
    mat_x_in,
    mat_y_in,
    decay_in,
    factor_in,
    out,
    link,
    send_a,
    edge_y,
    recv_a,
    edge_r,
    edge_z,
    below_z,
    field,
    send_b,
    recv_b,
    send_e,
    recv_e,
    send_c,
    recv_c,
    send_d,
    edge_d,
    main,
    above_z,
    edge_g,
    mat_x,
    mat_y,
    decay,
    factor,
    turn,
    turn_edge,
    load_sem,
    small_sem,
    own_sem,
    edge_sem,
    a_send,
    a_recv,
    b_send,
    b_recv,
    c_send,
    c_recv,
    d_send,
    d_recv,
    e_send,
    e_recv,
    z_send,
    z_recv,
):
    gz = lax.axis_index("gz")
    gy = lax.axis_index("gy")
    lines = L // nz
    extent = nz * BZ

    barrier = pltpu.get_barrier_semaphore()
    for r in range(1, ny):
        pl.semaphore_signal(
            barrier, inc=1, device_id=(gz, lax.rem(gy + r, ny)), device_id_type=MESH
        )
    for r in range(1, nz):
        pl.semaphore_signal(
            barrier, inc=1, device_id=(lax.rem(gz + r, nz), gy), device_id_type=MESH
        )
    between = lax.rem(gy + ny // 2, ny)
    for r in range(nz):
        pl.semaphore_signal(
            barrier, inc=1, device_id=(lax.rem(gz + r, nz), between), device_id_type=MESH
        )

    def load(mu, z):
        return pltpu.make_async_copy(
            links.at[mu, :, :, :, pl.ds(z, 1)],
            link.at[mu, :, :, :, pl.ds(z, 1)],
            load_sem.at[mu, z],
        )

    small = [
        pltpu.make_async_copy(src, dst, small_sem.at[n])
        for n, (src, dst) in enumerate(
            ((mat_x_in, mat_x), (mat_y_in, mat_y), (decay_in, decay), (factor_in, factor))
        )
    ]
    for z in range(BZ):
        load(1, z).start()
    load(2, BZ - 1).start()
    for z in range(BZ - 1, -1, -1):
        if z > 0:
            load(2, z - 1).start()
        load(0, z).start()
    for copy in small:
        copy.start()

    def remote(src, dst, send, recv, device):
        return pltpu.make_async_remote_copy(
            src_ref=src,
            dst_ref=dst,
            send_sem=send,
            recv_sem=recv,
            device_id=device,
            device_id_type=MESH,
        )

    def rows(block):
        return pl.ds(pl.multiple_of(block * BY, BY), BY)

    def tile(block):
        return pl.ds(pl.multiple_of(block * BZ, BZ), BZ)

    def y_target(r):
        return lax.rem(gy + r, ny)

    def y_sender(r):
        return lax.rem(gy + ny - r, ny)

    def z_target(r):
        return lax.rem(gz + r, nz)

    def z_sender(r):
        return lax.rem(gz + nz - r, nz)

    def copy_a(n, r, sender):
        lo, hi = FORTH[n]
        return remote(
            send_a.at[y_target(r), lo:hi],
            recv_a.at[lo:hi, rows(sender)],
            a_send.at[n, r],
            a_recv.at[n, r],
            (gz, y_target(r)),
        )

    def own_a(n):
        lo, hi = FORTH[n]
        return pltpu.make_async_copy(
            send_a.at[gy, lo:hi], recv_a.at[lo:hi, rows(gy)], own_sem.at[0, n]
        )

    def copy_edge_a(r, sender):
        return remote(
            edge_y.at[tile(y_target(r))],
            edge_r.at[tile(sender)],
            e_send.at[0, r],
            e_recv.at[0, r],
            (gz, y_target(r)),
        )

    copy_up = remote(edge_z, below_z, z_send.at[0], z_recv.at[0], (z_target(1), gy))
    copy_down = remote(
        main.at[:, 0], above_z, z_send.at[1], z_recv.at[1], (z_target(nz - 1), gy)
    )

    first_row = lax.broadcasted_iota(jnp.int32, (BY, L), 0) == 0

    def parts(mu, z):
        return algebra(
            lambda i, j: link[mu, 0, i, j, z], lambda i, j: link[mu, 1, i, j, z]
        )

    def part_y(z, carry):
        load(1, z).wait()
        along = parts(1, z)
        for c in range(NC):
            behind = jnp.where(first_row, 0.0, pltpu.roll(along[c], 1, 0))
            send_a[c, z] = behind - along[c]
            edge_y[pl.ds(c * BZ + z, 1), :] = along[c][BY - 1 : BY]
        return carry

    lax.fori_loop(0, BZ, part_y, 0)
    load(2, BZ - 1).wait()
    top = parts(2, BZ - 1)
    for c in range(NC):
        edge_z[c] = top[c]

    pl.semaphore_wait(barrier, 2 * nz + ny - 2)
    copy_up.start()
    for r in range(1, ny):
        copy_edge_a(r, gy).start()
    own_edge_a = pltpu.make_async_copy(edge_y.at[tile(gy)], edge_r.at[tile(gy)], edge_sem.at[0])
    own_edge_a.start()

    def gather(z, under, here):
        along = parts(0, z)
        for c in range(NC):
            shifted = pltpu.roll(along[c], 1, 1)
            send_a[c, z] += (shifted - along[c]) + (under[c] - here[c])

    def start_a(n):
        for r in range(1, ny):
            copy_a(n, r, gy).start()
        own_a(n).start()

    def step(t, here):
        z = BZ - 1 - t
        load(2, z - 1).wait()
        load(0, z).wait()
        under = parts(2, z - 1)
        gather(z, under, here)
        return under

    def receive(n):
        own_a(n).wait()
        for r in range(1, ny):
            copy_a(n, r, y_sender(r)).wait_recv()
        lo, hi = FORTH[n]
        for z in range(lo, hi):
            edge = pltpu.roll(edge_r[pl.ds(z, ny, stride=BZ), :], 1, 0)
            recv_a[z, pl.ds(0, ny, stride=BY), :] += edge
        data = transform_x([recv_a[z] for z in range(lo, hi)], mat_x[...])
        data = transform_y(data, mat_y[...])
        for z in range(lo, hi):
            field[z] = data[z - lo]

    bottom = top
    for n, (lo, hi) in enumerate(FORTH):
        if lo > 0:
            bottom = lax.fori_loop(BZ - hi, BZ - lo, step, bottom)
            start_a(n)
    load(0, 0).wait()
    copy_up.wait_recv()
    gather(0, [below_z[c] for c in range(NC)], bottom)
    start_a(len(FORTH) - 1)

    for copy in small:
        copy.wait()
    own_edge_a.wait()
    for r in range(1, ny):
        copy_edge_a(r, y_sender(r)).wait_recv()
    for n in range(len(FORTH)):
        receive(n)

    rate = decay[...]
    up = field[0]
    down = field[BZ - 1]
    for i in range(1, BZ):
        up = field[i] + rate * up
        down = field[BZ - 1 - i] + rate * down
    send_b[:, 0] = (rate * up).reshape(nz, lines, L)
    send_b[:, 1] = down.reshape(nz, lines, L)

    def copy_b(r, sender):
        return remote(
            send_b.at[z_target(r)],
            recv_b.at[sender],
            b_send.at[0, r],
            b_recv.at[0, r],
            (z_target(r), between),
        )

    def copy_e(r, sender):
        return remote(
            send_e.at[0],
            recv_e.at[sender],
            b_send.at[1, r],
            b_recv.at[1, r],
            (z_target(r), gy),
        )

    def copy_c(r, sender):
        return remote(
            send_c.at[z_target(r)],
            recv_c.at[sender],
            c_send.at[r],
            c_recv.at[r],
            (z_target(r), between),
        )

    for r in range(nz):
        copy_b(r, gz).start()
    lane = lax.broadcasted_iota(jnp.int32, (1, L), 1)
    packed = jnp.zeros((1, L), F32)
    for i in range(BZ):
        packed = jnp.where(lane == i, jnp.sum(jnp.where(lane == 0, field[i, 0:1, :], 0.0)), packed)
    send_e[0] = packed
    for r in range(1, nz):
        copy_e(r, gz).start()
    recv_e[gz] = packed

    rate8 = decay[pl.ds(pl.multiple_of(gz * lines, lines), lines), :]
    rate8 = rate8 * rate8
    rate8 = rate8 * rate8
    rate8 = rate8 * rate8
    whole = rate8
    for _ in range(int(math.log2(nz))):
        whole = whole * whole
    images = 1.0 / (1.0 - whole)

    for r in range(nz):
        copy_b(r, z_sender(r)).wait_recv()

    up = recv_b[0, 0]
    down = recv_b[nz - 1, 1]
    for j in range(1, nz):
        up = recv_b[j, 0] + rate8 * up
        down = recv_b[nz - 1 - j, 1] + rate8 * down
    up = up * images
    down = down * images
    for j in range(nz):
        send_c[j, 0] = up
        send_c[nz - 1 - j, 1] = down
        if j < nz - 1:
            up = recv_b[j, 0] + rate8 * up
            down = recv_b[nz - 1 - j, 1] + rate8 * down
    for r in range(nz):
        copy_c(r, gz).start()

    for r in range(1, nz):
        copy_e(r, z_sender(r)).wait_recv()
    sources = recv_e[:, 0, :]
    block = lax.broadcasted_iota(jnp.int32, (nz, L), 0)
    plane = lax.broadcasted_iota(jnp.int32, (nz, L), 1)
    corner = (lax.broadcasted_iota(jnp.int32, (8, L), 0) == 0) & (
        lax.broadcasted_iota(jnp.int32, (8, L), 1) == 0
    )
    constant = (1.0 + extent * extent - 1.0) / extent
    zero_line = []
    for i in range(BZ):
        gap = BZ * (gz - block) + i - plane
        gap = jnp.where(gap < 0, gap + extent, gap).astype(F32)
        weight = constant - (6.0 / extent) * gap * (extent - gap)
        weight = jnp.where(plane < BZ, weight * (ALPHA_HALF / (L * L)), 0.0)
        zero_line.append(jnp.where(corner, jnp.sum(weight * sources), 0.0))

    for r in range(nz):
        copy_c(r, z_sender(r)).wait_recv()

    rate = decay[...]
    scale = factor[...]
    down = rate * recv_c[:, 1].reshape(L, L)
    for i in range(BZ - 1, -1, -1):
        recv_a[i] = down
        if i > 0:
            down = rate * (down + field[i])
    up = recv_c[:, 0].reshape(L, L)
    for i in range(BZ):
        up = field[i] + (rate * up if i > 0 else up)
        recv_a[i] = scale * (up + recv_a[i])
        recv_a[i, 0:8, :] += zero_line[i]

    def copy_d(n, r, owner):
        lo, hi = BACK[n]
        return remote(
            send_d.at[lo:hi, rows(y_target(r))],
            main.at[owner, lo:hi],
            d_send.at[n, r],
            d_recv.at[n, r],
            (gz, y_target(r)),
        )

    def own_d(n):
        lo, hi = BACK[n]
        return pltpu.make_async_copy(
            send_d.at[lo:hi, rows(gy)], main.at[gy, lo:hi], own_sem.at[1, n]
        )

    def copy_edge_d(r, owner):
        return remote(
            edge_d.at[tile(y_target(r))],
            edge_g.at[tile(owner)],
            e_send.at[1, r],
            e_recv.at[1, r],
            (gz, y_target(r)),
        )

    own_edge_d = pltpu.make_async_copy(edge_d.at[tile(gy)], edge_g.at[tile(gy)], edge_sem.at[1])

    def start_d(n):
        for r in range(1, ny):
            copy_d(n, r, gy).start()
        own_d(n).start()

    for n, (lo, hi) in enumerate(BACK):
        data = transform_y([recv_a[z] for z in range(lo, hi)], mat_y[...])
        data = transform_x(data, mat_x[...])
        for z in range(lo, hi):
            send_d[z] = data[z - lo]
            edge = send_d[z, pl.ds(0, ny, stride=BY), :]
            edge_d[pl.ds(z, ny, stride=BZ), :] = pltpu.roll(edge, ny - 1, 0)
        if n < BACK_EARLY:
            start_d(n)
    for r in range(1, ny):
        copy_edge_d(r, gy).start()
    own_edge_d.start()
    for n in range(BACK_EARLY, len(BACK)):
        start_d(n)

    def fill(plane, value):
        for s in range(0, BY, 8):
            g = exponent([value(c, s) for c in range(NC)])
            for k in range(18):
                turn[plane, k, s : s + 8] = g[k]

    def rotate(z, directions, halves=(0, 8)):
        for s in halves:
            g = [turn[z, k, s : s + 8] for k in range(18)]
            for mu in directions:
                if mu == 0:
                    ahead = [pltpu.roll(x, L - 1, 1) for x in g]
                elif mu == 1:
                    ahead = [turn[z, k, s + 1 : s + 9] for k in range(18)]
                else:
                    ahead = [turn[z + 1, k, s : s + 8] for k in range(18)]
                rotate_link(link, out, mu, z, s, g, ahead)

    def arrive(n):
        own_d(n).wait()
        for r in range(1, ny):
            copy_d(n, r, y_sender(r)).wait_recv()

    def plane_step(z, carry):
        fill(z, lambda c, s: main[c, z, s : s + 8])
        rotate(z, (0,))
        rotate(z, (1,), (0,))
        rotate(z - 1, (2,))
        return carry

    def edge_step(z, carry):
        for k in range(18):
            turn[z, k, BY : BY + 1] = turn_edge[k, pl.ds(z, 1)]
        rotate(z, (1,), (8,))
        return carry

    for n, (lo, hi) in enumerate(BACK):
        arrive(n)
        if n == 0:
            copy_down.start()
            fill(0, lambda c, s: main[c, 0, s : s + 8])
            rotate(0, (0,))
            rotate(0, (1,), (0,))
        lax.fori_loop(max(lo, 1), hi, plane_step, 0)
    own_edge_d.wait()
    for r in range(1, ny):
        copy_edge_d(r, y_sender(r)).wait_recv()
    g = exponent([edge_g[c * BZ : (c + 1) * BZ] for c in range(NC)])
    for k in range(18):
        turn_edge[k] = g[k]
    lax.fori_loop(0, BZ, edge_step, 0)
    copy_down.wait_recv()
    fill(BZ, lambda c, s: above_z[c, s : s + 8])
    rotate(BZ - 1, (2,))

    for r in range(1, ny):
        for n in range(len(FORTH)):
            copy_a(n, r, gy).wait_send()
        for n in range(len(BACK)):
            copy_d(n, r, gy).wait_send()
        copy_edge_a(r, gy).wait_send()
        copy_edge_d(r, gy).wait_send()
    for r in range(nz):
        copy_b(r, gz).wait_send()
        copy_c(r, gz).wait_send()
    for r in range(1, nz):
        copy_e(r, gz).wait_send()
    copy_up.wait_send()
    copy_down.wait_send()


def rotate_link(link, out, mu, z, s, g, ahead):
    u = [link[mu, p, i, j, z, s : s + 8] for p in range(2) for i in range(3) for j in range(3)]
    for i in range(3):
        left = []
        for k in range(3):
            re = im = None
            for j in range(3):
                ar, ai = g[3 * i + j], g[9 + 3 * i + j]
                br, bi = u[3 * j + k], u[9 + 3 * j + k]
                tr = ar * br - ai * bi
                ti = ar * bi + ai * br
                re = tr if re is None else re + tr
                im = ti if im is None else im + ti
            left.append((re, im))
        for l in range(3):
            re = im = None
            for k in range(3):
                ar, ai = left[k]
                br, bi = ahead[3 * l + k], ahead[9 + 3 * l + k]
                tr = ar * br + ai * bi
                ti = ai * br - ar * bi
                re = tr if re is None else re + tr
                im = ti if im is None else im + ti
            out[mu, 0, i, l, z, s : s + 8] = re
            out[mu, 1, i, l, z, s : s + 8] = im


def fix(links, nz, ny):
    mat_x, mat_y, decay, factor = tables()
    lines = L // nz
    vmem = pltpu.VMEM
    dma = pltpu.SemaphoreType.DMA
    return pl.pallas_call(
        functools.partial(fix_kernel, nz, ny),
        out_shape=pltpu.VMEM(links.shape, F32),
        in_specs=[pl.BlockSpec(memory_space=pltpu.HBM)] * 5,
        out_specs=pl.BlockSpec(memory_space=pltpu.VMEM),
        scratch_shapes=[
            vmem((3, 2, 3, 3, BZ, BY, L), F32),
            vmem((NC, BZ, BY, L), F32),
            vmem((NC * BZ, L), F32),
            vmem((BZ, L, L), F32),
            vmem((ny * BZ, L), F32),
            vmem((NC, BY, L), F32),
            vmem((NC, BY, L), F32),
            vmem((BZ, L, L), F32),
            vmem((nz, 2, lines, L), F32),
            vmem((nz, 2, lines, L), F32),
            vmem((1, 1, L), F32),
            vmem((nz, 1, L), F32),
            vmem((nz, 2, lines, L), F32),
            vmem((nz, 2, lines, L), F32),
            vmem((BZ, L, L), F32),
            vmem((ny * BZ, L), F32),
            vmem((NC, BZ, BY, L), F32),
            vmem((NC, BY, L), F32),
            vmem((NC * BZ, L), F32),
            vmem((2 * L, 2 * L), BF16),
            vmem((2 * L, 2 * L), BF16),
            vmem((L, L), F32),
            vmem((L, L), F32),
            vmem((BZ + 1, 18, BY + 8, L), F32),
            vmem((18, BZ, L), F32),
            dma((3, BZ)),
            dma((4,)),
            dma((2, BZ)),
            dma((2,)),
            dma((BZ, ny)),
            dma((BZ, ny)),
            dma((2, nz)),
            dma((2, nz)),
            dma((nz,)),
            dma((nz,)),
            dma((BZ, ny)),
            dma((BZ, ny)),
            dma((2, ny)),
            dma((2, ny)),
            dma((2,)),
            dma((2,)),
        ],
        compiler_params=pltpu.CompilerParams(
            collective_id=0, has_side_effects=True, vmem_limit_bytes=32 << 20
        ),
        name="fix",
    )(*(pltpu.with_memory_space_constraint(jnp.asarray(x), pltpu.HBM)
        for x in (links, mat_x, mat_y, decay, factor)))


def exponent(h):
    h2 = -(h[0] + h[1])
    diag = (h[0], h[1], h2)
    re01, im01 = h[3], -h[2]
    re02, im02 = h[5], -h[4]
    re12, im12 = h[7], -h[6]
    n01 = re01 * re01 + im01 * im01
    n02 = re02 * re02 + im02 * im02
    n12 = re12 * re12 + im12 * im12
    s0 = h[0] * h[0] + n01 + n02
    s1 = h[1] * h[1] + n01 + n12
    s2 = h2 * h2 + n02 + n12
    s01re = re02 * re12 + im02 * im12 - h2 * re01
    s01im = im02 * re12 - re02 * im12 - h2 * im01
    s02re = re01 * re12 - im01 * im12 - h[1] * re02
    s02im = re01 * im12 + im01 * re12 - h[1] * im02
    s12re = re01 * re02 + im01 * im02 - h[0] * re12
    s12im = re01 * im02 - im01 * re02 - h[0] * im12
    p = 0.5 * (s0 + s1 + s2)
    cross = (re01 * re12 - im01 * im12) * re02 + (re01 * im12 + im01 * re12) * im02
    d = h[0] * h[1] * h2 + 2.0 * cross - h[0] * n12 - h[1] * n02 - h2 * n01
    pp = p * p
    dd = d * d
    dp = d * p
    cubes = dd + p * pp
    a0 = 1.0 + dd * (p * (2.0 / 40320.0) - 1.0 / 720.0)
    b0 = d * (-1.0 / 6.0 + p * (1.0 / 120.0) - pp * (1.0 / 5040.0))
    a1 = d * (1.0 / 24.0 - p * (2.0 / 720.0) + pp * (3.0 / 40320.0))
    b1 = 1.0 - p * (1.0 / 6.0) + pp * (1.0 / 120.0) - cubes * (1.0 / 5040.0)
    a2 = -0.5 + p * (1.0 / 24.0) - pp * (1.0 / 720.0) + cubes * (1.0 / 40320.0)
    b2 = d * (1.0 / 120.0) - dp * (2.0 / 5040.0)
    re = {}
    im = {}
    for j, s in enumerate((s0, s1, s2)):
        re[j, j] = a0 + a1 * diag[j] + a2 * s
        im[j, j] = b0 + b1 * diag[j] + b2 * s
    for i, j, hr, hi, sr, si in (
        (0, 1, re01, im01, s01re, s01im),
        (0, 2, re02, im02, s02re, s02im),
        (1, 2, re12, im12, s12re, s12im),
    ):
        rr = a1 * hr + a2 * sr
        ii = b1 * hi + b2 * si
        ri = a1 * hi + a2 * si
        ir = b1 * hr + b2 * sr
        re[i, j] = rr - ii
        im[i, j] = ri + ir
        re[j, i] = rr + ii
        im[j, i] = ir - ri
    return [re[i, j] for i in range(3) for j in range(3)] + [
        im[i, j] for i in range(3) for j in range(3)
    ]


def store_kernel(source, out, sem):
    copies = [
        pltpu.make_async_copy(source.at[mu, p], out.at[mu, p], sem.at[mu, p])
        for mu in range(3)
        for p in range(2)
    ]
    for copy in copies:
        copy.start()
    for copy in copies:
        copy.wait()


def store(source):
    return pl.pallas_call(
        store_kernel,
        out_shape=jax.ShapeDtypeStruct(source.shape, F32),
        in_specs=[pl.BlockSpec(memory_space=pltpu.VMEM)],
        out_specs=pl.BlockSpec(memory_space=pl.ANY),
        scratch_shapes=[pltpu.SemaphoreType.DMA((3, 2))],
        compiler_params=pltpu.CompilerParams(vmem_limit_bytes=16 << 20),
        name="store",
    )(source)


def solution(mesh):
    nz, ny = mesh.shape["gz"], mesh.shape["gy"]

    def body(links):
        return store(fix(links, nz, ny))

    spec = P(None, None, None, None, "gz", "gy", None)
    return jax.shard_map(body, mesh=mesh, in_specs=(spec,), out_specs=spec, check_vma=False)
```

```python
import functools
import math

import jax
import jax.numpy as jnp
import numpy as np
from jax import lax
from jax.experimental import pallas as pl
from jax.experimental.pallas import tpu as pltpu
from jax.sharding import PartitionSpec as P

L = 128
ALPHA_HALF = 0.04
BZ = 8
BY = 16
NC = 8
MESH = pl.DeviceIdType.MESH
F32 = jnp.float32
BF16 = jnp.bfloat16
HALF = L // 2
NQ = BZ // 2
FORTH = ((0, 2, 4), (0, 0, 2), (1, 2, 4), (1, 0, 2))
BACK = ((0, 0, 2), (1, 0, 2), (0, 2, 3), (1, 2, 3), (0, 3, 4), (1, 3, 4))
STEPS = ((1, 2), (0, 2), (1, 1), (1, 3), (0, 1), (0, 3), (1, 0))


def tables():
    k = np.arange(L)
    angle = 2.0 * np.pi / L * (np.outer(k, k) % L)
    hartley = np.cos(angle) + np.sin(angle)
    high = hartley.astype(np.float32).astype(jnp.bfloat16)
    low = (hartley - high.astype(np.float64)).astype(np.float32).astype(jnp.bfloat16)
    half = np.concatenate([high, low], axis=1)
    mat_x = np.concatenate([half, half], axis=0)
    mat_y = np.ascontiguousarray(mat_x.T)
    momentum = 4.0 * np.sin(np.pi * k / L) ** 2
    mass = momentum[:, None] + momentum[None, :]
    mass[0, 0] = 1.0
    root = np.sqrt(mass * mass / 4.0 + mass)
    decay = 1.0 / (1.0 + mass / 2.0 + root)
    factor = 12.0 * ALPHA_HALF / (L * L) / (2.0 * root)
    decay[0, 0] = 0.0
    factor[0, 0] = 0.0
    paired = [
        np.stack([np.tile(t[:, h * HALF : (h + 1) * HALF], (1, 2)) for h in range(2)])
        for t in (decay, factor)
    ]
    return mat_x, mat_y, paired[0].astype(np.float32), paired[1].astype(np.float32)


def split(x):
    high = x.astype(BF16)
    low = (x - high.astype(F32)).astype(BF16)
    return high, low


def transform_x(planes, mat_x):
    high, low = split(jnp.concatenate(planes, axis=0))
    out = jnp.dot(jnp.concatenate([high, low], axis=1), mat_x, preferred_element_type=F32)
    out = out[:, :L] + out[:, L:]
    return [out[i * L : (i + 1) * L] for i in range(len(planes))]


def transform_y(planes, mat_y):
    high, low = split(jnp.concatenate(planes, axis=1))
    out = jnp.dot(mat_y, jnp.concatenate([high, low], axis=0), preferred_element_type=F32)
    out = out[:L] + out[L:]
    return [out[:, i * L : (i + 1) * L] for i in range(len(planes))]


def algebra(re, im):
    trace_part = (im(0, 0) + im(1, 1) + im(2, 2)) * (1.0 / 3.0)
    return [
        im(0, 0) - trace_part,
        im(1, 1) - trace_part,
        (re(0, 1) - re(1, 0)) * 0.5,
        (im(0, 1) + im(1, 0)) * 0.5,
        (re(0, 2) - re(2, 0)) * 0.5,
        (im(0, 2) + im(2, 0)) * 0.5,
        (re(1, 2) - re(2, 1)) * 0.5,
        (im(1, 2) + im(2, 1)) * 0.5,
    ]


def fix_kernel(
    nz,
    ny,
    links,
    mat_x_in,
    mat_y_in,
    decay_in,
    factor_in,
    out,
    link,
    base,
    send_a,
    edge_y,
    recv_a,
    edge_r,
    edge_z,
    below_z,
    field,
    keep,
    send_b,
    recv_b,
    send_e,
    recv_e,
    send_c,
    recv_c,
    send_d,
    edge_d,
    main,
    smooth,
    above_z,
    edge_g,
    mat_x,
    mat_y,
    decay,
    factor,
    turn,
    turn_edge,
    load_sem,
    small_sem,
    own_sem,
    edge_sem,
    a_send,
    a_recv,
    b_send,
    b_recv,
    c_send,
    c_recv,
    d_send,
    d_recv,
    e_send,
    e_recv,
    z_send,
    z_recv,
    ring,
):
    gz = lax.axis_index("gz")
    gy = lax.axis_index("gy")
    lines = L // nz
    extent = nz * BZ

    side = ny // 2
    half = nz // 2
    my_z, my_y = lax.div(gy, side), lax.rem(gy, side)

    def y_target(r):
        a, b = STEPS[r - 1]
        return lax.rem(my_z + a, 2) * side + lax.rem(my_y + b, side)

    def y_sender(r):
        a, b = STEPS[r - 1]
        return lax.rem(my_z + 2 - a, 2) * side + lax.rem(my_y + side - b, side)

    def z_target(r):
        return lax.rem(gz + r, nz)

    def z_sender(r):
        return lax.rem(gz + nz - r, nz)

    my_half, my_place = lax.div(gz, half), lax.rem(gz, half)

    def near(r):
        return my_half * half + lax.rem(my_place + r, half)

    between = lax.rem(gy + side, ny)

    barrier = pltpu.get_barrier_semaphore()
    for r in range(1, ny):
        pl.semaphore_signal(barrier, inc=1, device_id=(gz, y_target(r)), device_id_type=MESH)
    for device in [z_target(half), z_target(1), z_target(nz - 1)] + [
        near(r) for r in range(1, half)
    ]:
        pl.semaphore_signal(barrier, inc=1, device_id=(device, gy), device_id_type=MESH)

    def load(mu, z):
        return pltpu.make_async_copy(
            links.at[mu, :, :, :, pl.ds(z, 1)],
            link.at[mu, :, :, :, pl.ds(z, 1)],
            load_sem.at[mu, z],
        )

    small = [
        pltpu.make_async_copy(src, dst, small_sem.at[n])
        for n, (src, dst) in enumerate(
            ((mat_x_in, mat_x), (mat_y_in, mat_y), (decay_in, decay), (factor_in, factor))
        )
    ]
    for z in range(BZ):
        load(1, z).start()
    small[0].start()
    load(2, BZ - 1).start()
    load(2, NQ - 1).start()
    for q in range(NQ - 1, -1, -1):
        if q > 0:
            load(2, q + NQ - 1).start()
            load(2, q - 1).start()
        load(0, q + NQ).start()
        load(0, q).start()
    for copy in small[1:]:
        copy.start()

    def remote(src, dst, send, recv, device):
        return pltpu.make_async_remote_copy(
            src_ref=src,
            dst_ref=dst,
            send_sem=send,
            recv_sem=recv,
            device_id=device,
            device_id_type=MESH,
        )

    def rows(block):
        return pl.ds(pl.multiple_of(block * BY, BY), BY)

    def tile(block):
        return pl.ds(pl.multiple_of(block * BZ, BZ), BZ)

    def copy_a(n, r, sender):
        h, lo, hi = FORTH[n]
        return remote(
            send_a.at[h, y_target(r), lo:hi],
            recv_a.at[h, lo:hi, rows(sender)],
            a_send.at[n, r],
            a_recv.at[n, r],
            (gz, y_target(r)),
        )

    def own_a(n):
        h, lo, hi = FORTH[n]
        return pltpu.make_async_copy(
            send_a.at[h, gy, lo:hi], recv_a.at[h, lo:hi, rows(gy)], own_sem.at[0, n]
        )

    def start_a(n):
        for r in range(1, ny):
            copy_a(n, r, gy).start()
        own_a(n).start()

    def copy_edge_a(r, sender):
        return remote(
            edge_y.at[tile(y_target(r))],
            edge_r.at[tile(sender)],
            e_send.at[0, r],
            e_recv.at[0, r],
            (gz, y_target(r)),
        )

    def copy_b(h, r, sender):
        return remote(
            send_b.at[h, z_target(r)],
            recv_b.at[h, sender],
            b_send.at[h, r],
            b_recv.at[h, r],
            (z_target(r), between),
        )

    def copy_e(r, sender):
        return remote(
            send_e.at[0],
            recv_e.at[sender],
            b_send.at[2, r],
            b_recv.at[2, r],
            (z_target(r), gy),
        )

    def copy_c(h, r, sender):
        return remote(
            send_c.at[h, z_target(r)],
            recv_c.at[h, sender],
            c_send.at[h, r],
            c_recv.at[h, r],
            (z_target(r), between),
        )

    def copy_d(n, r, owner):
        h, lo, hi = BACK[n]
        return remote(
            send_d.at[h, lo:hi, rows(y_target(r))],
            main.at[h, owner, lo:hi],
            d_send.at[n, r],
            d_recv.at[n, r],
            (gz, y_target(r)),
        )

    def own_d(n):
        h, lo, hi = BACK[n]
        return pltpu.make_async_copy(
            send_d.at[h, lo:hi, rows(gy)], main.at[h, gy, lo:hi], own_sem.at[1, n]
        )

    def start_d(n):
        for r in range(1, ny):
            copy_d(n, r, gy).start()
        own_d(n).start()

    def copy_edge_d(r, owner):
        return remote(
            edge_d.at[tile(y_target(r))],
            edge_g.at[tile(owner)],
            e_send.at[1, r],
            e_recv.at[1, r],
            (gz, y_target(r)),
        )

    copy_up = remote(edge_z, below_z, z_send.at[0], z_recv.at[0], (z_target(1), gy))
    copy_down = remote(smooth.at[0], above_z, z_send.at[1], z_recv.at[1], (z_target(nz - 1), gy))
    own_edge_a = pltpu.make_async_copy(edge_y.at[tile(gy)], edge_r.at[tile(gy)], edge_sem.at[0])
    own_edge_d = pltpu.make_async_copy(edge_d.at[tile(gy)], edge_g.at[tile(gy)], edge_sem.at[1])

    first_row = lax.broadcasted_iota(jnp.int32, (BY, L), 0) == 0
    left = lax.broadcasted_iota(jnp.int32, (L, L), 1) < HALF
    straight = (lax.broadcasted_iota(jnp.int32, (NC, BZ, L), 2) < HALF) == (
        lax.broadcasted_iota(jnp.int32, (NC, BZ, L), 1) < NQ
    )

    def swap(x):
        return pltpu.roll(x, HALF, 1)

    def pair(x, y):
        return jnp.where(left, x, swap(y)), jnp.where(left, swap(x), y)

    def pair_edge(x):
        other = pltpu.roll(swap(x).reshape(NC, BZ, L), NQ, 1)
        return jnp.where(straight, x.reshape(NC, BZ, L), other).reshape(NC * BZ, L)

    def parts(mu, z):
        return algebra(
            lambda i, j: link[mu, 0, i, j, z], lambda i, j: link[mu, 1, i, j, z]
        )

    def part_y(z, carry):
        load(1, z).wait()
        along = parts(1, z)
        for c in range(NC):
            behind = jnp.where(first_row, 0.0, pltpu.roll(along[c], 1, 0))
            base[c, z] = behind - along[c]
            edge_y[pl.ds(c * BZ + z, 1), :] = along[c][BY - 1 : BY]
        return carry

    lax.fori_loop(0, BZ, part_y, 0)
    load(2, BZ - 1).wait()
    top = parts(2, BZ - 1)
    for c in range(NC):
        edge_z[c] = top[c]
    small[0].wait()

    pl.semaphore_wait(barrier, ny + half + 1)
    copy_up.start()
    for r in range(1, half):
        pl.semaphore_signal(ring.at[0], inc=1, device_id=(near(r), gy), device_id_type=MESH)

    def divergence(z, under, here):
        along = parts(0, z)
        return jnp.concatenate(
            [
                base[c, z] + (pltpu.roll(along[c], 1, 1) - along[c]) + (under[c] - here[c])
                for c in range(NC)
            ],
            axis=0,
        )

    def spread(q, low, high):
        low, high = transform_x([low, high], mat_x[...])
        low, high = pair(low, high)
        send_a[0, :, q] = low.reshape(NC, BY, L)
        send_a[1, :, q] = high.reshape(NC, BY, L)

    def step(t, carry):
        here_low, here_high = carry
        q = NQ - 1 - t
        load(2, q + NQ - 1).wait()
        load(2, q - 1).wait()
        load(0, q + NQ).wait()
        load(0, q).wait()
        under_low = parts(2, q - 1)
        under_high = parts(2, q + NQ - 1)
        spread(
            q, divergence(q, under_low, here_low), divergence(q + NQ, under_high, here_high)
        )
        return under_low, under_high

    load(2, NQ - 1).wait()
    carry = (parts(2, NQ - 1), top)
    carry = lax.fori_loop(0, 2, step, carry)
    start_a(0)
    edge_y[...] = pair_edge(transform_x([edge_y[...]], mat_x[...])[0])
    for r in range(1, ny):
        copy_edge_a(r, gy).start()
    own_edge_a.start()
    carry = lax.fori_loop(2, NQ - 1, step, carry)
    load(0, NQ).wait()
    load(0, 0).wait()
    high = divergence(NQ, parts(2, NQ - 1), carry[1])
    copy_up.wait_recv()
    spread(0, divergence(0, [below_z[c] for c in range(NC)], carry[0]), high)
    for n in range(1, len(FORTH)):
        start_a(n)
    if half > 1:
        pl.semaphore_wait(ring.at[0], half - 1)
    pl.semaphore_signal(
        ring.at[1], inc=1, device_id=(z_target(half), gy), device_id_type=MESH
    )

    for copy in small[1:]:
        copy.wait()
    own_edge_a.wait()
    for r in range(1, ny):
        copy_edge_a(r, y_sender(r)).wait_recv()

    def receive(n):
        h, lo, hi = FORTH[n]
        own_a(n).wait()
        for r in range(1, ny):
            copy_a(n, r, y_sender(r)).wait_recv()
        for q in range(lo, hi):
            edge = pltpu.roll(edge_r[pl.ds(h * NQ + q, ny, stride=BZ), :], 1, 0)
            recv_a[h, q, pl.ds(0, ny, stride=BY), :] += edge
        data = transform_y([recv_a[h, q] for q in range(lo, hi)], mat_y[...])
        for q in range(lo, hi):
            field[h, q] = data[q - lo]

    def power4(x):
        x = x * x
        return x * x

    def moments(h):
        rate = decay[h]
        rate4 = power4(rate)
        up = field[h, 0]
        down = field[h, NQ - 1]
        for q in range(1, NQ):
            up = field[h, q] + rate * up
            down = field[h, NQ - 1 - q] + rate * down
        up = rate * up
        swapped = jnp.where(left, swap(down), swap(up))
        keep[h] = swapped
        send_b[h] = (jnp.where(left, down, up) + rate4 * swapped).reshape(nz, lines, L)
        for r in range(nz):
            copy_b(h, r, gz).start()

    narrow = lax.broadcasted_iota(jnp.int32, (lines, L), 1) < HALF

    def solve(h):
        rate8 = decay[h, pl.ds(pl.multiple_of(gz * lines, lines), lines), :]
        rate8 = power4(rate8 * rate8)
        whole = rate8
        for _ in range(int(math.log2(nz))):
            whole = whole * whole
        images = 1.0 / (1.0 - whole)
        for r in range(nz):
            copy_b(h, r, z_sender(r)).wait_recv()
        mixed = [
            jnp.where(narrow, recv_b[h, nz - 1 - j], recv_b[h, j]) for j in range(nz)
        ]
        state = mixed[0]
        for j in range(1, nz):
            state = mixed[j] + rate8 * state
        state = state * images
        result = []
        for j in range(nz):
            result.append(state)
            state = mixed[j] + rate8 * state
        for j in range(nz):
            send_c[h, j] = jnp.where(narrow, result[nz - 1 - j], result[j])
        for r in range(nz):
            copy_c(h, r, gz).start()

    receive(0)
    receive(1)
    pl.semaphore_wait(ring.at[1], 1)
    moments(0)
    lane = lax.broadcasted_iota(jnp.int32, (1, L), 1)
    packed = jnp.zeros((1, L), F32)
    for q in range(NQ):
        row = field[0, q, 0:1, :]
        packed = jnp.where(lane == q, jnp.sum(jnp.where(lane == 0, row, 0.0)), packed)
        packed = jnp.where(lane == q + NQ, jnp.sum(jnp.where(lane == HALF, row, 0.0)), packed)
    send_e[0] = packed
    for r in range(1, nz):
        copy_e(r, gz).start()
    recv_e[gz] = packed
    receive(2)
    receive(3)
    moments(1)
    solve(0)

    for r in range(1, nz):
        copy_e(r, z_sender(r)).wait_recv()
    sources = recv_e[:, 0, :]
    block = lax.broadcasted_iota(jnp.int32, (nz, L), 0)
    plane = lax.broadcasted_iota(jnp.int32, (nz, L), 1)
    constant = (1.0 + extent * extent - 1.0) / extent
    zero_line = []
    for i in range(BZ):
        gap = BZ * (gz - block) + i - plane
        gap = jnp.where(gap < 0, gap + extent, gap).astype(F32)
        weight = constant - (6.0 / extent) * gap * (extent - gap)
        weight = jnp.where(plane < BZ, weight * (ALPHA_HALF / (L * L)), 0.0)
        zero_line.append(jnp.sum(weight * sources))
    solve(1)

    tile_row = lax.broadcasted_iota(jnp.int32, (8, L), 0)
    tile_lane = lax.broadcasted_iota(jnp.int32, (8, L), 1)

    def evaluate(h):
        rate = decay[h]
        scale = factor[h]
        for r in range(nz):
            copy_c(h, r, z_sender(r)).wait_recv()
        outside = recv_c[h].reshape(L, L)
        inside = power4(rate) * outside + keep[h]
        outside = swap(outside)
        down = rate * jnp.where(left, inside, outside)
        for q in range(NQ - 1, -1, -1):
            recv_a[h, q] = down
            if q > 0:
                down = rate * (down + field[h, q])
        up = jnp.where(left, outside, inside)
        for q in range(NQ):
            up = field[h, q] + (rate * up if q > 0 else up)
            recv_a[h, q] = scale * (up + recv_a[h, q])
            if h == 0:
                low = jnp.where((tile_row == 0) & (tile_lane == 0), zero_line[q], 0.0)
                high = jnp.where(
                    (tile_row == 0) & (tile_lane == HALF), zero_line[q + NQ], 0.0
                )
                recv_a[h, q, 0:8, :] += low + high

    def inverse(h, lo, hi):
        data = transform_y([recv_a[h, q] for q in range(lo, hi)], mat_y[...])
        for q in range(lo, hi):
            send_d[h, q] = data[q - lo]
            edge = send_d[h, q, pl.ds(0, ny, stride=BY), :]
            edge_d[pl.ds(h * NQ + q, ny, stride=BZ), :] = pltpu.roll(edge, ny - 1, 0)

    evaluate(0)
    inverse(0, 0, 2)
    start_d(0)
    inverse(0, 2, 4)
    evaluate(1)
    inverse(1, 0, 2)
    start_d(1)
    inverse(1, 2, 4)
    for r in range(1, ny):
        copy_edge_d(r, gy).start()
    own_edge_d.start()
    for n in range(2, len(BACK)):
        start_d(n)

    for r in range(1, ny):
        for n in range(len(FORTH)):
            copy_a(n, r, gy).wait_send()
        copy_edge_a(r, gy).wait_send()
    for r in range(nz):
        for h in range(2):
            copy_b(h, r, gz).wait_send()
            copy_c(h, r, gz).wait_send()
    for r in range(1, nz):
        copy_e(r, gz).wait_send()
    copy_up.wait_send()

    def fill(plane, value):
        for s in range(0, BY, 8):
            g = exponent([value(c, s) for c in range(NC)])
            for k in range(18):
                turn[plane, k, s : s + 8] = g[k]

    def rotate(z, directions):
        for s in range(0, BY, 8):
            g = [turn[z, k, s : s + 8] for k in range(18)]
            for mu in directions:
                if mu == 0:
                    ahead = [pltpu.roll(x, L - 1, 1) for x in g]
                elif mu == 1:
                    ahead = [turn[z, k, s + 1 : s + 9] for k in range(18)]
                else:
                    ahead = [turn[z + 1, k, s : s + 8] for k in range(18)]
                rotate_link(link, out, mu, z, s, g, ahead)

    def arrive(n):
        own_d(n).wait()
        for r in range(1, ny):
            copy_d(n, r, y_sender(r)).wait_recv()

    def collect(lo, hi):
        planes = []
        for q in range(lo, hi):
            planes += pair(main[0, :, q].reshape(L, L), main[1, :, q].reshape(L, L))
        data = transform_x(planes, mat_x[...])
        for q in range(lo, hi):
            smooth[q] = data[2 * (q - lo)].reshape(NC, BY, L)
            smooth[q + NQ] = data[2 * (q - lo) + 1].reshape(NC, BY, L)

    def fill_plane(z):
        fill(z, lambda c, s: smooth[z, c, s : s + 8])
        for k in range(18):
            turn[z, k, BY : BY + 1] = turn_edge[k, pl.ds(z, 1)]

    def around(t, first):
        z = first + t * NQ
        fill_plane(z)
        rotate(z, (0, 1))
        return first

    def along_z(t, first):
        rotate(first + t * NQ, (2,))
        return first

    arrive(0)
    arrive(1)
    collect(0, 2)
    copy_down.start()
    own_edge_d.wait()
    for r in range(1, ny):
        copy_edge_d(r, y_sender(r)).wait_recv()
    edge_g[...] = transform_x([pair_edge(edge_g[...])], mat_x[...])[0]
    g = exponent([edge_g[c * BZ : (c + 1) * BZ] for c in range(NC)])
    for k in range(18):
        turn_edge[k] = g[k]
    lax.fori_loop(0, 2, around, 0)
    lax.fori_loop(0, 2, around, 1)
    lax.fori_loop(0, 2, along_z, 0)
    arrive(2)
    arrive(3)
    collect(2, 3)
    lax.fori_loop(0, 2, around, 2)
    lax.fori_loop(0, 2, along_z, 1)
    arrive(4)
    arrive(5)
    collect(3, 4)
    lax.fori_loop(0, 2, around, 3)
    lax.fori_loop(0, 2, along_z, 2)
    copy_down.wait_recv()
    fill(BZ, lambda c, s: above_z[c, s : s + 8])
    lax.fori_loop(0, 2, along_z, 3)

    for r in range(1, ny):
        for n in range(len(BACK)):
            copy_d(n, r, gy).wait_send()
        copy_edge_d(r, gy).wait_send()
    copy_down.wait_send()


def rotate_link(link, out, mu, z, s, g, ahead):
    u = [link[mu, p, i, j, z, s : s + 8] for p in range(2) for i in range(3) for j in range(3)]
    for i in range(3):
        left = []
        for k in range(3):
            re = im = None
            for j in range(3):
                ar, ai = g[3 * i + j], g[9 + 3 * i + j]
                br, bi = u[3 * j + k], u[9 + 3 * j + k]
                tr = ar * br - ai * bi
                ti = ar * bi + ai * br
                re = tr if re is None else re + tr
                im = ti if im is None else im + ti
            left.append((re, im))
        for l in range(3):
            re = im = None
            for k in range(3):
                ar, ai = left[k]
                br, bi = ahead[3 * l + k], ahead[9 + 3 * l + k]
                tr = ar * br + ai * bi
                ti = ai * br - ar * bi
                re = tr if re is None else re + tr
                im = ti if im is None else im + ti
            out[mu, 0, i, l, z, s : s + 8] = re
            out[mu, 1, i, l, z, s : s + 8] = im


def fix(links, nz, ny):
    mat_x, mat_y, decay, factor = tables()
    lines = L // nz
    vmem = pltpu.VMEM
    dma = pltpu.SemaphoreType.DMA
    return pl.pallas_call(
        functools.partial(fix_kernel, nz, ny),
        out_shape=pltpu.VMEM(links.shape, F32),
        in_specs=[pl.BlockSpec(memory_space=pltpu.HBM)] * 5,
        out_specs=pl.BlockSpec(memory_space=pltpu.VMEM),
        scratch_shapes=[
            vmem((3, 2, 3, 3, BZ, BY, L), F32),
            vmem((NC, BZ, BY, L), F32),
            vmem((2, NC, NQ, BY, L), F32),
            vmem((NC * BZ, L), F32),
            vmem((2, NQ, L, L), F32),
            vmem((ny * BZ, L), F32),
            vmem((NC, BY, L), F32),
            vmem((NC, BY, L), F32),
            vmem((2, NQ, L, L), F32),
            vmem((2, L, L), F32),
            vmem((2, nz, lines, L), F32),
            vmem((2, nz, lines, L), F32),
            vmem((1, 1, L), F32),
            vmem((nz, 1, L), F32),
            vmem((2, nz, lines, L), F32),
            vmem((2, nz, lines, L), F32),
            vmem((2, NQ, L, L), F32),
            vmem((ny * BZ, L), F32),
            vmem((2, NC, NQ, BY, L), F32),
            vmem((BZ, NC, BY, L), F32),
            vmem((NC, BY, L), F32),
            vmem((NC * BZ, L), F32),
            vmem((2 * L, 2 * L), BF16),
            vmem((2 * L, 2 * L), BF16),
            vmem((2, L, L), F32),
            vmem((2, L, L), F32),
            vmem((BZ + 1, 18, BY + 8, L), F32),
            vmem((18, BZ, L), F32),
            dma((3, BZ)),
            dma((4,)),
            dma((2, len(BACK))),
            dma((2,)),
            dma((len(FORTH), ny)),
            dma((len(FORTH), ny)),
            dma((3, nz)),
            dma((3, nz)),
            dma((2, nz)),
            dma((2, nz)),
            dma((len(BACK), ny)),
            dma((len(BACK), ny)),
            dma((2, ny)),
            dma((2, ny)),
            dma((2,)),
            dma((2,)),
            pltpu.SemaphoreType.REGULAR((2,)),
        ],
        compiler_params=pltpu.CompilerParams(
            collective_id=0, has_side_effects=True, vmem_limit_bytes=32 << 20
        ),
        name="fix",
    )(*(pltpu.with_memory_space_constraint(jnp.asarray(x), pltpu.HBM)
        for x in (links, mat_x, mat_y, decay, factor)))


def exponent(h):
    h2 = -(h[0] + h[1])
    diag = (h[0], h[1], h2)
    re01, im01 = h[3], -h[2]
    re02, im02 = h[5], -h[4]
    re12, im12 = h[7], -h[6]
    n01 = re01 * re01 + im01 * im01
    n02 = re02 * re02 + im02 * im02
    n12 = re12 * re12 + im12 * im12
    s0 = h[0] * h[0] + n01 + n02
    s1 = h[1] * h[1] + n01 + n12
    s2 = h2 * h2 + n02 + n12
    s01re = re02 * re12 + im02 * im12 - h2 * re01
    s01im = im02 * re12 - re02 * im12 - h2 * im01
    s02re = re01 * re12 - im01 * im12 - h[1] * re02
    s02im = re01 * im12 + im01 * re12 - h[1] * im02
    s12re = re01 * re02 + im01 * im02 - h[0] * re12
    s12im = re01 * im02 - im01 * re02 - h[0] * im12
    p = 0.5 * (s0 + s1 + s2)
    cross = (re01 * re12 - im01 * im12) * re02 + (re01 * im12 + im01 * re12) * im02
    d = h[0] * h[1] * h2 + 2.0 * cross - h[0] * n12 - h[1] * n02 - h2 * n01
    pp = p * p
    dd = d * d
    dp = d * p
    cubes = dd + p * pp
    a0 = 1.0 + dd * (p * (2.0 / 40320.0) - 1.0 / 720.0)
    b0 = d * (-1.0 / 6.0 + p * (1.0 / 120.0) - pp * (1.0 / 5040.0))
    a1 = d * (1.0 / 24.0 - p * (2.0 / 720.0) + pp * (3.0 / 40320.0))
    b1 = 1.0 - p * (1.0 / 6.0) + pp * (1.0 / 120.0) - cubes * (1.0 / 5040.0)
    a2 = -0.5 + p * (1.0 / 24.0) - pp * (1.0 / 720.0) + cubes * (1.0 / 40320.0)
    b2 = d * (1.0 / 120.0) - dp * (2.0 / 5040.0)
    re = {}
    im = {}
    for j, s in enumerate((s0, s1, s2)):
        re[j, j] = a0 + a1 * diag[j] + a2 * s
        im[j, j] = b0 + b1 * diag[j] + b2 * s
    for i, j, hr, hi, sr, si in (
        (0, 1, re01, im01, s01re, s01im),
        (0, 2, re02, im02, s02re, s02im),
        (1, 2, re12, im12, s12re, s12im),
    ):
        rr = a1 * hr + a2 * sr
        ii = b1 * hi + b2 * si
        ri = a1 * hi + a2 * si
        ir = b1 * hr + b2 * sr
        re[i, j] = rr - ii
        im[i, j] = ri + ir
        re[j, i] = rr + ii
        im[j, i] = ir - ri
    return [re[i, j] for i in range(3) for j in range(3)] + [
        im[i, j] for i in range(3) for j in range(3)
    ]


def store_kernel(source, out, sem):
    copies = [
        pltpu.make_async_copy(source.at[mu, p], out.at[mu, p], sem.at[mu, p])
        for mu in range(3)
        for p in range(2)
    ]
    for copy in copies:
        copy.start()
    for copy in copies:
        copy.wait()


def store(source):
    return pl.pallas_call(
        store_kernel,
        out_shape=jax.ShapeDtypeStruct(source.shape, F32),
        in_specs=[pl.BlockSpec(memory_space=pltpu.VMEM)],
        out_specs=pl.BlockSpec(memory_space=pl.ANY),
        scratch_shapes=[pltpu.SemaphoreType.DMA((3, 2))],
        compiler_params=pltpu.CompilerParams(vmem_limit_bytes=16 << 20),
        name="store",
    )(source)


def solution(mesh):
    nz, ny = mesh.shape["gz"], mesh.shape["gy"]

    def body(links):
        return store(fix(links, nz, ny))

    spec = P(None, None, None, None, "gz", "gy", None)
    return jax.shard_map(body, mesh=mesh, in_specs=(spec,), out_specs=spec, check_vma=False)
```

```python
import functools
import math

import jax
import jax.numpy as jnp
import numpy as np
from jax import lax
from jax.experimental import pallas as pl
from jax.experimental.pallas import tpu as pltpu
from jax.sharding import PartitionSpec as P

L = 128
ALPHA_HALF = 0.04
BZ = 8
BY = 16
NC = 8
MESH = pl.DeviceIdType.MESH
F32 = jnp.float32
BF16 = jnp.bfloat16
HALF = L // 2
NQ = BZ // 2
FORTH = ((0, 2, 4), (0, 1, 2), (1, 2, 4), (0, 0, 1), (1, 0, 2))
BACK = ((0, 0, 2), (1, 0, 1), (1, 1, 2), (0, 2, 3), (1, 2, 3), (0, 3, 4), (1, 3, 4))
STEPS = ((1, 2), (0, 2), (1, 1), (1, 3), (0, 1), (0, 3), (1, 0))


def tables():
    k = np.arange(L)
    angle = 2.0 * np.pi / L * (np.outer(k, k) % L)
    hartley = np.cos(angle) + np.sin(angle)
    high = hartley.astype(np.float32).astype(jnp.bfloat16)
    low = (hartley - high.astype(np.float64)).astype(np.float32).astype(jnp.bfloat16)
    half = np.concatenate([high, low], axis=1)
    mat_x = np.concatenate([half, half], axis=0)
    mat_y = np.ascontiguousarray(mat_x.T)
    momentum = 4.0 * np.sin(np.pi * k / L) ** 2
    mass = momentum[:, None] + momentum[None, :]
    mass[0, 0] = 1.0
    root = np.sqrt(mass * mass / 4.0 + mass)
    decay = 1.0 / (1.0 + mass / 2.0 + root)
    factor = 12.0 * ALPHA_HALF / (L * L) / (2.0 * root)
    decay[0, 0] = 0.0
    factor[0, 0] = 0.0
    paired = [
        np.stack([np.tile(t[:, h * HALF : (h + 1) * HALF], (1, 2)) for h in range(2)])
        for t in (decay, factor)
    ]
    return mat_x, mat_y, paired[0].astype(np.float32), paired[1].astype(np.float32)


def split(x):
    high = x.astype(BF16)
    low = (x - high.astype(F32)).astype(BF16)
    return high, low


def transform_x(planes, mat_x):
    high, low = split(jnp.concatenate(planes, axis=0))
    out = jnp.dot(jnp.concatenate([high, low], axis=1), mat_x, preferred_element_type=F32)
    out = out[:, :L] + out[:, L:]
    return [out[i * L : (i + 1) * L] for i in range(len(planes))]


def transform_y(planes, mat_y):
    high, low = split(jnp.concatenate(planes, axis=1))
    out = jnp.dot(mat_y, jnp.concatenate([high, low], axis=0), preferred_element_type=F32)
    out = out[:L] + out[L:]
    return [out[:, i * L : (i + 1) * L] for i in range(len(planes))]


def algebra(re, im):
    trace_part = (im(0, 0) + im(1, 1) + im(2, 2)) * (1.0 / 3.0)
    return [
        im(0, 0) - trace_part,
        im(1, 1) - trace_part,
        (re(0, 1) - re(1, 0)) * 0.5,
        (im(0, 1) + im(1, 0)) * 0.5,
        (re(0, 2) - re(2, 0)) * 0.5,
        (im(0, 2) + im(2, 0)) * 0.5,
        (re(1, 2) - re(2, 1)) * 0.5,
        (im(1, 2) + im(2, 1)) * 0.5,
    ]


def fix_kernel(
    nz,
    ny,
    links,
    mat_x_in,
    mat_y_in,
    decay_in,
    factor_in,
    out,
    link,
    turn,
    base,
    send_a,
    edge_y,
    recv_a,
    edge_r,
    edge_z,
    below_z,
    field,
    keep,
    send_b,
    recv_b,
    send_e,
    recv_e,
    send_c,
    recv_c,
    send_d,
    edge_d,
    main,
    smooth,
    above_z,
    edge_g,
    mat_x,
    mat_y,
    decay,
    factor,
    turn_edge,
    load_sem,
    small_sem,
    a_send,
    a_recv,
    b_send,
    b_recv,
    c_send,
    c_recv,
    d_send,
    d_recv,
    e_send,
    e_recv,
    z_send,
    z_recv,
    ring,
):
    gz = lax.axis_index("gz")
    gy = lax.axis_index("gy")
    lines = L // nz
    extent = nz * BZ

    side = ny // 2
    half = nz // 2
    my_z, my_y = lax.div(gy, side), lax.rem(gy, side)

    def y_target(r):
        a, b = STEPS[r - 1]
        return lax.rem(my_z + a, 2) * side + lax.rem(my_y + b, side)

    def y_sender(r):
        a, b = STEPS[r - 1]
        return lax.rem(my_z + 2 - a, 2) * side + lax.rem(my_y + side - b, side)

    def z_target(r):
        return lax.rem(gz + r, nz)

    def z_sender(r):
        return lax.rem(gz + nz - r, nz)

    my_half, my_place = lax.div(gz, half), lax.rem(gz, half)

    def near(r):
        return my_half * half + lax.rem(my_place + r, half)

    between = lax.rem(gy + side, ny)

    barrier = pltpu.get_barrier_semaphore()
    for r in range(1, ny):
        pl.semaphore_signal(barrier, inc=1, device_id=(gz, y_target(r)), device_id_type=MESH)
    for device in [z_target(half), z_target(1), z_target(nz - 1)] + [
        near(r) for r in range(1, half)
    ]:
        pl.semaphore_signal(barrier, inc=1, device_id=(device, gy), device_id_type=MESH)

    def load(mu, z, n):
        pltpu.make_async_copy(
            links.at[mu, :, :, :, pl.ds(z, 1)],
            link.at[mu, :, :, :, pl.ds(z, 1)],
            load_sem.at[n],
        ).start()

    def settle(ref, sem):
        pltpu.make_async_copy(ref, ref, sem).wait()

    def loaded(n, planes):
        settle(link.at[0, :, :, :, 0:planes], load_sem.at[n])

    small = [
        pltpu.make_async_copy(src, dst, small_sem.at[n])
        for n, (src, dst) in enumerate(
            ((mat_x_in, mat_x), (mat_y_in, mat_y), (decay_in, decay), (factor_in, factor))
        )
    ]
    for z in range(BZ):
        load(1, z, NQ)
    small[0].start()
    load(2, BZ - 1, NQ + 1)
    load(2, NQ - 1, NQ + 1)
    for q in range(NQ - 1, -1, -1):
        if q > 0:
            load(2, q + NQ - 1, q)
            load(2, q - 1, q)
        load(0, q + NQ, q)
        load(0, q, q)
    for copy in small[1:]:
        copy.start()

    def remote(src, dst, send, recv, device):
        return pltpu.make_async_remote_copy(
            src_ref=src,
            dst_ref=dst,
            send_sem=send,
            recv_sem=recv,
            device_id=device,
            device_id_type=MESH,
        )

    def rows(block):
        return pl.ds(pl.multiple_of(block * BY, BY), BY)

    def tile(block):
        return pl.ds(pl.multiple_of(block * BZ, BZ), BZ)

    def copy_a(n, r, sender):
        h, lo, hi = FORTH[n]
        return remote(
            send_a.at[h, y_target(r), lo:hi],
            recv_a.at[h, lo:hi, rows(sender)],
            a_send.at[0],
            a_recv.at[n],
            (gz, y_target(r)),
        )

    def own_a(n):
        h, lo, hi = FORTH[n]
        return pltpu.make_async_copy(
            send_a.at[h, gy, lo:hi], recv_a.at[h, lo:hi, rows(gy)], a_recv.at[n]
        )

    def start_a(n):
        for r in range(1, ny):
            copy_a(n, r, gy).start()
        own_a(n).start()

    def copy_edge_a(r, sender):
        return remote(
            edge_y.at[tile(y_target(r))],
            edge_r.at[tile(sender)],
            e_send.at[0],
            e_recv.at[0],
            (gz, y_target(r)),
        )

    def copy_b(h, r, sender):
        return remote(
            send_b.at[h, z_target(r)],
            recv_b.at[h, sender],
            b_send.at[0],
            b_recv.at[h],
            (z_target(r), between),
        )

    def copy_e(r, sender):
        return remote(
            send_e.at[0],
            recv_e.at[sender],
            b_send.at[1],
            b_recv.at[2],
            (z_target(r), gy),
        )

    def copy_c(h, r, sender):
        return remote(
            send_c.at[h, z_target(r)],
            recv_c.at[h, sender],
            c_send.at[0],
            c_recv.at[h],
            (z_target(r), between),
        )

    def copy_d(n, r, owner):
        h, lo, hi = BACK[n]
        return remote(
            send_d.at[h, lo:hi, rows(y_target(r))],
            main.at[h, owner, lo:hi],
            d_send.at[0],
            d_recv.at[n],
            (gz, y_target(r)),
        )

    def own_d(n):
        h, lo, hi = BACK[n]
        return pltpu.make_async_copy(
            send_d.at[h, lo:hi, rows(gy)], main.at[h, gy, lo:hi], d_recv.at[n]
        )

    def start_d(n):
        for r in range(1, ny):
            copy_d(n, r, gy).start()
        own_d(n).start()

    def copy_edge_d(r, owner):
        return remote(
            edge_d.at[tile(y_target(r))],
            edge_g.at[tile(owner)],
            e_send.at[1],
            e_recv.at[1],
            (gz, y_target(r)),
        )

    copy_up = remote(edge_z, below_z, z_send.at[0], z_recv.at[0], (z_target(1), gy))
    copy_down = remote(smooth.at[0], above_z, z_send.at[1], z_recv.at[1], (z_target(nz - 1), gy))
    own_edge_a = pltpu.make_async_copy(edge_y.at[tile(gy)], edge_r.at[tile(gy)], e_recv.at[0])
    own_edge_d = pltpu.make_async_copy(edge_d.at[tile(gy)], edge_g.at[tile(gy)], e_recv.at[1])

    first_row = lax.broadcasted_iota(jnp.int32, (BY, L), 0) == 0
    left = lax.broadcasted_iota(jnp.int32, (L, L), 1) < HALF
    straight = (lax.broadcasted_iota(jnp.int32, (NC, BZ, L), 2) < HALF) == (
        lax.broadcasted_iota(jnp.int32, (NC, BZ, L), 1) < NQ
    )

    def swap(x):
        return pltpu.roll(x, HALF, 1)

    def pair(x, y):
        return jnp.where(left, x, swap(y)), jnp.where(left, swap(x), y)

    def pair_edge(x):
        other = pltpu.roll(swap(x).reshape(NC, BZ, L), NQ, 1)
        return jnp.where(straight, x.reshape(NC, BZ, L), other).reshape(NC * BZ, L)

    def parts(mu, z):
        return algebra(
            lambda i, j: link[mu, 0, i, j, z], lambda i, j: link[mu, 1, i, j, z]
        )

    def part_y(z, carry):
        along = parts(1, z)
        for c in range(NC):
            behind = jnp.where(first_row, 0.0, pltpu.roll(along[c], 1, 0))
            base[c, z] = behind - along[c]
            edge_y[pl.ds(c * BZ + z, 1), :] = along[c][BY - 1 : BY]
        return carry

    loaded(NQ, BZ)
    lax.fori_loop(0, BZ, part_y, 0)
    loaded(NQ + 1, 2)
    top = parts(2, BZ - 1)
    for c in range(NC):
        edge_z[c] = top[c]
    pl.semaphore_wait(barrier, ny + half + 1)
    copy_up.start()
    for r in range(1, half):
        pl.semaphore_signal(ring.at[0], inc=1, device_id=(near(r), gy), device_id_type=MESH)

    def divergence(z, under, here):
        along = parts(0, z)
        return jnp.concatenate(
            [
                base[c, z] + (pltpu.roll(along[c], 1, 1) - along[c]) + (under[c] - here[c])
                for c in range(NC)
            ],
            axis=0,
        )

    def spread(q, low, high):
        low, high = transform_x([low, high], mat_x[...])
        low, high = pair(low, high)
        send_a[0, :, q] = low.reshape(NC, BY, L)
        send_a[1, :, q] = high.reshape(NC, BY, L)

    def step(t, carry):
        here_low, here_high = carry
        q = NQ - 1 - t
        loaded(q, 4)
        under_low = parts(2, q - 1)
        under_high = parts(2, q + NQ - 1)
        spread(
            q, divergence(q, under_low, here_low), divergence(q + NQ, under_high, here_high)
        )
        return under_low, under_high

    small[0].wait()
    carry = (parts(2, NQ - 1), top)
    carry = lax.fori_loop(0, 2, step, carry)
    start_a(0)
    edge_y[...] = pair_edge(transform_x([edge_y[...]], mat_x[...])[0])
    for r in range(1, ny):
        copy_edge_a(r, gy).start()
    own_edge_a.start()
    carry = lax.fori_loop(2, NQ - 1, step, carry)
    start_a(1)
    start_a(2)
    loaded(0, 2)
    high = divergence(NQ, parts(2, NQ - 1), carry[1])
    copy_up.wait_recv()
    spread(0, divergence(0, [below_z[c] for c in range(NC)], carry[0]), high)
    start_a(3)
    start_a(4)
    if half > 1:
        pl.semaphore_wait(ring.at[0], half - 1)
    pl.semaphore_signal(
        ring.at[1], inc=1, device_id=(z_target(half), gy), device_id_type=MESH
    )

    for copy in small[1:]:
        copy.wait()
    settle(edge_r, e_recv.at[0])

    def receive(n):
        h, lo, hi = FORTH[n]
        settle(recv_a.at[h, lo:hi], a_recv.at[n])
        for q in range(lo, hi):
            edge = pltpu.roll(edge_r[pl.ds(h * NQ + q, ny, stride=BZ), :], 1, 0)
            recv_a[h, q, pl.ds(0, ny, stride=BY), :] += edge
        data = transform_y([recv_a[h, q] for q in range(lo, hi)], mat_y[...])
        for q in range(lo, hi):
            field[h, q] = data[q - lo]

    def power4(x):
        x = x * x
        return x * x

    def moments(h):
        rate = decay[h]
        rate4 = power4(rate)
        up = field[h, 0]
        down = field[h, NQ - 1]
        for q in range(1, NQ):
            up = field[h, q] + rate * up
            down = field[h, NQ - 1 - q] + rate * down
        up = rate * up
        swapped = jnp.where(left, swap(down), swap(up))
        keep[h] = swapped
        send_b[h] = (jnp.where(left, down, up) + rate4 * swapped).reshape(nz, lines, L)
        for r in range(nz):
            copy_b(h, r, gz).start()

    narrow = lax.broadcasted_iota(jnp.int32, (lines, L), 1) < HALF

    def solve(h):
        rate8 = decay[h, pl.ds(pl.multiple_of(gz * lines, lines), lines), :]
        rate8 = power4(rate8 * rate8)
        whole = rate8
        for _ in range(int(math.log2(nz))):
            whole = whole * whole
        images = 1.0 / (1.0 - whole)
        settle(recv_b.at[h], b_recv.at[h])
        mixed = [
            jnp.where(narrow, recv_b[h, nz - 1 - j], recv_b[h, j]) for j in range(nz)
        ]
        state = mixed[0]
        for j in range(1, nz):
            state = mixed[j] + rate8 * state
        state = state * images
        result = []
        for j in range(nz):
            result.append(state)
            state = mixed[j] + rate8 * state
        for j in range(nz):
            send_c[h, j] = jnp.where(narrow, result[nz - 1 - j], result[j])
        for r in range(nz):
            copy_c(h, r, gz).start()

    receive(0)
    receive(1)
    receive(2)
    receive(3)
    pl.semaphore_wait(ring.at[1], 1)
    moments(0)
    lane = lax.broadcasted_iota(jnp.int32, (1, L), 1)
    packed = jnp.zeros((1, L), F32)
    for q in range(NQ):
        row = field[0, q, 0:1, :]
        packed = jnp.where(lane == q, jnp.sum(jnp.where(lane == 0, row, 0.0)), packed)
        packed = jnp.where(lane == q + NQ, jnp.sum(jnp.where(lane == HALF, row, 0.0)), packed)
    send_e[0] = packed
    for r in range(1, nz):
        copy_e(r, gz).start()
    recv_e[gz] = packed
    receive(4)
    moments(1)
    solve(0)

    settle(recv_e.at[0 : nz - 1], b_recv.at[2])
    sources = recv_e[:, 0, :]
    block = lax.broadcasted_iota(jnp.int32, (nz, L), 0)
    plane = lax.broadcasted_iota(jnp.int32, (nz, L), 1)
    constant = (1.0 + extent * extent - 1.0) / extent
    zero_line = []
    for i in range(BZ):
        gap = BZ * (gz - block) + i - plane
        gap = jnp.where(gap < 0, gap + extent, gap).astype(F32)
        weight = constant - (6.0 / extent) * gap * (extent - gap)
        weight = jnp.where(plane < BZ, weight * (ALPHA_HALF / (L * L)), 0.0)
        zero_line.append(jnp.sum(weight * sources))
    solve(1)

    tile_row = lax.broadcasted_iota(jnp.int32, (8, L), 0)
    tile_lane = lax.broadcasted_iota(jnp.int32, (8, L), 1)

    def evaluate(h):
        rate = decay[h]
        scale = factor[h]
        settle(recv_c.at[h], c_recv.at[h])
        outside = recv_c[h].reshape(L, L)
        inside = power4(rate) * outside + keep[h]
        outside = swap(outside)
        down = rate * jnp.where(left, inside, outside)
        for q in range(NQ - 1, -1, -1):
            recv_a[h, q] = down
            if q > 0:
                down = rate * (down + field[h, q])
        up = jnp.where(left, outside, inside)
        for q in range(NQ):
            up = field[h, q] + (rate * up if q > 0 else up)
            recv_a[h, q] = scale * (up + recv_a[h, q])
            if h == 0:
                low = jnp.where((tile_row == 0) & (tile_lane == 0), zero_line[q], 0.0)
                high = jnp.where(
                    (tile_row == 0) & (tile_lane == HALF), zero_line[q + NQ], 0.0
                )
                recv_a[h, q, 0:8, :] += low + high

    def inverse(h, lo, hi):
        data = transform_y([recv_a[h, q] for q in range(lo, hi)], mat_y[...])
        for q in range(lo, hi):
            send_d[h, q] = data[q - lo]
            edge = send_d[h, q, pl.ds(0, ny, stride=BY), :]
            edge_d[pl.ds(h * NQ + q, ny, stride=BZ), :] = pltpu.roll(edge, ny - 1, 0)

    evaluate(0)
    inverse(0, 0, 2)
    start_d(0)
    inverse(0, 2, 4)
    evaluate(1)
    inverse(1, 0, 2)
    start_d(1)
    start_d(2)
    inverse(1, 2, 4)
    for r in range(1, ny):
        copy_edge_d(r, gy).start()
    own_edge_d.start()
    for n in range(3, len(BACK)):
        start_d(n)

    settle(send_a.at[:, 0 : ny - 1], a_send.at[0])
    settle(edge_y.at[0 : (ny - 1) * BZ], e_send.at[0])
    settle(send_b, b_send.at[0])
    settle(send_c, c_send.at[0])
    settle(recv_e.at[0 : nz - 1], b_send.at[1])
    copy_up.wait_send()

    def fill(plane, value):
        for s in range(0, BY, 8):
            g = exponent([value(c, s) for c in range(NC)])
            for k in range(18):
                turn[plane, k, s : s + 8] = g[k]

    def rotate(z, directions):
        rotate_plane(link, turn, out, z, directions)

    def arrive(n):
        h, lo, hi = BACK[n]
        settle(main.at[h, :, lo:hi], d_recv.at[n])

    def collect(lo, hi):
        planes = []
        for q in range(lo, hi):
            planes += pair(main[0, :, q].reshape(L, L), main[1, :, q].reshape(L, L))
        data = transform_x(planes, mat_x[...])
        for q in range(lo, hi):
            smooth[q] = data[2 * (q - lo)].reshape(NC, BY, L)
            smooth[q + NQ] = data[2 * (q - lo) + 1].reshape(NC, BY, L)

    def fill_plane(z):
        fill(z, lambda c, s: smooth[z, c, s : s + 8])

    def add_edge(z):
        for k in range(18):
            turn[z, k, BY : BY + 1] = turn_edge[k, pl.ds(z, 1)]

    def along_z(t, first):
        rotate(first + t * NQ, (2,))
        return first

    def around(t, first):
        z = first + t * NQ
        add_edge(z)
        rotate(z, (0, 1))
        return first

    def fill_pair(q):
        lax.fori_loop(0, 2, lambda t, first: (fill_plane(first + t * NQ), first)[1], q)

    arrive(0)
    arrive(1)
    collect(0, 1)
    copy_down.start()
    fill_pair(0)
    settle(edge_g, e_recv.at[1])
    edge_g[...] = transform_x([pair_edge(edge_g[...])], mat_x[...])[0]
    g = exponent([edge_g[c * BZ : (c + 1) * BZ] for c in range(NC)])
    for k in range(18):
        turn_edge[k] = g[k]
    lax.fori_loop(0, 2, around, 0)
    for n, q in ((2, 1), (4, 2)):
        arrive(n)
        if q > 1:
            arrive(n - 1)
        collect(q, q + 1)
        fill_pair(q)
        lax.fori_loop(0, 2, around, q)
        lax.fori_loop(0, 2, along_z, q - 1)
    arrive(5)
    arrive(6)
    collect(3, 4)
    fill_pair(3)
    lax.fori_loop(0, 2, lambda t, first: (add_edge(first + t * NQ), first)[1], 3)
    copy_down.wait_recv()
    fill(BZ, lambda c, s: above_z[c, s : s + 8])

    settle(send_d.at[:, :, 0 : (ny - 1) * BY], d_send.at[0])
    settle(edge_d.at[0 : (ny - 1) * BZ], e_send.at[1])
    copy_down.wait_send()


def rotate_plane(link, turn, out, z, directions):
    for s in range(0, BY, 8):
        g = [turn[z, k, s : s + 8] for k in range(18)]
        for mu in directions:
            if mu == 0:
                ahead = [pltpu.roll(x, L - 1, 1) for x in g]
            elif mu == 1:
                ahead = [turn[z, k, s + 1 : s + 9] for k in range(18)]
            else:
                ahead = [turn[z + 1, k, s : s + 8] for k in range(18)]
            rotate_link(link, out, mu, z, s, g, ahead)


def rotate_link(link, out, mu, z, s, g, ahead):
    u = [link[mu, p, i, j, z, s : s + 8] for p in range(2) for i in range(3) for j in range(3)]
    for i in range(3):
        left = []
        for k in range(3):
            re = im = None
            for j in range(3):
                ar, ai = g[3 * i + j], g[9 + 3 * i + j]
                br, bi = u[3 * j + k], u[9 + 3 * j + k]
                tr = ar * br - ai * bi
                ti = ar * bi + ai * br
                re = tr if re is None else re + tr
                im = ti if im is None else im + ti
            left.append((re, im))
        for l in range(3):
            re = im = None
            for k in range(3):
                ar, ai = left[k]
                br, bi = ahead[3 * l + k], ahead[9 + 3 * l + k]
                tr = ar * br + ai * bi
                ti = ai * br - ar * bi
                re = tr if re is None else re + tr
                im = ti if im is None else im + ti
            out[mu, 0, i, l, z, s : s + 8] = re
            out[mu, 1, i, l, z, s : s + 8] = im


def fix(links, nz, ny):
    mat_x, mat_y, decay, factor = tables()
    lines = L // nz
    vmem = pltpu.VMEM
    dma = pltpu.SemaphoreType.DMA
    return pl.pallas_call(
        functools.partial(fix_kernel, nz, ny),
        out_shape=(
            pltpu.VMEM(links.shape, F32),
            pltpu.VMEM(links.shape, F32),
            pltpu.VMEM((BZ + 1, 18, BY + 8, L), F32),
        ),
        in_specs=[pl.BlockSpec(memory_space=pltpu.HBM)] * 5,
        out_specs=(pl.BlockSpec(memory_space=pltpu.VMEM),) * 3,
        scratch_shapes=[
            vmem((NC, BZ, BY, L), F32),
            vmem((2, NC, NQ, BY, L), F32),
            vmem((NC * BZ, L), F32),
            vmem((2, NQ, L, L), F32),
            vmem((ny * BZ, L), F32),
            vmem((NC, BY, L), F32),
            vmem((NC, BY, L), F32),
            vmem((2, NQ, L, L), F32),
            vmem((2, L, L), F32),
            vmem((2, nz, lines, L), F32),
            vmem((2, nz, lines, L), F32),
            vmem((1, 1, L), F32),
            vmem((nz, 1, L), F32),
            vmem((2, nz, lines, L), F32),
            vmem((2, nz, lines, L), F32),
            vmem((2, NQ, L, L), F32),
            vmem((ny * BZ, L), F32),
            vmem((2, NC, NQ, BY, L), F32),
            vmem((BZ, NC, BY, L), F32),
            vmem((NC, BY, L), F32),
            vmem((NC * BZ, L), F32),
            vmem((2 * L, 2 * L), BF16),
            vmem((2 * L, 2 * L), BF16),
            vmem((2, L, L), F32),
            vmem((2, L, L), F32),
            vmem((18, BZ, L), F32),
            dma((NQ + 2,)),
            dma((4,)),
            dma((1,)),
            dma((len(FORTH),)),
            dma((2,)),
            dma((3,)),
            dma((1,)),
            dma((2,)),
            dma((1,)),
            dma((len(BACK),)),
            dma((2,)),
            dma((2,)),
            dma((2,)),
            dma((2,)),
            pltpu.SemaphoreType.REGULAR((2,)),
        ],
        compiler_params=pltpu.CompilerParams(
            collective_id=0, has_side_effects=True, vmem_limit_bytes=32 << 20
        ),
        name="fix",
    )(*(pltpu.with_memory_space_constraint(jnp.asarray(x), pltpu.HBM)
        for x in (links, mat_x, mat_y, decay, factor)))


def exponent(h):
    h2 = -(h[0] + h[1])
    diag = (h[0], h[1], h2)
    re01, im01 = h[3], -h[2]
    re02, im02 = h[5], -h[4]
    re12, im12 = h[7], -h[6]
    n01 = re01 * re01 + im01 * im01
    n02 = re02 * re02 + im02 * im02
    n12 = re12 * re12 + im12 * im12
    s0 = h[0] * h[0] + n01 + n02
    s1 = h[1] * h[1] + n01 + n12
    s2 = h2 * h2 + n02 + n12
    s01re = re02 * re12 + im02 * im12 - h2 * re01
    s01im = im02 * re12 - re02 * im12 - h2 * im01
    s02re = re01 * re12 - im01 * im12 - h[1] * re02
    s02im = re01 * im12 + im01 * re12 - h[1] * im02
    s12re = re01 * re02 + im01 * im02 - h[0] * re12
    s12im = re01 * im02 - im01 * re02 - h[0] * im12
    p = 0.5 * (s0 + s1 + s2)
    cross = (re01 * re12 - im01 * im12) * re02 + (re01 * im12 + im01 * re12) * im02
    d = h[0] * h[1] * h2 + 2.0 * cross - h[0] * n12 - h[1] * n02 - h2 * n01
    pp = p * p
    dd = d * d
    dp = d * p
    cubes = dd + p * pp
    a0 = 1.0 + dd * (p * (2.0 / 40320.0) - 1.0 / 720.0)
    b0 = d * (-1.0 / 6.0 + p * (1.0 / 120.0) - pp * (1.0 / 5040.0))
    a1 = d * (1.0 / 24.0 - p * (2.0 / 720.0) + pp * (3.0 / 40320.0))
    b1 = 1.0 - p * (1.0 / 6.0) + pp * (1.0 / 120.0) - cubes * (1.0 / 5040.0)
    a2 = -0.5 + p * (1.0 / 24.0) - pp * (1.0 / 720.0) + cubes * (1.0 / 40320.0)
    b2 = d * (1.0 / 120.0) - dp * (2.0 / 5040.0)
    re = {}
    im = {}
    for j, s in enumerate((s0, s1, s2)):
        re[j, j] = a0 + a1 * diag[j] + a2 * s
        im[j, j] = b0 + b1 * diag[j] + b2 * s
    for i, j, hr, hi, sr, si in (
        (0, 1, re01, im01, s01re, s01im),
        (0, 2, re02, im02, s02re, s02im),
        (1, 2, re12, im12, s12re, s12im),
    ):
        rr = a1 * hr + a2 * sr
        ii = b1 * hi + b2 * si
        ri = a1 * hi + a2 * si
        ir = b1 * hr + b2 * sr
        re[i, j] = rr - ii
        im[i, j] = ri + ir
        re[j, i] = rr + ii
        im[j, i] = ir - ri
    return [re[i, j] for i in range(3) for j in range(3)] + [
        im[i, j] for i in range(3) for j in range(3)
    ]


def store_kernel(source, link, turn, out, last, sem):
    def put(src, lo, hi, mus):
        for mu in mus:
            pltpu.make_async_copy(
                src.at[mu, :, :, :, lo:hi], out.at[mu, :, :, :, lo:hi], sem.at[0]
            ).start()

    put(source, 0, 2, (0, 1, 2))
    put(source, NQ, NQ + 2, (0, 1, 2))
    put(source, 2, 3, (0, 1))
    put(source, NQ + 2, NQ + 3, (0, 1))
    for z in (2, NQ + 2):
        rotate_plane(link, turn, last, z, (2,))
        put(last, z, z + 1, (2,))
    for z in (3, NQ + 3):
        rotate_plane(link, turn, last, z, (0, 1, 2))
        put(last, z, z + 1, (0, 1, 2))
    pltpu.make_async_copy(source, out, sem.at[0]).wait()


def store(source, link, turn):
    return pl.pallas_call(
        store_kernel,
        out_shape=jax.ShapeDtypeStruct(source.shape, F32),
        in_specs=[pl.BlockSpec(memory_space=pltpu.VMEM)] * 3,
        out_specs=pl.BlockSpec(memory_space=pl.ANY),
        scratch_shapes=[
            pltpu.VMEM((3, 2, 3, 3, BZ, BY, L), F32),
            pltpu.SemaphoreType.DMA((1,)),
        ],
        compiler_params=pltpu.CompilerParams(vmem_limit_bytes=16 << 20),
        name="store",
    )(source, link, turn)


def solution(mesh):
    nz, ny = mesh.shape["gz"], mesh.shape["gy"]

    def body(links):
        return store(*fix(links, nz, ny))

    spec = P(None, None, None, None, "gz", "gy", None)
    return jax.shard_map(body, mesh=mesh, in_specs=(spec,), out_specs=spec, check_vma=False)
```

```python
import functools
import math

import jax
import jax.numpy as jnp
import numpy as np
from jax import lax
from jax.experimental import pallas as pl
from jax.experimental.pallas import tpu as pltpu
from jax.sharding import PartitionSpec as P

L = 128
ALPHA_HALF = 0.04
BZ = 8
BY = 16
NC = 8
MESH = pl.DeviceIdType.MESH
F32 = jnp.float32
BF16 = jnp.bfloat16
HALF = L // 2
NQ = BZ // 2
FORTH = ((0, 2, 4), (0, 1, 2), (0, 0, 1), (1, 2, 4), (1, 0, 2))
BACK = ((0, 0, 2), (0, 2, 3), (1, 0, 1), (1, 1, 2), (1, 2, 3), (0, 3, 4), (1, 3, 4))
STEPS = ((1, 2), (0, 2), (1, 1), (1, 3), (0, 1), (0, 3), (1, 0))


def tables():
    k = np.arange(L)
    angle = 2.0 * np.pi / L * (np.outer(k, k) % L)
    hartley = np.cos(angle) + np.sin(angle)
    high = hartley.astype(np.float32).astype(jnp.bfloat16)
    low = (hartley - high.astype(np.float64)).astype(np.float32).astype(jnp.bfloat16)
    half = np.concatenate([high, low], axis=1)
    mat_x = np.concatenate([half, half], axis=0)
    mat_y = np.ascontiguousarray(mat_x.T)
    momentum = 4.0 * np.sin(np.pi * k / L) ** 2
    mass = momentum[:, None] + momentum[None, :]
    mass[0, 0] = 1.0
    root = np.sqrt(mass * mass / 4.0 + mass)
    decay = 1.0 / (1.0 + mass / 2.0 + root)
    factor = 12.0 * ALPHA_HALF / (L * L) / (2.0 * root)
    decay[0, 0] = 0.0
    factor[0, 0] = 0.0
    paired = [
        np.stack([np.tile(t[:, h * HALF : (h + 1) * HALF], (1, 2)) for h in range(2)])
        for t in (decay, factor)
    ]
    return mat_x, mat_y, paired[0].astype(np.float32), paired[1].astype(np.float32)


def split(x):
    high = x.astype(BF16)
    low = (x - high.astype(F32)).astype(BF16)
    return high, low


def transform_x(planes, mat_x):
    high, low = split(jnp.concatenate(planes, axis=0))
    out = jnp.dot(jnp.concatenate([high, low], axis=1), mat_x, preferred_element_type=F32)
    out = out[:, :L] + out[:, L:]
    return [out[i * L : (i + 1) * L] for i in range(len(planes))]


def transform_y(planes, mat_y):
    high, low = split(jnp.concatenate(planes, axis=1))
    out = jnp.dot(mat_y, jnp.concatenate([high, low], axis=0), preferred_element_type=F32)
    out = out[:L] + out[L:]
    return [out[:, i * L : (i + 1) * L] for i in range(len(planes))]


def algebra(re, im):
    trace_part = (im(0, 0) + im(1, 1) + im(2, 2)) * (1.0 / 3.0)
    return [
        im(0, 0) - trace_part,
        im(1, 1) - trace_part,
        (re(0, 1) - re(1, 0)) * 0.5,
        (im(0, 1) + im(1, 0)) * 0.5,
        (re(0, 2) - re(2, 0)) * 0.5,
        (im(0, 2) + im(2, 0)) * 0.5,
        (re(1, 2) - re(2, 1)) * 0.5,
        (im(1, 2) + im(2, 1)) * 0.5,
    ]


def fix_kernel(
    nz,
    ny,
    links,
    mat_x_in,
    mat_y_in,
    decay_in,
    factor_in,
    out,
    link,
    turn,
    base,
    send_a,
    edge_y,
    recv_a,
    edge_r,
    face_s,
    face_r,
    face,
    field,
    keep,
    send_b,
    recv_b,
    send_e,
    recv_e,
    send_c,
    recv_c,
    send_d,
    edge_d,
    main,
    smooth,
    above_z,
    edge_g,
    mat_x,
    mat_y,
    decay,
    factor,
    turn_edge,
    load_sem,
    small_sem,
    a_send,
    a_recv,
    b_send,
    b_recv,
    c_send,
    c_recv,
    d_send,
    d_recv,
    e_send,
    e_recv,
    z_send,
    z_recv,
    ring,
):
    gz = lax.axis_index("gz")
    gy = lax.axis_index("gy")
    lines = L // nz
    extent = nz * BZ

    side = ny // 2
    half = nz // 2
    my_z, my_y = lax.div(gy, side), lax.rem(gy, side)

    def y_target(r):
        a, b = STEPS[r - 1]
        return lax.rem(my_z + a, 2) * side + lax.rem(my_y + b, side)

    def y_sender(r):
        a, b = STEPS[r - 1]
        return lax.rem(my_z + 2 - a, 2) * side + lax.rem(my_y + side - b, side)

    def z_target(r):
        return lax.rem(gz + r, nz)

    def z_sender(r):
        return lax.rem(gz + nz - r, nz)

    my_half, my_place = lax.div(gz, half), lax.rem(gz, half)

    def near(r):
        return my_half * half + lax.rem(my_place + r, half)

    between = lax.rem(gy + side, ny)

    barrier = pltpu.get_barrier_semaphore()
    for r in range(1, ny):
        pl.semaphore_signal(barrier, inc=1, device_id=(gz, y_target(r)), device_id_type=MESH)
    for device in [z_target(half)] + [near(r) for r in range(1, half)]:
        pl.semaphore_signal(barrier, inc=1, device_id=(device, gy), device_id_type=MESH)

    def load(mu, z, n):
        pltpu.make_async_copy(
            links.at[mu, :, :, :, pl.ds(z, 1)],
            link.at[mu, :, :, :, pl.ds(z, 1)],
            load_sem.at[n],
        ).start()

    def settle(ref, sem):
        pltpu.make_async_copy(ref, ref, sem).wait()

    def loaded(n, planes):
        settle(link.at[0, :, :, :, 0:planes], load_sem.at[n])

    small = [
        pltpu.make_async_copy(src, dst, small_sem.at[n])
        for n, (src, dst) in enumerate(
            ((mat_x_in, mat_x), (mat_y_in, mat_y), (decay_in, decay), (factor_in, factor))
        )
    ]
    for z in range(BZ):
        load(1, z, NQ)
    small[0].start()
    load(2, BZ - 1, NQ + 1)
    load(2, NQ - 1, NQ + 1)
    for q in range(NQ - 1, -1, -1):
        if q > 0:
            load(2, q + NQ - 1, q)
            load(2, q - 1, q)
        load(0, q + NQ, q)
        load(0, q, q)
    for copy in small[1:]:
        copy.start()

    def remote(src, dst, send, recv, device):
        return pltpu.make_async_remote_copy(
            src_ref=src,
            dst_ref=dst,
            send_sem=send,
            recv_sem=recv,
            device_id=device,
            device_id_type=MESH,
        )

    def rows(block):
        return pl.ds(pl.multiple_of(block * BY, BY), BY)

    def tile(block):
        return pl.ds(pl.multiple_of(block * BZ, BZ), BZ)

    def copy_a(n, r, sender):
        h, lo, hi = FORTH[n]
        return remote(
            send_a.at[h, y_target(r), lo:hi],
            recv_a.at[h, lo:hi, rows(sender)],
            a_send.at[0],
            a_recv.at[n],
            (gz, y_target(r)),
        )

    def own_a(n):
        h, lo, hi = FORTH[n]
        return pltpu.make_async_copy(
            send_a.at[h, gy, lo:hi], recv_a.at[h, lo:hi, rows(gy)], a_recv.at[n]
        )

    def start_a(n):
        for r in range(1, ny):
            copy_a(n, r, gy).start()
        own_a(n).start()

    def copy_edge_a(r, sender):
        return remote(
            edge_y.at[tile(y_target(r))],
            edge_r.at[tile(sender)],
            e_send.at[0],
            e_recv.at[0],
            (gz, y_target(r)),
        )

    def copy_b(h, r, sender):
        return remote(
            send_b.at[h, z_target(r)],
            recv_b.at[h, sender],
            b_send.at[0],
            b_recv.at[h],
            (z_target(r), between),
        )

    def copy_e(r, sender):
        return remote(
            send_e.at[0],
            recv_e.at[sender],
            b_send.at[1],
            b_recv.at[2],
            (z_target(r), gy),
        )

    def copy_c(h, r, sender):
        return remote(
            send_c.at[h, z_target(r)],
            recv_c.at[h, sender],
            c_send.at[0],
            c_recv.at[h],
            (z_target(r), between),
        )

    def copy_d(n, r, owner):
        h, lo, hi = BACK[n]
        return remote(
            send_d.at[h, lo:hi, rows(y_target(r))],
            main.at[h, owner, lo:hi],
            d_send.at[0],
            d_recv.at[n],
            (gz, y_target(r)),
        )

    def own_d(n):
        h, lo, hi = BACK[n]
        return pltpu.make_async_copy(
            send_d.at[h, lo:hi, rows(gy)], main.at[h, gy, lo:hi], d_recv.at[n]
        )

    def start_d(n):
        for r in range(1, ny):
            copy_d(n, r, gy).start()
        own_d(n).start()

    def copy_edge_d(r, owner):
        return remote(
            edge_d.at[tile(y_target(r))],
            edge_g.at[tile(owner)],
            e_send.at[1],
            e_recv.at[1],
            (gz, y_target(r)),
        )

    def copy_face(r, sender):
        return remote(
            face_s.at[y_target(r)],
            face_r.at[rows(sender)],
            z_send.at[0],
            z_recv.at[0],
            (gz, y_target(r)),
        )

    copy_down = remote(smooth.at[0], above_z, z_send.at[1], z_recv.at[1], (z_target(nz - 1), gy))
    own_edge_a = pltpu.make_async_copy(edge_y.at[tile(gy)], edge_r.at[tile(gy)], e_recv.at[0])
    own_edge_d = pltpu.make_async_copy(edge_d.at[tile(gy)], edge_g.at[tile(gy)], e_recv.at[1])

    first_row = lax.broadcasted_iota(jnp.int32, (BY, L), 0) == 0
    left = lax.broadcasted_iota(jnp.int32, (L, L), 1) < HALF
    straight = (lax.broadcasted_iota(jnp.int32, (NC, BZ, L), 2) < HALF) == (
        lax.broadcasted_iota(jnp.int32, (NC, BZ, L), 1) < NQ
    )

    def swap(x):
        return pltpu.roll(x, HALF, 1)

    def pair(x, y):
        return jnp.where(left, x, swap(y)), jnp.where(left, swap(x), y)

    def pair_edge(x):
        other = pltpu.roll(swap(x).reshape(NC, BZ, L), NQ, 1)
        return jnp.where(straight, x.reshape(NC, BZ, L), other).reshape(NC * BZ, L)

    def parts(mu, z):
        return algebra(
            lambda i, j: link[mu, 0, i, j, z], lambda i, j: link[mu, 1, i, j, z]
        )

    def part_y(z, carry):
        along = parts(1, z)
        for c in range(NC):
            behind = jnp.where(first_row, 0.0, pltpu.roll(along[c], 1, 0))
            base[c, z] = behind - along[c]
            edge_y[pl.ds(c * BZ + z, 1), :] = along[c][BY - 1 : BY]
        return carry

    loaded(NQ, BZ)
    lax.fori_loop(0, BZ, part_y, 0)
    loaded(NQ + 1, 2)
    top = parts(2, BZ - 1)
    small[0].wait()
    face_s[...] = transform_x([jnp.concatenate(top, axis=0)], mat_x[...])[0].reshape(NC, BY, L)
    pl.semaphore_wait(barrier, ny + half - 1)
    for r in range(1, ny):
        copy_face(r, gy).start()
    pltpu.make_async_copy(face_s.at[gy], face_r.at[rows(gy)], z_recv.at[0]).start()
    for r in range(1, half):
        pl.semaphore_signal(ring.at[0], inc=1, device_id=(near(r), gy), device_id_type=MESH)

    def divergence(z, under, here):
        along = parts(0, z)
        return jnp.concatenate(
            [
                base[c, z] + (pltpu.roll(along[c], 1, 1) - along[c]) + (-here[c] if under is None else under[c] - here[c])
                for c in range(NC)
            ],
            axis=0,
        )

    def spread(q, low, high):
        low, high = transform_x([low, high], mat_x[...])
        low, high = pair(low, high)
        send_a[0, :, q] = low.reshape(NC, BY, L)
        send_a[1, :, q] = high.reshape(NC, BY, L)

    def step(t, carry):
        here_low, here_high = carry
        q = NQ - 1 - t
        loaded(q, 4)
        under_low = parts(2, q - 1)
        under_high = parts(2, q + NQ - 1)
        spread(
            q, divergence(q, under_low, here_low), divergence(q + NQ, under_high, here_high)
        )
        return under_low, under_high

    carry = (parts(2, NQ - 1), top)
    carry = step(0, carry)
    carry = step(1, carry)
    start_a(0)
    edge_y[...] = pair_edge(transform_x([edge_y[...]], mat_x[...])[0])
    for r in range(1, ny):
        copy_edge_a(r, gy).start()
    own_edge_a.start()
    carry = step(2, carry)
    start_a(1)
    loaded(0, 2)
    high = divergence(NQ, parts(2, NQ - 1), carry[1])
    spread(0, divergence(0, None, carry[0]), high)
    start_a(2)
    start_a(3)
    start_a(4)
    if half > 1:
        pl.semaphore_wait(ring.at[0], half - 1)
    pl.semaphore_signal(
        ring.at[1], inc=1, device_id=(z_target(half), gy), device_id_type=MESH
    )

    for copy in small[1:]:
        copy.wait()
    settle(edge_r, e_recv.at[0])

    def receive(n):
        h, lo, hi = FORTH[n]
        settle(recv_a.at[h, lo:hi], a_recv.at[n])
        for q in range(lo, hi):
            edge = pltpu.roll(edge_r[pl.ds(h * NQ + q, ny, stride=BZ), :], 1, 0)
            recv_a[h, q, pl.ds(0, ny, stride=BY), :] += edge
        data = transform_y([recv_a[h, q] for q in range(lo, hi)], mat_y[...])
        for q in range(lo, hi):
            field[h, q] = data[q - lo]

    def power4(x):
        x = x * x
        return x * x

    def moments(h):
        rate = decay[h]
        rate4 = power4(rate)
        up = field[h, 0]
        down = field[h, NQ - 1]
        for q in range(1, NQ):
            up = field[h, q] + rate * up
            down = field[h, NQ - 1 - q] + rate * down
        up = rate * up
        swapped = jnp.where(left, swap(down), swap(up))
        keep[h] = swapped
        beyond = face[h]
        packed = jnp.where(left, down + rate4 * rate4 * beyond, up + beyond)
        send_b[h] = (packed + rate4 * swapped).reshape(nz, lines, L)
        for r in range(nz):
            copy_b(h, r, gz).start()

    narrow = lax.broadcasted_iota(jnp.int32, (lines, L), 1) < HALF

    def solve(h):
        rate8 = decay[h, pl.ds(pl.multiple_of(gz * lines, lines), lines), :]
        rate8 = power4(rate8 * rate8)
        whole = rate8
        for _ in range(int(math.log2(nz))):
            whole = whole * whole
        images = 1.0 / (1.0 - whole)
        settle(recv_b.at[h], b_recv.at[h])
        mixed = [
            jnp.where(narrow, recv_b[h, nz - 1 - j], recv_b[h, j]) for j in range(nz)
        ]
        state = mixed[0]
        for j in range(1, nz):
            state = mixed[j] + rate8 * state
        state = state * images
        result = []
        for j in range(nz):
            result.append(state)
            state = mixed[j] + rate8 * state
        for j in range(nz):
            send_c[h, j] = jnp.where(narrow, result[nz - 1 - j], result[j])
        for r in range(nz):
            copy_c(h, r, gz).start()

    receive(0)
    receive(1)
    settle(face_r, z_recv.at[0])
    beyond = transform_y([face_r[...]], mat_y[...])[0]
    face[0], face[1] = pair(beyond, beyond)
    receive(2)
    pl.semaphore_wait(ring.at[1], 1)
    moments(0)
    lane = lax.broadcasted_iota(jnp.int32, (1, L), 1)
    packed = jnp.zeros((1, L), F32)
    for q in range(NQ):
        row = field[0, q, 0:1, :]
        packed = jnp.where(lane == q, jnp.sum(jnp.where(lane == 0, row, 0.0)), packed)
        packed = jnp.where(lane == q + NQ, jnp.sum(jnp.where(lane == HALF, row, 0.0)), packed)
    row = face[0, 0:1, :]
    packed = jnp.where(lane == BZ, jnp.sum(jnp.where(lane == 0, row, 0.0)), packed)
    send_e[0] = packed
    for r in range(1, nz):
        copy_e(r, gz).start()
    recv_e[gz] = packed
    receive(3)
    receive(4)
    moments(1)
    solve(0)

    settle(recv_e.at[0 : nz - 1], b_recv.at[2])
    sources = recv_e[:, 0, :]
    block = lax.broadcasted_iota(jnp.int32, (nz, L), 0)
    plane = lax.broadcasted_iota(jnp.int32, (nz, L), 1)
    constant = (1.0 + extent * extent - 1.0) / extent
    zero_line = []
    for i in range(BZ):
        gap = BZ * (gz - block) + i - plane
        gap = jnp.where(gap < 0, gap + extent, gap).astype(F32)
        weight = constant - (6.0 / extent) * gap * (extent - gap)
        weight = jnp.where(plane <= BZ, weight * (ALPHA_HALF / (L * L)), 0.0)
        zero_line.append(jnp.sum(weight * sources))
    solve(1)

    tile_row = lax.broadcasted_iota(jnp.int32, (8, L), 0)
    tile_lane = lax.broadcasted_iota(jnp.int32, (8, L), 1)

    def evaluate(h):
        rate = decay[h]
        scale = factor[h]
        settle(recv_c.at[h], c_recv.at[h])
        outside = recv_c[h].reshape(L, L) + jnp.where(left, face[h], 0.0)
        inside = power4(rate) * outside + keep[h]
        outside = swap(outside)
        down = rate * jnp.where(left, inside, outside)
        for q in range(NQ - 1, -1, -1):
            recv_a[h, q] = down
            if q > 0:
                down = rate * (down + field[h, q])
        up = jnp.where(left, outside, inside)
        for q in range(NQ):
            up = field[h, q] + (rate * up if q > 0 else up)
            recv_a[h, q] = scale * (up + recv_a[h, q])
            if h == 0:
                low = jnp.where((tile_row == 0) & (tile_lane == 0), zero_line[q], 0.0)
                high = jnp.where(
                    (tile_row == 0) & (tile_lane == HALF), zero_line[q + NQ], 0.0
                )
                recv_a[h, q, 0:8, :] += low + high

    def inverse(h, lo, hi):
        data = transform_y([recv_a[h, q] for q in range(lo, hi)], mat_y[...])
        for q in range(lo, hi):
            send_d[h, q] = data[q - lo]
            edge = send_d[h, q, pl.ds(0, ny, stride=BY), :]
            edge_d[pl.ds(h * NQ + q, ny, stride=BZ), :] = pltpu.roll(edge, ny - 1, 0)

    evaluate(0)
    inverse(0, 0, 2)
    start_d(0)
    inverse(0, 2, 4)
    start_d(1)
    evaluate(1)
    inverse(1, 0, 2)
    start_d(2)
    start_d(3)
    inverse(1, 2, 4)
    for r in range(1, ny):
        copy_edge_d(r, gy).start()
    own_edge_d.start()
    for n in range(4, len(BACK)):
        start_d(n)

    settle(send_a.at[:, 0 : ny - 1], a_send.at[0])
    settle(edge_y.at[0 : (ny - 1) * BZ], e_send.at[0])
    settle(send_b, b_send.at[0])
    settle(send_c, c_send.at[0])
    settle(recv_e.at[0 : nz - 1], b_send.at[1])
    settle(face_s.at[0 : ny - 1], z_send.at[0])

    def fill(plane, value):
        for s in range(0, BY, 8):
            g = exponent([value(c, s) for c in range(NC)])
            for k in range(18):
                turn[plane, k, s : s + 8] = g[k]

    def rotate(z, directions):
        rotate_plane(link, turn, out, z, directions)

    def arrive(n):
        h, lo, hi = BACK[n]
        settle(main.at[h, :, lo:hi], d_recv.at[n])

    def collect(lo, hi):
        planes = []
        for q in range(lo, hi):
            planes += pair(main[0, :, q].reshape(L, L), main[1, :, q].reshape(L, L))
        data = transform_x(planes, mat_x[...])
        for q in range(lo, hi):
            smooth[q] = data[2 * (q - lo)].reshape(NC, BY, L)
            smooth[q + NQ] = data[2 * (q - lo) + 1].reshape(NC, BY, L)

    def fill_plane(z):
        fill(z, lambda c, s: smooth[z, c, s : s + 8])

    def add_edge(z):
        for k in range(18):
            turn[z, k, BY : BY + 1] = turn_edge[k, pl.ds(z, 1)]

    def along_z(t, first):
        rotate(first + t * NQ, (2,))
        return first

    def around(q):
        for z in (q, q + NQ):
            add_edge(z)
            rotate(z, (0, 1))

    def fill_pair(q):
        for z in (q, q + NQ):
            fill_plane(z)

    arrive(0)
    arrive(2)
    collect(0, 1)
    copy_down.start()
    fill_pair(0)
    arrive(3)
    collect(1, 2)
    settle(edge_g, e_recv.at[1])
    edge_g[...] = transform_x([pair_edge(edge_g[...])], mat_x[...])[0]
    g = exponent([edge_g[c * BZ : (c + 1) * BZ] for c in range(NC)])
    for k in range(18):
        turn_edge[k] = g[k]
    fill_pair(1)
    around(0)
    around(1)
    lax.fori_loop(0, 2, along_z, 0)
    arrive(1)
    arrive(4)
    collect(2, 3)
    fill_pair(2)
    around(2)
    lax.fori_loop(0, 2, along_z, 1)
    arrive(5)
    arrive(6)
    collect(3, 4)
    fill_pair(3)
    for z in (3, 3 + NQ):
        add_edge(z)
    copy_down.wait_recv()
    fill(BZ, lambda c, s: above_z[c, s : s + 8])

    settle(send_d.at[:, :, 0 : (ny - 1) * BY], d_send.at[0])
    settle(edge_d.at[0 : (ny - 1) * BZ], e_send.at[1])
    copy_down.wait_send()


def rotate_plane(link, turn, out, z, directions):
    for s in range(0, BY, 8):
        g = [turn[z, k, s : s + 8] for k in range(18)]
        for mu in directions:
            if mu == 0:
                ahead = [pltpu.roll(x, L - 1, 1) for x in g]
            elif mu == 1:
                ahead = [turn[z, k, s + 1 : s + 9] for k in range(18)]
            else:
                ahead = [turn[z + 1, k, s : s + 8] for k in range(18)]
            rotate_link(link, out, mu, z, s, g, ahead)


def rotate_link(link, out, mu, z, s, g, ahead):
    u = [link[mu, p, i, j, z, s : s + 8] for p in range(2) for i in range(3) for j in range(3)]
    for i in range(3):
        left = []
        for k in range(3):
            re = im = None
            for j in range(3):
                ar, ai = g[3 * i + j], g[9 + 3 * i + j]
                br, bi = u[3 * j + k], u[9 + 3 * j + k]
                tr = ar * br - ai * bi
                ti = ar * bi + ai * br
                re = tr if re is None else re + tr
                im = ti if im is None else im + ti
            left.append((re, im))
        for l in range(3):
            re = im = None
            for k in range(3):
                ar, ai = left[k]
                br, bi = ahead[3 * l + k], ahead[9 + 3 * l + k]
                tr = ar * br + ai * bi
                ti = ai * br - ar * bi
                re = tr if re is None else re + tr
                im = ti if im is None else im + ti
            out[mu, 0, i, l, z, s : s + 8] = re
            out[mu, 1, i, l, z, s : s + 8] = im


def fix(links, nz, ny):
    mat_x, mat_y, decay, factor = tables()
    lines = L // nz
    vmem = pltpu.VMEM
    dma = pltpu.SemaphoreType.DMA
    return pl.pallas_call(
        functools.partial(fix_kernel, nz, ny),
        out_shape=(
            pltpu.VMEM(links.shape, F32),
            pltpu.VMEM(links.shape, F32),
            pltpu.VMEM((BZ + 1, 18, BY + 8, L), F32),
        ),
        in_specs=[pl.BlockSpec(memory_space=pltpu.HBM)] * 5,
        out_specs=(pl.BlockSpec(memory_space=pltpu.VMEM),) * 3,
        scratch_shapes=[
            vmem((NC, BZ, BY, L), F32),
            vmem((2, NC, NQ, BY, L), F32),
            vmem((NC * BZ, L), F32),
            vmem((2, NQ, L, L), F32),
            vmem((ny * BZ, L), F32),
            vmem((NC, BY, L), F32),
            vmem((L, L), F32),
            vmem((2, L, L), F32),
            vmem((2, NQ, L, L), F32),
            vmem((2, L, L), F32),
            vmem((2, nz, lines, L), F32),
            vmem((2, nz, lines, L), F32),
            vmem((1, 1, L), F32),
            vmem((nz, 1, L), F32),
            vmem((2, nz, lines, L), F32),
            vmem((2, nz, lines, L), F32),
            vmem((2, NQ, L, L), F32),
            vmem((ny * BZ, L), F32),
            vmem((2, NC, NQ, BY, L), F32),
            vmem((BZ, NC, BY, L), F32),
            vmem((NC, BY, L), F32),
            vmem((NC * BZ, L), F32),
            vmem((2 * L, 2 * L), BF16),
            vmem((2 * L, 2 * L), BF16),
            vmem((2, L, L), F32),
            vmem((2, L, L), F32),
            vmem((18, BZ, L), F32),
            dma((NQ + 2,)),
            dma((4,)),
            dma((1,)),
            dma((len(FORTH),)),
            dma((2,)),
            dma((3,)),
            dma((1,)),
            dma((2,)),
            dma((1,)),
            dma((len(BACK),)),
            dma((2,)),
            dma((2,)),
            dma((2,)),
            dma((2,)),
            pltpu.SemaphoreType.REGULAR((2,)),
        ],
        compiler_params=pltpu.CompilerParams(
            collective_id=0, has_side_effects=True, vmem_limit_bytes=32 << 20
        ),
        name="fix",
    )(*(pltpu.with_memory_space_constraint(jnp.asarray(x), pltpu.HBM)
        for x in (links, mat_x, mat_y, decay, factor)))


def exponent(h):
    h2 = -(h[0] + h[1])
    diag = (h[0], h[1], h2)
    re01, im01 = h[3], -h[2]
    re02, im02 = h[5], -h[4]
    re12, im12 = h[7], -h[6]
    n01 = re01 * re01 + im01 * im01
    n02 = re02 * re02 + im02 * im02
    n12 = re12 * re12 + im12 * im12
    s0 = h[0] * h[0] + n01 + n02
    s1 = h[1] * h[1] + n01 + n12
    s2 = h2 * h2 + n02 + n12
    s01re = re02 * re12 + im02 * im12 - h2 * re01
    s01im = im02 * re12 - re02 * im12 - h2 * im01
    s02re = re01 * re12 - im01 * im12 - h[1] * re02
    s02im = re01 * im12 + im01 * re12 - h[1] * im02
    s12re = re01 * re02 + im01 * im02 - h[0] * re12
    s12im = re01 * im02 - im01 * re02 - h[0] * im12
    p = 0.5 * (s0 + s1 + s2)
    cross = (re01 * re12 - im01 * im12) * re02 + (re01 * im12 + im01 * re12) * im02
    d = h[0] * h[1] * h2 + 2.0 * cross - h[0] * n12 - h[1] * n02 - h2 * n01
    pp = p * p
    dd = d * d
    dp = d * p
    cubes = dd + p * pp
    a0 = 1.0 + dd * (p * (2.0 / 40320.0) - 1.0 / 720.0)
    b0 = d * (-1.0 / 6.0 + p * (1.0 / 120.0) - pp * (1.0 / 5040.0))
    a1 = d * (1.0 / 24.0 - p * (2.0 / 720.0) + pp * (3.0 / 40320.0))
    b1 = 1.0 - p * (1.0 / 6.0) + pp * (1.0 / 120.0) - cubes * (1.0 / 5040.0)
    a2 = -0.5 + p * (1.0 / 24.0) - pp * (1.0 / 720.0) + cubes * (1.0 / 40320.0)
    b2 = d * (1.0 / 120.0) - dp * (2.0 / 5040.0)
    re = {}
    im = {}
    for j, s in enumerate((s0, s1, s2)):
        re[j, j] = a0 + a1 * diag[j] + a2 * s
        im[j, j] = b0 + b1 * diag[j] + b2 * s
    for i, j, hr, hi, sr, si in (
        (0, 1, re01, im01, s01re, s01im),
        (0, 2, re02, im02, s02re, s02im),
        (1, 2, re12, im12, s12re, s12im),
    ):
        rr = a1 * hr + a2 * sr
        ii = b1 * hi + b2 * si
        ri = a1 * hi + a2 * si
        ir = b1 * hr + b2 * sr
        re[i, j] = rr - ii
        im[i, j] = ri + ir
        re[j, i] = rr + ii
        im[j, i] = ir - ri
    return [re[i, j] for i in range(3) for j in range(3)] + [
        im[i, j] for i in range(3) for j in range(3)
    ]


def store_kernel(source, link, turn, out, last, sem):
    def put(src, lo, hi, mus):
        for mu in mus:
            pltpu.make_async_copy(
                src.at[mu, :, :, :, lo:hi], out.at[mu, :, :, :, lo:hi], sem.at[0]
            ).start()

    put(source, 0, 2, (0, 1, 2))
    put(source, NQ, NQ + 2, (0, 1, 2))
    put(source, 2, 3, (0, 1))
    put(source, NQ + 2, NQ + 3, (0, 1))
    for z in (2, NQ + 2):
        rotate_plane(link, turn, last, z, (2,))
        put(last, z, z + 1, (2,))
    for z in (3, NQ + 3):
        rotate_plane(link, turn, last, z, (0, 1, 2))
        put(last, z, z + 1, (0, 1, 2))
    pltpu.make_async_copy(source, out, sem.at[0]).wait()


def store(source, link, turn):
    return pl.pallas_call(
        store_kernel,
        out_shape=jax.ShapeDtypeStruct(source.shape, F32),
        in_specs=[pl.BlockSpec(memory_space=pltpu.VMEM)] * 3,
        out_specs=pl.BlockSpec(memory_space=pl.ANY),
        scratch_shapes=[
            pltpu.VMEM((3, 2, 3, 3, BZ, BY, L), F32),
            pltpu.SemaphoreType.DMA((1,)),
        ],
        compiler_params=pltpu.CompilerParams(vmem_limit_bytes=16 << 20),
        name="store",
    )(source, link, turn)


def solution(mesh):
    nz, ny = mesh.shape["gz"], mesh.shape["gy"]

    def body(links):
        return store(*fix(links, nz, ny))

    spec = P(None, None, None, None, "gz", "gy", None)
    return jax.shard_map(body, mesh=mesh, in_specs=(spec,), out_specs=spec, check_vma=False)
```

```python
import functools
import math

import jax
import jax.numpy as jnp
import numpy as np
from jax import lax
from jax.experimental import pallas as pl
from jax.experimental.pallas import tpu as pltpu
from jax.sharding import PartitionSpec as P

L = 128
ALPHA_HALF = 0.04
BZ = 8
BY = 16
NC = 8
MESH = pl.DeviceIdType.MESH
F32 = jnp.float32
BF16 = jnp.bfloat16
HALF = L // 2
NQ = BZ // 2
FORTH = ((0, 2, 4), (0, 1, 2), (0, 0, 1), (1, 2, 4), (1, 0, 2))
BACK = ((0, 0, 2), (0, 2, 3), (1, 0, 1), (1, 1, 2), (1, 2, 3), (0, 3, 4), (1, 3, 4))
STEPS = ((1, 2), (0, 2), (1, 1), (1, 3), (0, 1), (0, 3), (1, 0))


def tables():
    k = np.arange(L)
    angle = 2.0 * np.pi / L * (np.outer(k, k) % L)
    hartley = np.cos(angle) + np.sin(angle)
    high = hartley.astype(np.float32).astype(jnp.bfloat16)
    low = (hartley - high.astype(np.float64)).astype(np.float32).astype(jnp.bfloat16)
    half = np.concatenate([high, low], axis=1)
    mat_x = np.concatenate([half, half], axis=0)
    mat_y = np.ascontiguousarray(mat_x.T)
    momentum = 4.0 * np.sin(np.pi * k / L) ** 2
    mass = momentum[:, None] + momentum[None, :]
    mass[0, 0] = 1.0
    root = np.sqrt(mass * mass / 4.0 + mass)
    decay = 1.0 / (1.0 + mass / 2.0 + root)
    factor = 12.0 * ALPHA_HALF / (L * L) / (2.0 * root)
    decay[0, 0] = 0.0
    factor[0, 0] = 0.0
    paired = [
        np.stack([np.tile(t[:, h * HALF : (h + 1) * HALF], (1, 2)) for h in range(2)])
        for t in (decay, factor)
    ]
    return mat_x, mat_y, paired[0].astype(np.float32), paired[1].astype(np.float32)


def split(x):
    high = x.astype(BF16)
    low = (x - high.astype(F32)).astype(BF16)
    return high, low


def transform_x(planes, mat_x):
    high, low = split(jnp.concatenate(planes, axis=0))
    out = jnp.dot(jnp.concatenate([high, low], axis=1), mat_x, preferred_element_type=F32)
    out = out[:, :L] + out[:, L:]
    return [out[i * L : (i + 1) * L] for i in range(len(planes))]


def transform_y(planes, mat_y):
    high, low = split(jnp.concatenate(planes, axis=1))
    out = jnp.dot(mat_y, jnp.concatenate([high, low], axis=0), preferred_element_type=F32)
    out = out[:L] + out[L:]
    return [out[:, i * L : (i + 1) * L] for i in range(len(planes))]


def algebra(re, im):
    trace_part = (im(0, 0) + im(1, 1) + im(2, 2)) * (1.0 / 3.0)
    return [
        im(0, 0) - trace_part,
        im(1, 1) - trace_part,
        (re(0, 1) - re(1, 0)) * 0.5,
        (im(0, 1) + im(1, 0)) * 0.5,
        (re(0, 2) - re(2, 0)) * 0.5,
        (im(0, 2) + im(2, 0)) * 0.5,
        (re(1, 2) - re(2, 1)) * 0.5,
        (im(1, 2) + im(2, 1)) * 0.5,
    ]


def fix_kernel(
    nz,
    ny,
    links,
    mat_x_in,
    mat_y_in,
    decay_in,
    factor_in,
    out,
    link,
    turn,
    base,
    send_a,
    edge_y,
    recv_a,
    edge_r,
    face_s,
    face_r,
    face,
    field,
    keep,
    send_b,
    recv_b,
    send_e,
    recv_e,
    send_c,
    recv_c,
    send_d,
    edge_d,
    main,
    smooth,
    above_z,
    edge_g,
    ninth,
    send_n,
    above_k,
    mat_x,
    mat_y,
    decay,
    factor,
    turn_edge,
    load_sem,
    small_sem,
    a_send,
    a_recv,
    b_send,
    b_recv,
    c_send,
    c_recv,
    d_send,
    d_recv,
    e_send,
    e_recv,
    z_send,
    z_recv,
    n_sem,
    ring,
):
    gz = lax.axis_index("gz")
    gy = lax.axis_index("gy")
    lines = L // nz
    extent = nz * BZ

    side = ny // 2
    half = nz // 2
    my_z, my_y = lax.div(gy, side), lax.rem(gy, side)

    def y_target(r):
        a, b = STEPS[r - 1]
        return lax.rem(my_z + a, 2) * side + lax.rem(my_y + b, side)

    def y_sender(r):
        a, b = STEPS[r - 1]
        return lax.rem(my_z + 2 - a, 2) * side + lax.rem(my_y + side - b, side)

    def z_target(r):
        return lax.rem(gz + r, nz)

    def z_sender(r):
        return lax.rem(gz + nz - r, nz)

    my_half, my_place = lax.div(gz, half), lax.rem(gz, half)

    def near(r):
        return my_half * half + lax.rem(my_place + r, half)

    between = lax.rem(gy + side, ny)

    barrier = pltpu.get_barrier_semaphore()
    for r in range(1, ny):
        pl.semaphore_signal(barrier, inc=1, device_id=(gz, y_target(r)), device_id_type=MESH)
    for device in [z_target(half)] + [near(r) for r in range(1, half)]:
        pl.semaphore_signal(barrier, inc=1, device_id=(device, gy), device_id_type=MESH)

    def load(mu, z, n):
        pltpu.make_async_copy(
            links.at[mu, :, :, :, pl.ds(z, 1)],
            link.at[mu, :, :, :, pl.ds(z, 1)],
            load_sem.at[n],
        ).start()

    def settle(ref, sem):
        pltpu.make_async_copy(ref, ref, sem).wait()

    def loaded(n, planes):
        settle(link.at[0, :, :, :, 0:planes], load_sem.at[n])

    small = [
        pltpu.make_async_copy(src, dst, small_sem.at[n])
        for n, (src, dst) in enumerate(
            ((mat_x_in, mat_x), (mat_y_in, mat_y), (decay_in, decay), (factor_in, factor))
        )
    ]
    for z in range(BZ):
        load(1, z, NQ)
    small[0].start()
    load(2, BZ - 1, NQ + 1)
    load(2, NQ - 1, NQ + 1)
    for q in range(NQ - 1, -1, -1):
        if q > 0:
            load(2, q + NQ - 1, q)
            load(2, q - 1, q)
        load(0, q + NQ, q)
        load(0, q, q)
    for copy in small[1:]:
        copy.start()

    def remote(src, dst, send, recv, device):
        return pltpu.make_async_remote_copy(
            src_ref=src,
            dst_ref=dst,
            send_sem=send,
            recv_sem=recv,
            device_id=device,
            device_id_type=MESH,
        )

    def rows(block):
        return pl.ds(pl.multiple_of(block * BY, BY), BY)

    def tile(block):
        return pl.ds(pl.multiple_of(block * BZ, BZ), BZ)

    def copy_a(n, r, sender):
        h, lo, hi = FORTH[n]
        return remote(
            send_a.at[h, y_target(r), lo:hi],
            recv_a.at[h, lo:hi, rows(sender)],
            a_send.at[0],
            a_recv.at[n],
            (gz, y_target(r)),
        )

    def own_a(n):
        h, lo, hi = FORTH[n]
        return pltpu.make_async_copy(
            send_a.at[h, gy, lo:hi], recv_a.at[h, lo:hi, rows(gy)], a_recv.at[n]
        )

    def start_a(n):
        for r in range(1, ny):
            copy_a(n, r, gy).start()
        own_a(n).start()

    def copy_edge_a(r, sender):
        return remote(
            edge_y.at[tile(y_target(r))],
            edge_r.at[tile(sender)],
            e_send.at[0],
            e_recv.at[0],
            (gz, y_target(r)),
        )

    def copy_b(h, r, sender):
        return remote(
            send_b.at[h, z_target(r)],
            recv_b.at[h, sender],
            b_send.at[0],
            b_recv.at[h],
            (z_target(r), between),
        )

    def copy_e(r, sender):
        return remote(
            send_e.at[0],
            recv_e.at[sender],
            b_send.at[1],
            b_recv.at[2],
            (z_target(r), gy),
        )

    def copy_c(h, r, sender):
        return remote(
            send_c.at[h, z_target(r)],
            recv_c.at[h, sender],
            c_send.at[0],
            c_recv.at[h],
            (z_target(r), between),
        )

    def copy_d(n, r, owner):
        h, lo, hi = BACK[n]
        return remote(
            send_d.at[h, lo:hi, rows(y_target(r))],
            main.at[h, owner, lo:hi],
            d_send.at[0],
            d_recv.at[n],
            (gz, y_target(r)),
        )

    def own_d(n):
        h, lo, hi = BACK[n]
        return pltpu.make_async_copy(
            send_d.at[h, lo:hi, rows(gy)], main.at[h, gy, lo:hi], d_recv.at[n]
        )

    def start_d(n):
        for r in range(1, ny):
            copy_d(n, r, gy).start()
        own_d(n).start()

    def copy_edge_d(r, owner):
        return remote(
            edge_d.at[tile(y_target(r))],
            edge_g.at[tile(owner)],
            e_send.at[1],
            e_recv.at[1],
            (gz, y_target(r)),
        )

    def copy_face(r, sender):
        return remote(
            face_s.at[y_target(r)],
            face_r.at[rows(sender)],
            z_send.at[0],
            z_recv.at[0],
            (gz, y_target(r)),
        )

    copy_down = remote(smooth.at[0], above_z, z_send.at[1], z_recv.at[1], (z_target(nz - 1), gy))
    own_edge_a = pltpu.make_async_copy(edge_y.at[tile(gy)], edge_r.at[tile(gy)], e_recv.at[0])
    own_edge_d = pltpu.make_async_copy(edge_d.at[tile(gy)], edge_g.at[tile(gy)], e_recv.at[1])

    first_row = lax.broadcasted_iota(jnp.int32, (BY, L), 0) == 0
    left = lax.broadcasted_iota(jnp.int32, (L, L), 1) < HALF
    straight = (lax.broadcasted_iota(jnp.int32, (NC, BZ, L), 2) < HALF) == (
        lax.broadcasted_iota(jnp.int32, (NC, BZ, L), 1) < NQ
    )

    def swap(x):
        return pltpu.roll(x, HALF, 1)

    def pair(x, y):
        return jnp.where(left, x, swap(y)), jnp.where(left, swap(x), y)

    def pair_edge(x):
        other = pltpu.roll(swap(x).reshape(NC, BZ, L), NQ, 1)
        return jnp.where(straight, x.reshape(NC, BZ, L), other).reshape(NC * BZ, L)

    def parts(mu, z):
        return algebra(
            lambda i, j: link[mu, 0, i, j, z], lambda i, j: link[mu, 1, i, j, z]
        )

    def part_y(z, carry):
        along = parts(1, z)
        for c in range(NC):
            behind = jnp.where(first_row, 0.0, pltpu.roll(along[c], 1, 0))
            base[c, z] = behind - along[c]
            edge_y[pl.ds(c * BZ + z, 1), :] = along[c][BY - 1 : BY]
        return carry

    loaded(NQ, BZ)
    lax.fori_loop(0, BZ, part_y, 0)
    loaded(NQ + 1, 2)
    top = parts(2, BZ - 1)
    small[0].wait()
    face_s[...] = transform_x([jnp.concatenate(top, axis=0)], mat_x[...])[0].reshape(NC, BY, L)
    pl.semaphore_wait(barrier, ny + half - 1)
    for r in range(1, ny):
        copy_face(r, gy).start()
    pltpu.make_async_copy(face_s.at[gy], face_r.at[rows(gy)], z_recv.at[0]).start()
    for r in range(1, half):
        pl.semaphore_signal(ring.at[0], inc=1, device_id=(near(r), gy), device_id_type=MESH)

    def divergence(z, under, here):
        along = parts(0, z)
        return jnp.concatenate(
            [
                base[c, z] + (pltpu.roll(along[c], 1, 1) - along[c]) + (-here[c] if under is None else under[c] - here[c])
                for c in range(NC)
            ],
            axis=0,
        )

    def spread(q, low, high):
        low, high = transform_x([low, high], mat_x[...])
        low, high = pair(low, high)
        send_a[0, :, q] = low.reshape(NC, BY, L)
        send_a[1, :, q] = high.reshape(NC, BY, L)

    def step(t, carry):
        here_low, here_high = carry
        q = NQ - 1 - t
        loaded(q, 4)
        under_low = parts(2, q - 1)
        under_high = parts(2, q + NQ - 1)
        spread(
            q, divergence(q, under_low, here_low), divergence(q + NQ, under_high, here_high)
        )
        return under_low, under_high

    carry = (parts(2, NQ - 1), top)
    carry = step(0, carry)
    carry = step(1, carry)
    start_a(0)
    edge_y[...] = pair_edge(transform_x([edge_y[...]], mat_x[...])[0])
    for r in range(1, ny):
        copy_edge_a(r, gy).start()
    own_edge_a.start()
    carry = step(2, carry)
    start_a(1)
    loaded(0, 2)
    high = divergence(NQ, parts(2, NQ - 1), carry[1])
    spread(0, divergence(0, None, carry[0]), high)
    start_a(2)
    start_a(3)
    start_a(4)
    if half > 1:
        pl.semaphore_wait(ring.at[0], half - 1)
    pl.semaphore_signal(
        ring.at[1], inc=1, device_id=(z_target(half), gy), device_id_type=MESH
    )

    for copy in small[1:]:
        copy.wait()
    settle(edge_r, e_recv.at[0])

    def receive(n):
        h, lo, hi = FORTH[n]
        settle(recv_a.at[h, lo:hi], a_recv.at[n])
        for q in range(lo, hi):
            edge = pltpu.roll(edge_r[pl.ds(h * NQ + q, ny, stride=BZ), :], 1, 0)
            recv_a[h, q, pl.ds(0, ny, stride=BY), :] += edge
        data = transform_y([recv_a[h, q] for q in range(lo, hi)], mat_y[...])
        for q in range(lo, hi):
            field[h, q] = data[q - lo]

    def power4(x):
        x = x * x
        return x * x

    def moments(h):
        rate = decay[h]
        rate4 = power4(rate)
        up = field[h, 0]
        down = field[h, NQ - 1]
        for q in range(1, NQ):
            up = field[h, q] + rate * up
            down = field[h, NQ - 1 - q] + rate * down
        up = rate * up
        swapped = jnp.where(left, swap(down), swap(up))
        keep[h] = swapped
        beyond = face[h]
        packed = jnp.where(left, down + rate4 * rate4 * beyond, up + beyond)
        send_b[h] = (packed + rate4 * swapped).reshape(nz, lines, L)
        for r in range(nz):
            copy_b(h, r, gz).start()

    narrow = lax.broadcasted_iota(jnp.int32, (lines, L), 1) < HALF

    def solve(h):
        rate8 = decay[h, pl.ds(pl.multiple_of(gz * lines, lines), lines), :]
        rate8 = power4(rate8 * rate8)
        whole = rate8
        for _ in range(int(math.log2(nz))):
            whole = whole * whole
        images = 1.0 / (1.0 - whole)
        settle(recv_b.at[h], b_recv.at[h])
        mixed = [
            jnp.where(narrow, recv_b[h, nz - 1 - j], recv_b[h, j]) for j in range(nz)
        ]
        state = mixed[0]
        for j in range(1, nz):
            state = mixed[j] + rate8 * state
        state = state * images
        result = []
        for j in range(nz):
            result.append(state)
            state = mixed[j] + rate8 * state
        for j in range(nz):
            send_c[h, j] = jnp.where(narrow, result[nz - 1 - j], result[j])
        for r in range(nz):
            copy_c(h, r, gz).start()

    receive(0)
    receive(1)
    settle(face_r, z_recv.at[0])
    beyond = transform_y([face_r[...]], mat_y[...])[0]
    face[0], face[1] = pair(beyond, beyond)
    receive(2)
    pl.semaphore_wait(ring.at[1], 1)
    moments(0)
    lane = lax.broadcasted_iota(jnp.int32, (1, L), 1)
    packed = jnp.zeros((1, L), F32)
    for q in range(NQ):
        row = field[0, q, 0:1, :]
        packed = jnp.where(lane == q, jnp.sum(jnp.where(lane == 0, row, 0.0)), packed)
        packed = jnp.where(lane == q + NQ, jnp.sum(jnp.where(lane == HALF, row, 0.0)), packed)
    row = face[0, 0:1, :]
    packed = jnp.where(lane == BZ, jnp.sum(jnp.where(lane == 0, row, 0.0)), packed)
    send_e[0] = packed
    for r in range(1, nz):
        copy_e(r, gz).start()
    recv_e[gz] = packed
    receive(3)
    receive(4)
    moments(1)
    solve(0)

    settle(recv_e.at[0 : nz - 1], b_recv.at[2])
    sources = recv_e[:, 0, :]
    block = lax.broadcasted_iota(jnp.int32, (nz, L), 0)
    plane = lax.broadcasted_iota(jnp.int32, (nz, L), 1)
    constant = (1.0 + extent * extent - 1.0) / extent
    zero_line = []
    for i in range(BZ + 1):
        gap = BZ * (gz - block) + i - plane
        gap = jnp.where(gap < 0, gap + extent, gap).astype(F32)
        weight = constant - (6.0 / extent) * gap * (extent - gap)
        weight = jnp.where(plane <= BZ, weight * (ALPHA_HALF / (L * L)), 0.0)
        zero_line.append(jnp.sum(weight * sources))
    solve(1)

    tile_row = lax.broadcasted_iota(jnp.int32, (8, L), 0)
    tile_lane = lax.broadcasted_iota(jnp.int32, (8, L), 1)

    def evaluate(h):
        rate = decay[h]
        scale = factor[h]
        settle(recv_c.at[h], c_recv.at[h])
        outside = recv_c[h].reshape(L, L) + jnp.where(left, face[h], 0.0)
        inside = power4(rate) * outside + keep[h]
        outside = swap(outside)
        down = rate * jnp.where(left, inside, outside)
        for q in range(NQ - 1, -1, -1):
            recv_a[h, q] = down
            if q > 0:
                down = rate * (down + field[h, q])
        up = jnp.where(left, outside, inside)
        for q in range(NQ):
            up = field[h, q] + (rate * up if q > 0 else up)
            recv_a[h, q] = scale * (up + recv_a[h, q])
            if h == 0:
                low = jnp.where((tile_row == 0) & (tile_lane == 0), zero_line[q], 0.0)
                high = jnp.where(
                    (tile_row == 0) & (tile_lane == HALF), zero_line[q + NQ], 0.0
                )
                recv_a[h, q, 0:8, :] += low + high
        ninth[h] = scale * (rate * up + outside)

    def inverse(h, lo, hi):
        data = transform_y([recv_a[h, q] for q in range(lo, hi)], mat_y[...])
        for q in range(lo, hi):
            send_d[h, q] = data[q - lo]
            edge = send_d[h, q, pl.ds(0, ny, stride=BY), :]
            edge_d[pl.ds(h * NQ + q, ny, stride=BZ), :] = pltpu.roll(edge, ny - 1, 0)

    evaluate(0)
    inverse(0, 0, 2)
    start_d(0)
    inverse(0, 2, 4)
    start_d(1)
    evaluate(1)
    inverse(1, 0, 2)
    start_d(2)
    start_d(3)
    inverse(1, 2, 4)
    for r in range(1, ny):
        copy_edge_d(r, gy).start()
    own_edge_d.start()
    for n in range(4, len(BACK)):
        start_d(n)

    def copy_ninth(r):
        return remote(
            send_n.at[rows(y_target(r))],
            above_k.at[gy],
            n_sem.at[0],
            n_sem.at[1],
            (gz, y_target(r)),
        )

    @pl.when(my_place == half - 1)
    def _():
        plane = jnp.where(left, swap(ninth[0]), ninth[1])
        origin = (lax.broadcasted_iota(jnp.int32, (L, L), 0) == 0) & (
            lax.broadcasted_iota(jnp.int32, (L, L), 1) == 0
        )
        plane = plane + jnp.where(origin, zero_line[BZ], 0.0)
        send_n[...] = transform_y([plane], mat_y[...])[0]
        for r in range(1, ny):
            copy_ninth(r).start()
        pltpu.make_async_copy(send_n.at[rows(gy)], above_k.at[gy], n_sem.at[1]).start()


    settle(send_a.at[:, 0 : ny - 1], a_send.at[0])
    settle(edge_y.at[0 : (ny - 1) * BZ], e_send.at[0])
    settle(send_b, b_send.at[0])
    settle(send_c, c_send.at[0])
    settle(recv_e.at[0 : nz - 1], b_send.at[1])
    settle(face_s.at[0 : ny - 1], z_send.at[0])

    def fill(plane, value):
        for s in range(0, BY, 8):
            g = exponent([value(c, s) for c in range(NC)])
            for k in range(18):
                turn[plane, k, s : s + 8] = g[k]

    def rotate(z, directions):
        rotate_plane(link, turn, out, z, directions)

    def arrive(n):
        h, lo, hi = BACK[n]
        settle(main.at[h, :, lo:hi], d_recv.at[n])

    def collect(lo, hi):
        planes = []
        for q in range(lo, hi):
            planes += pair(main[0, :, q].reshape(L, L), main[1, :, q].reshape(L, L))
        data = transform_x(planes, mat_x[...])
        for q in range(lo, hi):
            smooth[q] = data[2 * (q - lo)].reshape(NC, BY, L)
            smooth[q + NQ] = data[2 * (q - lo) + 1].reshape(NC, BY, L)

    def fill_plane(z):
        fill(z, lambda c, s: smooth[z, c, s : s + 8])

    def add_edge(z):
        for k in range(18):
            turn[z, k, BY : BY + 1] = turn_edge[k, pl.ds(z, 1)]

    def along_z(t, first):
        rotate(first + t * NQ, (2,))
        return first

    def around(q):
        for z in (q, q + NQ):
            add_edge(z)
            rotate(z, (0, 1))

    def fill_pair(q):
        for z in (q, q + NQ):
            fill_plane(z)

    arrive(0)
    arrive(2)
    collect(0, 1)
    @pl.when(my_place != 0)
    def _():
        copy_down.start()

    fill_pair(0)
    arrive(3)
    collect(1, 2)
    settle(edge_g, e_recv.at[1])
    edge_g[...] = transform_x([pair_edge(edge_g[...])], mat_x[...])[0]
    g = exponent([edge_g[c * BZ : (c + 1) * BZ] for c in range(NC)])
    for k in range(18):
        turn_edge[k] = g[k]
    fill_pair(1)
    around(0)
    around(1)
    lax.fori_loop(0, 2, along_z, 0)
    arrive(1)
    arrive(4)
    collect(2, 3)
    fill_pair(2)
    around(2)
    lax.fori_loop(0, 2, along_z, 1)
    arrive(5)
    arrive(6)
    collect(3, 4)
    fill_pair(3)
    for z in (3, 3 + NQ):
        add_edge(z)
    @pl.when(my_place != half - 1)
    def _():
        copy_down.wait_recv()

    @pl.when(my_place == half - 1)
    def _():
        settle(above_k, n_sem.at[1])
        plane = transform_x([above_k[...].reshape(L, L)], mat_x[...])[0]
        above_z[...] = plane.reshape(NC, BY, L)

    fill(BZ, lambda c, s: above_z[c, s : s + 8])

    settle(send_d.at[:, :, 0 : (ny - 1) * BY], d_send.at[0])
    settle(edge_d.at[0 : (ny - 1) * BZ], e_send.at[1])
    @pl.when(my_place != 0)
    def _():
        copy_down.wait_send()

    @pl.when(my_place == half - 1)
    def _():
        settle(send_n.at[0 : (ny - 1) * BY], n_sem.at[0])


def rotate_plane(link, turn, out, z, directions):
    for s in range(0, BY, 8):
        g = [turn[z, k, s : s + 8] for k in range(18)]
        for mu in directions:
            if mu == 0:
                ahead = [pltpu.roll(x, L - 1, 1) for x in g]
            elif mu == 1:
                ahead = [turn[z, k, s + 1 : s + 9] for k in range(18)]
            else:
                ahead = [turn[z + 1, k, s : s + 8] for k in range(18)]
            rotate_link(link, out, mu, z, s, g, ahead)


def rotate_link(link, out, mu, z, s, g, ahead):
    u = [link[mu, p, i, j, z, s : s + 8] for p in range(2) for i in range(3) for j in range(3)]
    for i in range(3):
        left = []
        for k in range(3):
            re = im = None
            for j in range(3):
                ar, ai = g[3 * i + j], g[9 + 3 * i + j]
                br, bi = u[3 * j + k], u[9 + 3 * j + k]
                tr = ar * br - ai * bi
                ti = ar * bi + ai * br
                re = tr if re is None else re + tr
                im = ti if im is None else im + ti
            left.append((re, im))
        for l in range(3):
            re = im = None
            for k in range(3):
                ar, ai = left[k]
                br, bi = ahead[3 * l + k], ahead[9 + 3 * l + k]
                tr = ar * br + ai * bi
                ti = ai * br - ar * bi
                re = tr if re is None else re + tr
                im = ti if im is None else im + ti
            out[mu, 0, i, l, z, s : s + 8] = re
            out[mu, 1, i, l, z, s : s + 8] = im


def fix(links, nz, ny):
    mat_x, mat_y, decay, factor = tables()
    lines = L // nz
    vmem = pltpu.VMEM
    dma = pltpu.SemaphoreType.DMA
    return pl.pallas_call(
        functools.partial(fix_kernel, nz, ny),
        out_shape=(
            pltpu.VMEM(links.shape, F32),
            pltpu.VMEM(links.shape, F32),
            pltpu.VMEM((BZ + 1, 18, BY + 8, L), F32),
        ),
        in_specs=[pl.BlockSpec(memory_space=pltpu.HBM)] * 5,
        out_specs=(pl.BlockSpec(memory_space=pltpu.VMEM),) * 3,
        scratch_shapes=[
            vmem((NC, BZ, BY, L), F32),
            vmem((2, NC, NQ, BY, L), F32),
            vmem((NC * BZ, L), F32),
            vmem((2, NQ, L, L), F32),
            vmem((ny * BZ, L), F32),
            vmem((NC, BY, L), F32),
            vmem((L, L), F32),
            vmem((2, L, L), F32),
            vmem((2, NQ, L, L), F32),
            vmem((2, L, L), F32),
            vmem((2, nz, lines, L), F32),
            vmem((2, nz, lines, L), F32),
            vmem((1, 1, L), F32),
            vmem((nz, 1, L), F32),
            vmem((2, nz, lines, L), F32),
            vmem((2, nz, lines, L), F32),
            vmem((2, NQ, L, L), F32),
            vmem((ny * BZ, L), F32),
            vmem((2, NC, NQ, BY, L), F32),
            vmem((BZ, NC, BY, L), F32),
            vmem((NC, BY, L), F32),
            vmem((NC * BZ, L), F32),
            vmem((2, L, L), F32),
            vmem((L, L), F32),
            vmem((NC, BY, L), F32),
            vmem((2 * L, 2 * L), BF16),
            vmem((2 * L, 2 * L), BF16),
            vmem((2, L, L), F32),
            vmem((2, L, L), F32),
            vmem((18, BZ, L), F32),
            dma((NQ + 2,)),
            dma((4,)),
            dma((1,)),
            dma((len(FORTH),)),
            dma((2,)),
            dma((3,)),
            dma((1,)),
            dma((2,)),
            dma((1,)),
            dma((len(BACK),)),
            dma((2,)),
            dma((2,)),
            dma((2,)),
            dma((2,)),
            dma((2,)),
            pltpu.SemaphoreType.REGULAR((2,)),
        ],
        compiler_params=pltpu.CompilerParams(
            collective_id=0, has_side_effects=True, vmem_limit_bytes=32 << 20
        ),
        name="fix",
    )(*(pltpu.with_memory_space_constraint(jnp.asarray(x), pltpu.HBM)
        for x in (links, mat_x, mat_y, decay, factor)))


def exponent(h):
    h2 = -(h[0] + h[1])
    diag = (h[0], h[1], h2)
    re01, im01 = h[3], -h[2]
    re02, im02 = h[5], -h[4]
    re12, im12 = h[7], -h[6]
    n01 = re01 * re01 + im01 * im01
    n02 = re02 * re02 + im02 * im02
    n12 = re12 * re12 + im12 * im12
    s0 = h[0] * h[0] + n01 + n02
    s1 = h[1] * h[1] + n01 + n12
    s2 = h2 * h2 + n02 + n12
    s01re = re02 * re12 + im02 * im12 - h2 * re01
    s01im = im02 * re12 - re02 * im12 - h2 * im01
    s02re = re01 * re12 - im01 * im12 - h[1] * re02
    s02im = re01 * im12 + im01 * re12 - h[1] * im02
    s12re = re01 * re02 + im01 * im02 - h[0] * re12
    s12im = re01 * im02 - im01 * re02 - h[0] * im12
    p = 0.5 * (s0 + s1 + s2)
    cross = (re01 * re12 - im01 * im12) * re02 + (re01 * im12 + im01 * re12) * im02
    d = h[0] * h[1] * h2 + 2.0 * cross - h[0] * n12 - h[1] * n02 - h2 * n01
    pp = p * p
    dd = d * d
    dp = d * p
    cubes = dd + p * pp
    a0 = 1.0 + dd * (p * (2.0 / 40320.0) - 1.0 / 720.0)
    b0 = d * (-1.0 / 6.0 + p * (1.0 / 120.0) - pp * (1.0 / 5040.0))
    a1 = d * (1.0 / 24.0 - p * (2.0 / 720.0) + pp * (3.0 / 40320.0))
    b1 = 1.0 - p * (1.0 / 6.0) + pp * (1.0 / 120.0) - cubes * (1.0 / 5040.0)
    a2 = -0.5 + p * (1.0 / 24.0) - pp * (1.0 / 720.0) + cubes * (1.0 / 40320.0)
    b2 = d * (1.0 / 120.0) - dp * (2.0 / 5040.0)
    re = {}
    im = {}
    for j, s in enumerate((s0, s1, s2)):
        re[j, j] = a0 + a1 * diag[j] + a2 * s
        im[j, j] = b0 + b1 * diag[j] + b2 * s
    for i, j, hr, hi, sr, si in (
        (0, 1, re01, im01, s01re, s01im),
        (0, 2, re02, im02, s02re, s02im),
        (1, 2, re12, im12, s12re, s12im),
    ):
        rr = a1 * hr + a2 * sr
        ii = b1 * hi + b2 * si
        ri = a1 * hi + a2 * si
        ir = b1 * hr + b2 * sr
        re[i, j] = rr - ii
        im[i, j] = ri + ir
        re[j, i] = rr + ii
        im[j, i] = ir - ri
    return [re[i, j] for i in range(3) for j in range(3)] + [
        im[i, j] for i in range(3) for j in range(3)
    ]


def store_kernel(source, link, turn, out, last, sem):
    def put(src, lo, hi, mus):
        for mu in mus:
            pltpu.make_async_copy(
                src.at[mu, :, :, :, lo:hi], out.at[mu, :, :, :, lo:hi], sem.at[0]
            ).start()

    put(source, 0, 2, (0, 1, 2))
    put(source, NQ, NQ + 2, (0, 1, 2))
    put(source, 2, 3, (0, 1))
    put(source, NQ + 2, NQ + 3, (0, 1))
    for z in (2, NQ + 2):
        rotate_plane(link, turn, last, z, (2,))
        put(last, z, z + 1, (2,))
    for z in (3, NQ + 3):
        rotate_plane(link, turn, last, z, (0, 1, 2))
        put(last, z, z + 1, (0, 1, 2))
    pltpu.make_async_copy(source, out, sem.at[0]).wait()


def store(source, link, turn):
    return pl.pallas_call(
        store_kernel,
        out_shape=jax.ShapeDtypeStruct(source.shape, F32),
        in_specs=[pl.BlockSpec(memory_space=pltpu.VMEM)] * 3,
        out_specs=pl.BlockSpec(memory_space=pl.ANY),
        scratch_shapes=[
            pltpu.VMEM((3, 2, 3, 3, BZ, BY, L), F32),
            pltpu.SemaphoreType.DMA((1,)),
        ],
        compiler_params=pltpu.CompilerParams(vmem_limit_bytes=16 << 20),
        name="store",
    )(source, link, turn)


def solution(mesh):
    nz, ny = mesh.shape["gz"], mesh.shape["gy"]

    def body(links):
        return store(*fix(links, nz, ny))

    spec = P(None, None, None, None, "gz", "gy", None)
    return jax.shard_map(body, mesh=mesh, in_specs=(spec,), out_specs=spec, check_vma=False)
```

```python
import functools
import math

import jax
import jax.numpy as jnp
import numpy as np
from jax import lax
from jax.experimental import pallas as pl
from jax.experimental.pallas import tpu as pltpu
from jax.sharding import PartitionSpec as P

L = 128
ALPHA_HALF = 0.04
BZ = 8
BY = 16
NC = 8
MESH = pl.DeviceIdType.MESH
F32 = jnp.float32
BF16 = jnp.bfloat16
HALF = L // 2
NQ = BZ // 2
FORTH = ((0, 3, 4), (0, 2, 3), (0, 1, 2), (0, 0, 1), (1, 2, 4), (1, 0, 2))
BACK = ((0, 0, 2), (0, 2, 3), (1, 0, 1), (1, 1, 2), (1, 2, 3), (0, 3, 4), (1, 3, 4))
WAITED = (0, 2, 0, 1, 2, 3, 3)
STEPS = ((1, 2), (0, 2), (1, 1), (1, 3), (0, 1), (0, 3), (1, 0))


def tables():
    k = np.arange(L)
    angle = 2.0 * np.pi / L * (np.outer(k, k) % L)
    hartley = np.cos(angle) + np.sin(angle)
    high = hartley.astype(np.float32).astype(jnp.bfloat16)
    low = (hartley - high.astype(np.float64)).astype(np.float32).astype(jnp.bfloat16)
    half = np.concatenate([high, low], axis=1)
    mat_x = np.concatenate([half, half], axis=0)
    mat_y = np.ascontiguousarray(mat_x.T)
    momentum = 4.0 * np.sin(np.pi * k / L) ** 2
    mass = momentum[:, None] + momentum[None, :]
    mass[0, 0] = 1.0
    root = np.sqrt(mass * mass / 4.0 + mass)
    decay = 1.0 / (1.0 + mass / 2.0 + root)
    factor = 12.0 * ALPHA_HALF / (L * L) / (2.0 * root)
    decay[0, 0] = 0.0
    factor[0, 0] = 0.0
    paired = [
        np.stack([np.tile(t[:, h * HALF : (h + 1) * HALF], (1, 2)) for h in range(2)])
        for t in (decay, factor)
    ]
    return mat_x, mat_y, paired[0].astype(np.float32), paired[1].astype(np.float32)


def split(x):
    high = x.astype(BF16)
    low = (x - high.astype(F32)).astype(BF16)
    return high, low


def transform_x(planes, mat_x):
    high, low = split(jnp.concatenate(planes, axis=0))
    out = jnp.dot(jnp.concatenate([high, low], axis=1), mat_x, preferred_element_type=F32)
    out = out[:, :L] + out[:, L:]
    return [out[i * L : (i + 1) * L] for i in range(len(planes))]


def transform_y(planes, mat_y):
    high, low = split(jnp.concatenate(planes, axis=1))
    out = jnp.dot(mat_y, jnp.concatenate([high, low], axis=0), preferred_element_type=F32)
    out = out[:L] + out[L:]
    return [out[:, i * L : (i + 1) * L] for i in range(len(planes))]


def algebra(re, im):
    trace_part = (im(0, 0) + im(1, 1) + im(2, 2)) * (1.0 / 3.0)
    return [
        im(0, 0) - trace_part,
        im(1, 1) - trace_part,
        (re(0, 1) - re(1, 0)) * 0.5,
        (im(0, 1) + im(1, 0)) * 0.5,
        (re(0, 2) - re(2, 0)) * 0.5,
        (im(0, 2) + im(2, 0)) * 0.5,
        (re(1, 2) - re(2, 1)) * 0.5,
        (im(1, 2) + im(2, 1)) * 0.5,
    ]


def fix_kernel(
    nz,
    ny,
    links,
    mat_x_in,
    mat_y_in,
    decay_in,
    factor_in,
    out,
    link,
    turn,
    base,
    send_a,
    edge_y,
    recv_a,
    edge_r,
    face_s,
    face_r,
    face,
    field,
    keep,
    send_b,
    recv_b,
    send_e,
    recv_e,
    send_c,
    recv_c,
    send_d,
    edge_d,
    main,
    smooth,
    above_z,
    edge_g,
    ninth,
    send_n,
    above_k,
    mat_x,
    mat_y,
    decay,
    factor,
    turn_edge,
    load_sem,
    small_sem,
    a_send,
    a_recv,
    b_send,
    b_recv,
    c_send,
    c_recv,
    d_send,
    d_recv,
    e_send,
    e_recv,
    z_send,
    z_recv,
    n_sem,
    ring,
):
    gz = lax.axis_index("gz")
    gy = lax.axis_index("gy")
    lines = L // nz
    extent = nz * BZ

    side = ny // 2
    half = nz // 2
    my_z, my_y = lax.div(gy, side), lax.rem(gy, side)

    def y_target(r):
        a, b = STEPS[r - 1]
        return lax.rem(my_z + a, 2) * side + lax.rem(my_y + b, side)

    def y_sender(r):
        a, b = STEPS[r - 1]
        return lax.rem(my_z + 2 - a, 2) * side + lax.rem(my_y + side - b, side)

    def z_target(r):
        return lax.rem(gz + r, nz)

    def z_sender(r):
        return lax.rem(gz + nz - r, nz)

    my_half, my_place = lax.div(gz, half), lax.rem(gz, half)

    def near(r):
        return my_half * half + lax.rem(my_place + r, half)

    between = lax.rem(gy + side, ny)

    barrier = pltpu.get_barrier_semaphore()
    for r in range(1, ny):
        pl.semaphore_signal(barrier, inc=1, device_id=(gz, y_target(r)), device_id_type=MESH)
    for device in [z_target(half)] + [near(r) for r in range(1, half)]:
        pl.semaphore_signal(barrier, inc=1, device_id=(device, gy), device_id_type=MESH)

    def load(mu, z, n):
        pltpu.make_async_copy(
            links.at[mu, :, :, :, pl.ds(z, 1)],
            link.at[mu, :, :, :, pl.ds(z, 1)],
            load_sem.at[n],
        ).start()

    def settle(ref, sem):
        pltpu.make_async_copy(ref, ref, sem).wait()

    def loaded(n, planes):
        settle(link.at[0, :, :, :, 0:planes], load_sem.at[n])

    small = [
        pltpu.make_async_copy(src, dst, small_sem.at[n])
        for n, (src, dst) in enumerate(
            ((mat_x_in, mat_x), (mat_y_in, mat_y), (decay_in, decay), (factor_in, factor))
        )
    ]
    for z in range(BZ):
        load(1, z, NQ)
    small[0].start()
    load(2, BZ - 1, NQ + 1)
    load(2, NQ - 1, NQ + 1)
    for q in range(NQ - 1, -1, -1):
        if q > 0:
            load(2, q + NQ - 1, q)
            load(2, q - 1, q)
        load(0, q + NQ, q)
        load(0, q, q)
    for copy in small[1:]:
        copy.start()

    def remote(src, dst, send, recv, device):
        return pltpu.make_async_remote_copy(
            src_ref=src,
            dst_ref=dst,
            send_sem=send,
            recv_sem=recv,
            device_id=device,
            device_id_type=MESH,
        )

    def rows(block):
        return pl.ds(pl.multiple_of(block * BY, BY), BY)

    def tile(block):
        return pl.ds(pl.multiple_of(block * BZ, BZ), BZ)

    def copy_a(n, r, sender):
        h, lo, hi = FORTH[n]
        return remote(
            send_a.at[h, y_target(r), lo:hi],
            recv_a.at[h, lo:hi, rows(sender)],
            a_send.at[0],
            a_recv.at[n],
            (gz, y_target(r)),
        )

    def own_a(n):
        h, lo, hi = FORTH[n]
        return pltpu.make_async_copy(
            send_a.at[h, gy, lo:hi], recv_a.at[h, lo:hi, rows(gy)], a_recv.at[n]
        )

    def start_a(n):
        for r in range(1, ny):
            copy_a(n, r, gy).start()
        own_a(n).start()

    def copy_edge_a(r, sender):
        return remote(
            edge_y.at[tile(y_target(r))],
            edge_r.at[tile(sender)],
            e_send.at[0],
            e_recv.at[0],
            (gz, y_target(r)),
        )

    def copy_b(h, r, sender):
        return remote(
            send_b.at[h, z_target(r)],
            recv_b.at[h, sender],
            b_send.at[0],
            b_recv.at[h],
            (z_target(r), between),
        )

    def copy_e(r, sender):
        return remote(
            send_e.at[0],
            recv_e.at[sender],
            b_send.at[1],
            b_recv.at[2],
            (z_target(r), gy),
        )

    def copy_c(h, r, sender):
        return remote(
            send_c.at[h, z_target(r)],
            recv_c.at[h, sender],
            c_send.at[0],
            c_recv.at[h],
            (z_target(r), between),
        )

    def copy_d(n, r, owner):
        h, lo, hi = BACK[n]
        return remote(
            send_d.at[h, lo:hi, rows(y_target(r))],
            main.at[h, owner, lo:hi],
            d_send.at[0],
            d_recv.at[WAITED[n]],
            (gz, y_target(r)),
        )

    def own_d(n):
        h, lo, hi = BACK[n]
        return pltpu.make_async_copy(
            send_d.at[h, lo:hi, rows(gy)], main.at[h, gy, lo:hi], d_recv.at[WAITED[n]]
        )

    def start_d(n):
        for r in range(1, ny):
            copy_d(n, r, gy).start()
        own_d(n).start()

    def copy_edge_d(r, owner):
        return remote(
            edge_d.at[tile(y_target(r))],
            edge_g.at[tile(owner)],
            e_send.at[1],
            e_recv.at[1],
            (gz, y_target(r)),
        )

    def copy_face(r, sender):
        return remote(
            face_s.at[y_target(r)],
            face_r.at[rows(sender)],
            z_send.at[0],
            z_recv.at[0],
            (gz, y_target(r)),
        )

    copy_down = remote(smooth.at[0], above_z, z_send.at[1], z_recv.at[1], (z_target(nz - 1), gy))
    own_edge_a = pltpu.make_async_copy(edge_y.at[tile(gy)], edge_r.at[tile(gy)], e_recv.at[0])
    own_edge_d = pltpu.make_async_copy(edge_d.at[tile(gy)], edge_g.at[tile(gy)], e_recv.at[1])

    first_row = lax.broadcasted_iota(jnp.int32, (BY, L), 0) == 0
    left = lax.broadcasted_iota(jnp.int32, (L, L), 1) < HALF
    straight = (lax.broadcasted_iota(jnp.int32, (NC, BZ, L), 2) < HALF) == (
        lax.broadcasted_iota(jnp.int32, (NC, BZ, L), 1) < NQ
    )

    def swap(x):
        return pltpu.roll(x, HALF, 1)

    def pair(x, y):
        return jnp.where(left, x, swap(y)), jnp.where(left, swap(x), y)

    def pair_edge(x):
        other = pltpu.roll(swap(x).reshape(NC, BZ, L), NQ, 1)
        return jnp.where(straight, x.reshape(NC, BZ, L), other).reshape(NC * BZ, L)

    def parts(mu, z):
        return algebra(
            lambda i, j: link[mu, 0, i, j, z], lambda i, j: link[mu, 1, i, j, z]
        )

    def part_y(z, carry):
        along = parts(1, z)
        for c in range(NC):
            behind = jnp.where(first_row, 0.0, pltpu.roll(along[c], 1, 0))
            base[c, z] = behind - along[c]
            edge_y[pl.ds(c * BZ + z, 1), :] = along[c][BY - 1 : BY]
        return carry

    loaded(NQ, BZ)
    lax.fori_loop(0, BZ, part_y, 0)
    loaded(NQ + 1, 2)
    top = parts(2, BZ - 1)
    small[0].wait()
    face_s[...] = transform_x([jnp.concatenate(top, axis=0)], mat_x[...])[0].reshape(NC, BY, L)
    pl.semaphore_wait(barrier, ny + half - 1)
    for r in range(1, ny):
        copy_face(r, gy).start()
    pltpu.make_async_copy(face_s.at[gy], face_r.at[rows(gy)], z_recv.at[0]).start()
    for r in range(1, half):
        pl.semaphore_signal(ring.at[0], inc=1, device_id=(near(r), gy), device_id_type=MESH)

    def divergence(z, under, here):
        along = parts(0, z)
        return jnp.concatenate(
            [
                base[c, z] + (pltpu.roll(along[c], 1, 1) - along[c]) + (-here[c] if under is None else under[c] - here[c])
                for c in range(NC)
            ],
            axis=0,
        )

    def spread(q, low, high):
        low, high = transform_x([low, high], mat_x[...])
        low, high = pair(low, high)
        send_a[0, :, q] = low.reshape(NC, BY, L)
        send_a[1, :, q] = high.reshape(NC, BY, L)

    def step(t, carry):
        here_low, here_high = carry
        q = NQ - 1 - t
        loaded(q, 4)
        under_low = parts(2, q - 1)
        under_high = parts(2, q + NQ - 1)
        spread(
            q, divergence(q, under_low, here_low), divergence(q + NQ, under_high, here_high)
        )
        return under_low, under_high

    carry = (parts(2, NQ - 1), top)
    carry = step(0, carry)
    start_a(0)
    carry = step(1, carry)
    start_a(1)
    edge_y[...] = pair_edge(transform_x([edge_y[...]], mat_x[...])[0])
    for r in range(1, ny):
        copy_edge_a(r, gy).start()
    own_edge_a.start()
    carry = step(2, carry)
    start_a(2)
    loaded(0, 2)
    high = divergence(NQ, parts(2, NQ - 1), carry[1])
    spread(0, divergence(0, None, carry[0]), high)
    for n in range(3, len(FORTH)):
        start_a(n)
    if half > 1:
        pl.semaphore_wait(ring.at[0], half - 1)
    pl.semaphore_signal(
        ring.at[1], inc=1, device_id=(z_target(half), gy), device_id_type=MESH
    )

    for copy in small[1:]:
        copy.wait()
    settle(edge_r, e_recv.at[0])

    def receive(n):
        h, lo, hi = FORTH[n]
        settle(recv_a.at[h, lo:hi], a_recv.at[n])
        for q in range(lo, hi):
            edge = pltpu.roll(edge_r[pl.ds(h * NQ + q, ny, stride=BZ), :], 1, 0)
            recv_a[h, q, pl.ds(0, ny, stride=BY), :] += edge
        data = transform_y([recv_a[h, q] for q in range(lo, hi)], mat_y[...])
        for q in range(lo, hi):
            field[h, q] = data[q - lo]

    def power4(x):
        x = x * x
        return x * x

    def moments(h):
        rate = decay[h]
        rate4 = power4(rate)
        up = field[h, 0]
        down = field[h, NQ - 1]
        for q in range(1, NQ):
            up = field[h, q] + rate * up
            down = field[h, NQ - 1 - q] + rate * down
        up = rate * up
        swapped = jnp.where(left, swap(down), swap(up))
        keep[h] = swapped
        beyond = face[h]
        packed = jnp.where(left, down + rate4 * rate4 * beyond, up + beyond)
        send_b[h] = (packed + rate4 * swapped).reshape(nz, lines, L)
        for r in range(nz):
            copy_b(h, r, gz).start()

    narrow = lax.broadcasted_iota(jnp.int32, (lines, L), 1) < HALF

    def solve(h):
        rate8 = decay[h, pl.ds(pl.multiple_of(gz * lines, lines), lines), :]
        rate8 = power4(rate8 * rate8)
        whole = rate8
        for _ in range(int(math.log2(nz))):
            whole = whole * whole
        images = 1.0 / (1.0 - whole)
        settle(recv_b.at[h], b_recv.at[h])
        mixed = [
            jnp.where(narrow, recv_b[h, nz - 1 - j], recv_b[h, j]) for j in range(nz)
        ]
        state = mixed[0]
        for j in range(1, nz):
            state = mixed[j] + rate8 * state
        state = state * images
        result = []
        for j in range(nz):
            result.append(state)
            state = mixed[j] + rate8 * state
        for j in range(nz):
            send_c[h, j] = jnp.where(narrow, result[nz - 1 - j], result[j])
        for r in range(nz):
            copy_c(h, r, gz).start()

    receive(0)
    receive(1)
    settle(face_r, z_recv.at[0])
    beyond = transform_y([face_r[...]], mat_y[...])[0]
    face[0], face[1] = pair(beyond, beyond)
    receive(2)
    receive(3)
    pl.semaphore_wait(ring.at[1], 1)
    moments(0)
    lane = lax.broadcasted_iota(jnp.int32, (1, L), 1)
    packed = jnp.zeros((1, L), F32)
    for q in range(NQ):
        row = field[0, q, 0:1, :]
        packed = jnp.where(lane == q, jnp.sum(jnp.where(lane == 0, row, 0.0)), packed)
        packed = jnp.where(lane == q + NQ, jnp.sum(jnp.where(lane == HALF, row, 0.0)), packed)
    row = face[0, 0:1, :]
    packed = jnp.where(lane == BZ, jnp.sum(jnp.where(lane == 0, row, 0.0)), packed)
    send_e[0] = packed
    for r in range(1, nz):
        copy_e(r, gz).start()
    recv_e[gz] = packed
    receive(4)
    receive(5)
    moments(1)
    solve(0)

    settle(recv_e.at[0 : nz - 1], b_recv.at[2])
    sources = recv_e[:, 0, :]
    block = lax.broadcasted_iota(jnp.int32, (nz, L), 0)
    plane = lax.broadcasted_iota(jnp.int32, (nz, L), 1)
    constant = (1.0 + extent * extent - 1.0) / extent
    zero_line = []
    for i in range(BZ + 1):
        gap = BZ * (gz - block) + i - plane
        gap = jnp.where(gap < 0, gap + extent, gap).astype(F32)
        weight = constant - (6.0 / extent) * gap * (extent - gap)
        weight = jnp.where(plane <= BZ, weight * (ALPHA_HALF / (L * L)), 0.0)
        zero_line.append(jnp.sum(weight * sources))
    solve(1)

    tile_row = lax.broadcasted_iota(jnp.int32, (8, L), 0)
    tile_lane = lax.broadcasted_iota(jnp.int32, (8, L), 1)

    def evaluate(h):
        rate = decay[h]
        scale = factor[h]
        settle(recv_c.at[h], c_recv.at[h])
        outside = recv_c[h].reshape(L, L) + jnp.where(left, face[h], 0.0)
        inside = power4(rate) * outside + keep[h]
        outside = swap(outside)
        down = rate * jnp.where(left, inside, outside)
        for q in range(NQ - 1, -1, -1):
            recv_a[h, q] = down
            if q > 0:
                down = rate * (down + field[h, q])
        up = jnp.where(left, outside, inside)
        for q in range(NQ):
            up = field[h, q] + (rate * up if q > 0 else up)
            recv_a[h, q] = scale * (up + recv_a[h, q])
            if h == 0:
                low = jnp.where((tile_row == 0) & (tile_lane == 0), zero_line[q], 0.0)
                high = jnp.where(
                    (tile_row == 0) & (tile_lane == HALF), zero_line[q + NQ], 0.0
                )
                recv_a[h, q, 0:8, :] += low + high
        ninth[h] = scale * (rate * up + outside)

    def inverse(h, lo, hi):
        data = transform_y([recv_a[h, q] for q in range(lo, hi)], mat_y[...])
        for q in range(lo, hi):
            send_d[h, q] = data[q - lo]
            edge = send_d[h, q, pl.ds(0, ny, stride=BY), :]
            edge_d[pl.ds(h * NQ + q, ny, stride=BZ), :] = pltpu.roll(edge, ny - 1, 0)

    evaluate(0)
    inverse(0, 0, 2)
    start_d(0)
    inverse(0, 2, 4)
    start_d(1)
    evaluate(1)
    inverse(1, 0, 2)
    start_d(2)
    start_d(3)
    inverse(1, 2, 4)
    for r in range(1, ny):
        copy_edge_d(r, gy).start()
    own_edge_d.start()
    for n in range(4, len(BACK)):
        start_d(n)

    def copy_ninth(r):
        return remote(
            send_n.at[rows(y_target(r))],
            above_k.at[gy],
            n_sem.at[0],
            n_sem.at[1],
            (gz, y_target(r)),
        )

    @pl.when(my_place == half - 1)
    def _():
        plane = jnp.where(left, swap(ninth[0]), ninth[1])
        origin = (lax.broadcasted_iota(jnp.int32, (L, L), 0) == 0) & (
            lax.broadcasted_iota(jnp.int32, (L, L), 1) == 0
        )
        plane = plane + jnp.where(origin, zero_line[BZ], 0.0)
        send_n[...] = transform_y([plane], mat_y[...])[0]
        for r in range(1, ny):
            copy_ninth(r).start()
        pltpu.make_async_copy(send_n.at[rows(gy)], above_k.at[gy], n_sem.at[1]).start()


    settle(send_a.at[:, 0 : ny - 1], a_send.at[0])
    settle(edge_y.at[0 : (ny - 1) * BZ], e_send.at[0])
    settle(send_b, b_send.at[0])
    settle(send_c, c_send.at[0])
    settle(recv_e.at[0 : nz - 1], b_send.at[1])
    settle(face_s.at[0 : ny - 1], z_send.at[0])

    def fill(plane, value):
        for s in range(0, BY, 8):
            g = exponent([value(c, s) for c in range(NC)])
            for k in range(18):
                turn[plane, k, s : s + 8] = g[k]

    def rotate(z, directions):
        rotate_plane(link, turn, out, z, directions)

    def arrive(n, planes):
        settle(main.at[0, :, 0:planes], d_recv.at[n])

    def collect(lo, hi):
        planes = []
        for q in range(lo, hi):
            planes += pair(main[0, :, q].reshape(L, L), main[1, :, q].reshape(L, L))
        data = transform_x(planes, mat_x[...])
        for q in range(lo, hi):
            smooth[q] = data[2 * (q - lo)].reshape(NC, BY, L)
            smooth[q + NQ] = data[2 * (q - lo) + 1].reshape(NC, BY, L)

    def fill_plane(z):
        fill(z, lambda c, s: smooth[z, c, s : s + 8])

    def add_edge(z):
        for k in range(18):
            turn[z, k, BY : BY + 1] = turn_edge[k, pl.ds(z, 1)]

    def along_z(t, first):
        rotate(first + t * NQ, (2,))
        return first

    def around(q):
        for z in (q, q + NQ):
            add_edge(z)
            rotate(z, (0, 1))

    def fill_pair(q):
        for z in (q, q + NQ):
            fill_plane(z)

    arrive(0, 3)
    collect(0, 1)
    @pl.when(my_place != 0)
    def _():
        copy_down.start()

    fill_pair(0)
    arrive(1, 1)
    collect(1, 2)
    settle(edge_g, e_recv.at[1])
    edge_g[...] = transform_x([pair_edge(edge_g[...])], mat_x[...])[0]
    g = exponent([edge_g[c * BZ : (c + 1) * BZ] for c in range(NC)])
    for k in range(18):
        turn_edge[k] = g[k]
    fill_pair(1)
    around(0)
    around(1)
    lax.fori_loop(0, 2, along_z, 0)
    arrive(2, 2)
    collect(2, 3)
    fill_pair(2)
    around(2)
    lax.fori_loop(0, 2, along_z, 1)
    arrive(3, 2)
    collect(3, 4)
    fill_pair(3)
    for z in (3, 3 + NQ):
        add_edge(z)
    @pl.when(my_place != half - 1)
    def _():
        copy_down.wait_recv()

    @pl.when(my_place == half - 1)
    def _():
        settle(above_k, n_sem.at[1])
        plane = transform_x([above_k[...].reshape(L, L)], mat_x[...])[0]
        above_z[...] = plane.reshape(NC, BY, L)

    fill(BZ, lambda c, s: above_z[c, s : s + 8])

    settle(send_d.at[:, :, 0 : (ny - 1) * BY], d_send.at[0])
    settle(edge_d.at[0 : (ny - 1) * BZ], e_send.at[1])
    @pl.when(my_place != 0)
    def _():
        copy_down.wait_send()

    @pl.when(my_place == half - 1)
    def _():
        settle(send_n.at[0 : (ny - 1) * BY], n_sem.at[0])


def rotate_plane(link, turn, out, z, directions):
    for s in range(0, BY, 8):
        g = [turn[z, k, s : s + 8] for k in range(18)]
        for mu in directions:
            if mu == 0:
                ahead = [pltpu.roll(x, L - 1, 1) for x in g]
            elif mu == 1:
                ahead = [turn[z, k, s + 1 : s + 9] for k in range(18)]
            else:
                ahead = [turn[z + 1, k, s : s + 8] for k in range(18)]
            rotate_link(link, out, mu, z, s, g, ahead)


def rotate_link(link, out, mu, z, s, g, ahead):
    u = [link[mu, p, i, j, z, s : s + 8] for p in range(2) for i in range(3) for j in range(3)]
    for i in range(3):
        left = []
        for k in range(3):
            re = im = None
            for j in range(3):
                ar, ai = g[3 * i + j], g[9 + 3 * i + j]
                br, bi = u[3 * j + k], u[9 + 3 * j + k]
                tr = ar * br - ai * bi
                ti = ar * bi + ai * br
                re = tr if re is None else re + tr
                im = ti if im is None else im + ti
            left.append((re, im))
        for l in range(3):
            re = im = None
            for k in range(3):
                ar, ai = left[k]
                br, bi = ahead[3 * l + k], ahead[9 + 3 * l + k]
                tr = ar * br + ai * bi
                ti = ai * br - ar * bi
                re = tr if re is None else re + tr
                im = ti if im is None else im + ti
            out[mu, 0, i, l, z, s : s + 8] = re
            out[mu, 1, i, l, z, s : s + 8] = im


def fix(links, nz, ny):
    mat_x, mat_y, decay, factor = tables()
    lines = L // nz
    vmem = pltpu.VMEM
    dma = pltpu.SemaphoreType.DMA
    return pl.pallas_call(
        functools.partial(fix_kernel, nz, ny),
        out_shape=(
            pltpu.VMEM(links.shape, F32),
            pltpu.VMEM(links.shape, F32),
            pltpu.VMEM((BZ + 1, 18, BY + 8, L), F32),
        ),
        in_specs=[pl.BlockSpec(memory_space=pltpu.HBM)] * 5,
        out_specs=(pl.BlockSpec(memory_space=pltpu.VMEM),) * 3,
        scratch_shapes=[
            vmem((NC, BZ, BY, L), F32),
            vmem((2, NC, NQ, BY, L), F32),
            vmem((NC * BZ, L), F32),
            vmem((2, NQ, L, L), F32),
            vmem((ny * BZ, L), F32),
            vmem((NC, BY, L), F32),
            vmem((L, L), F32),
            vmem((2, L, L), F32),
            vmem((2, NQ, L, L), F32),
            vmem((2, L, L), F32),
            vmem((2, nz, lines, L), F32),
            vmem((2, nz, lines, L), F32),
            vmem((1, 1, L), F32),
            vmem((nz, 1, L), F32),
            vmem((2, nz, lines, L), F32),
            vmem((2, nz, lines, L), F32),
            vmem((2, NQ, L, L), F32),
            vmem((ny * BZ, L), F32),
            vmem((2, NC, NQ, BY, L), F32),
            vmem((BZ, NC, BY, L), F32),
            vmem((NC, BY, L), F32),
            vmem((NC * BZ, L), F32),
            vmem((2, L, L), F32),
            vmem((L, L), F32),
            vmem((NC, BY, L), F32),
            vmem((2 * L, 2 * L), BF16),
            vmem((2 * L, 2 * L), BF16),
            vmem((2, L, L), F32),
            vmem((2, L, L), F32),
            vmem((18, BZ, L), F32),
            dma((NQ + 2,)),
            dma((4,)),
            dma((1,)),
            dma((len(FORTH),)),
            dma((2,)),
            dma((3,)),
            dma((1,)),
            dma((2,)),
            dma((1,)),
            dma((4,)),
            dma((2,)),
            dma((2,)),
            dma((2,)),
            dma((2,)),
            dma((2,)),
            pltpu.SemaphoreType.REGULAR((2,)),
        ],
        compiler_params=pltpu.CompilerParams(
            collective_id=0, has_side_effects=True, vmem_limit_bytes=32 << 20
        ),
        name="fix",
    )(*(pltpu.with_memory_space_constraint(jnp.asarray(x), pltpu.HBM)
        for x in (links, mat_x, mat_y, decay, factor)))


def exponent(h):
    h2 = -(h[0] + h[1])
    diag = (h[0], h[1], h2)
    re01, im01 = h[3], -h[2]
    re02, im02 = h[5], -h[4]
    re12, im12 = h[7], -h[6]
    n01 = re01 * re01 + im01 * im01
    n02 = re02 * re02 + im02 * im02
    n12 = re12 * re12 + im12 * im12
    s0 = h[0] * h[0] + n01 + n02
    s1 = h[1] * h[1] + n01 + n12
    s2 = h2 * h2 + n02 + n12
    s01re = re02 * re12 + im02 * im12 - h2 * re01
    s01im = im02 * re12 - re02 * im12 - h2 * im01
    s02re = re01 * re12 - im01 * im12 - h[1] * re02
    s02im = re01 * im12 + im01 * re12 - h[1] * im02
    s12re = re01 * re02 + im01 * im02 - h[0] * re12
    s12im = re01 * im02 - im01 * re02 - h[0] * im12
    p = 0.5 * (s0 + s1 + s2)
    cross = (re01 * re12 - im01 * im12) * re02 + (re01 * im12 + im01 * re12) * im02
    d = h[0] * h[1] * h2 + 2.0 * cross - h[0] * n12 - h[1] * n02 - h2 * n01
    pp = p * p
    dd = d * d
    dp = d * p
    cubes = dd + p * pp
    a0 = 1.0 + dd * (p * (2.0 / 40320.0) - 1.0 / 720.0)
    b0 = d * (-1.0 / 6.0 + p * (1.0 / 120.0) - pp * (1.0 / 5040.0))
    a1 = d * (1.0 / 24.0 - p * (2.0 / 720.0) + pp * (3.0 / 40320.0))
    b1 = 1.0 - p * (1.0 / 6.0) + pp * (1.0 / 120.0) - cubes * (1.0 / 5040.0)
    a2 = -0.5 + p * (1.0 / 24.0) - pp * (1.0 / 720.0) + cubes * (1.0 / 40320.0)
    b2 = d * (1.0 / 120.0) - dp * (2.0 / 5040.0)
    re = {}
    im = {}
    for j, s in enumerate((s0, s1, s2)):
        re[j, j] = a0 + a1 * diag[j] + a2 * s
        im[j, j] = b0 + b1 * diag[j] + b2 * s
    for i, j, hr, hi, sr, si in (
        (0, 1, re01, im01, s01re, s01im),
        (0, 2, re02, im02, s02re, s02im),
        (1, 2, re12, im12, s12re, s12im),
    ):
        rr = a1 * hr + a2 * sr
        ii = b1 * hi + b2 * si
        ri = a1 * hi + a2 * si
        ir = b1 * hr + b2 * sr
        re[i, j] = rr - ii
        im[i, j] = ri + ir
        re[j, i] = rr + ii
        im[j, i] = ir - ri
    return [re[i, j] for i in range(3) for j in range(3)] + [
        im[i, j] for i in range(3) for j in range(3)
    ]


def store_kernel(source, link, turn, out, last, sem):
    def put(src, lo, hi, mus):
        for mu in mus:
            pltpu.make_async_copy(
                src.at[mu, :, :, :, lo:hi], out.at[mu, :, :, :, lo:hi], sem.at[0]
            ).start()

    put(source, 0, 2, (0, 1, 2))
    put(source, NQ, NQ + 2, (0, 1, 2))
    put(source, 2, 3, (0, 1))
    put(source, NQ + 2, NQ + 3, (0, 1))
    for z in (2, NQ + 2):
        rotate_plane(link, turn, last, z, (2,))
        put(last, z, z + 1, (2,))
    for z in (3, NQ + 3):
        rotate_plane(link, turn, last, z, (0, 1, 2))
        put(last, z, z + 1, (0, 1, 2))
    pltpu.make_async_copy(source, out, sem.at[0]).wait()


def store(source, link, turn):
    return pl.pallas_call(
        store_kernel,
        out_shape=jax.ShapeDtypeStruct(source.shape, F32),
        in_specs=[pl.BlockSpec(memory_space=pltpu.VMEM)] * 3,
        out_specs=pl.BlockSpec(memory_space=pl.ANY),
        scratch_shapes=[
            pltpu.VMEM((3, 2, 3, 3, BZ, BY, L), F32),
            pltpu.SemaphoreType.DMA((1,)),
        ],
        compiler_params=pltpu.CompilerParams(vmem_limit_bytes=16 << 20),
        name="store",
    )(source, link, turn)


def solution(mesh):
    nz, ny = mesh.shape["gz"], mesh.shape["gy"]

    def body(links):
        return store(*fix(links, nz, ny))

    spec = P(None, None, None, None, "gz", "gy", None)
    return jax.shard_map(body, mesh=mesh, in_specs=(spec,), out_specs=spec, check_vma=False)
```
